128 devices in a mesh: dp: 4 (over z_lo, core), ctx: 32 (over z_hi, x, y).
Axes of the slice: x: 4, y: 4, z: 4 (z_hi: 2, z_lo: 2; z = z_hi * 2 + z_lo), core: 2. Of those that a mesh axis runs over, the one named last changes fastest.
Arguments:
- layer_input: bfloat16 [16384, 1024], P(('dp', 'ctx')), may hold values from -3 to 3
- query_heads: bfloat16 [16384, 512], P(('dp', 'ctx')), may hold values from -6 to 6
- key_heads: bfloat16 [16384, 512], P(('dp', 'ctx')), may hold values from -6 to 6
- value_heads: bfloat16 [16384, 512], P(('dp', 'ctx')), may hold values from -12 to 12
- out_weight: bfloat16 [1024, 512], replicated, may hold values from -0.25 to 0.25
- conv_kernel: bfloat16 [1024, 9], replicated, may hold values from -2 to 2
- record_lengths: int32 [4, 4], replicated, may hold values from 1 to 2048, 4096 in all within a row
- upstream_grad: bfloat16 [16384, 1024], P(('dp', 'ctx')), may hold values from -24 to 24
Outputs:
- layer_output: bfloat16 [16384, 1024], P(('dp', 'ctx'))
- input_grad: bfloat16 [16384, 1024], P(('dp', 'ctx'))
- query_grad: bfloat16 [16384, 512], P(('dp', 'ctx'))
- key_grad: bfloat16 [16384, 512], P(('dp', 'ctx'))
- value_grad: bfloat16 [16384, 512], P(('dp', 'ctx'))
- out_weight_grad: float32 [1024, 512], P(('dp', 'ctx'))
- kernel_grad: float32 [1024, 9], replicated
The draws below stay inside these ranges and needn't reach their ends.
Inputs may be any that keep to these rules, and one draw needn't show every extreme that they name: `record_lengths`: each row lists the 4 recordings of one group in packing order; a row sums to 4096 and its longest recording has exactly 2048 frames.
All inputs are finite; a program needn't handle non-finite values.
Results may differ from the reference program's by a relative error of at most 0.023.
Values may be sent and summed in bfloat16 or wider, within the bound.
A program may use at most 128 MiB of HBM per device.

```python
import math
import jax
import jax.numpy as jnp
import numpy as np
from jax import lax

D = 1024
H = 8
E = 64
KW = 9
RECS = 4
HD = 512
CTXLEN = 4096
GROUPS = 4
FRAMES = 16384


def drawn_pair(key):
    base_key = jax.random.fold_in(key, 7001)
    query_key, keys_key = jax.random.split(base_key, 2)
    queries = jnp.clip(1.5 * jax.random.normal(query_key, (FRAMES, HD), jnp.float32), -6.0, 6.0)
    key_rows = jnp.clip(1.5 * jax.random.normal(keys_key, (FRAMES, HD), jnp.float32), -6.0, 6.0)
    return (queries, key_rows)


def draw_query_heads(key, part):
    return drawn_pair(key)[0].astype(jnp.bfloat16)


def draw_key_heads(key, part):
    return drawn_pair(key)[1].astype(jnp.bfloat16)


def spiked(drawn, rng, source, target, parts, factor):
    def block_of(dim):
        return (jnp.arange(drawn.shape[dim]) // (drawn.shape[dim] // parts)).reshape((-1,) + (1,) * (drawn.ndim - 1 - dim))

    one_side = jax.random.permutation(rng, parts)[block_of(target)]
    second = (block_of(target) + parts // 2) % parts
    return jnp.where((block_of(source) == one_side) | (block_of(source) == second), factor * drawn, drawn)


def steps_of(rng, extent, cuts, smallest, top_value):
    loudness = 1.0
    for axis_at, parts in cuts:
        draws = jax.random.uniform(jax.random.fold_in(jax.random.fold_in(rng, 6), axis_at), (parts,), jnp.float32, smallest / len(cuts), top_value / len(cuts))
        loudness = loudness * jnp.repeat(jnp.exp(draws), extent[axis_at] // parts).reshape((-1,) + (1,) * (len(extent) - 1 - axis_at))
    return loudness


def profile(count, total, bound, skew):
    weights = [(1 << 20) // math.isqrt(rank ** skew) + 1 for rank in range(2, count + 1)]
    spare, holding = total - bound - (count - 1), [1] * (count - 1)
    while spare > 0:
        movable = [i for i in range(count - 1) if holding[i] < bound]
        pool, left = sum([weights[i] for i in movable]), spare
        for i in movable:
            addition = min(bound - holding[i], max(1, left * weights[i] // pool), spare)
            holding[i] = holding[i] + addition
            spare = spare - addition
    return np.array([bound] + holding)


def uneven_parts(own_key, amount, total, reach, slope):
    if amount == 2:
        one = jax.random.randint(own_key, (), max(1, total - reach), min(reach, total - 1) + 1)
        return jnp.stack([one, total - one])
    tallies = jnp.asarray(profile(amount, total, reach, slope), jnp.int32)
    pairs = (amount - 1) // 2
    source_of, taker = tallies[1:1 + 2 * pairs:2], tallies[2:2 + 2 * pairs:2]
    slack = jnp.minimum(source_of - 1, reach - taker)
    moved = jax.random.randint(jax.random.fold_in(own_key, 1), (pairs,), 0, 1 << 20) % (slack + 1)
    tallies = tallies.at[1:1 + 2 * pairs:2].set(source_of - moved).at[2:2 + 2 * pairs:2].set(taker + moved)
    return tallies[jax.random.permutation(jax.random.fold_in(own_key, 2), amount)]


def centred(own_key, extent, spread, bound, pieces=(), kind=jnp.bfloat16):
    entries = jax.random.normal(own_key, extent, jnp.float32) * spread
    if len(pieces) > 0:
        entries = steps_of(own_key, extent, pieces, -0.22, 0.18) * entries
    return jnp.clip(entries, min=-bound, max=bound).astype(kind)


def noise_with(own_key, shape, scale, most, cuts, heavy, kind=jnp.bfloat16):
    values = scale * jax.random.normal(own_key, shape, jnp.float32)
    if cuts:
        values = values * steps_of(own_key, shape, cuts, -0.22, 0.18)
    return jnp.clip(spiked(values, jax.random.fold_in(own_key, 3), *heavy), -most, most).astype(kind)


def setup_inputs(seed: int = 0) -> dict:
    keys = jax.random.split(jax.random.key(seed), 9)
    return {
        "layer_input": centred(keys[0], (FRAMES, D), 0.5, 3.0, ((0, 128),)),
        "query_heads": draw_query_heads(jax.random.fold_in(keys[8], 71), 0),
        "key_heads": draw_key_heads(jax.random.fold_in(keys[8], 71), 0),
        "value_heads": centred(keys[3], (FRAMES, HD), 2.0, 12.0, ((0, 128),)),
        "out_weight": centred(keys[4], (D, HD), HD ** -0.5, 0.25),
        "conv_kernel": centred(keys[5], (D, KW), KW ** -0.5, 2.0),
        "record_lengths": jax.vmap(lambda own: uneven_parts(own, RECS, CTXLEN, CTXLEN // 2, 2))(jax.random.split(keys[6], GROUPS)).reshape((GROUPS, RECS)).astype(jnp.int32),
        "upstream_grad": noise_with(keys[7], (FRAMES, D), 1.0, 24.0, ((0, 128),), (0, 1, 128, 5.5)),
    }


SCORE_SCALE = 0.125
MASKED_SCORE = -1e+30

def frame_ids(positions, record_sizes):
    record_ends = jnp.cumsum(record_sizes).astype(jnp.int32)
    record_starts = (record_ends - record_sizes).astype(jnp.int32)
    counted = lax.optimization_barrier(jnp.sum((positions[:, None] >= record_starts[None, :]).astype(jnp.int32), axis=1)).astype(jnp.int32)
    inside = (positions >= 0) & (positions < record_ends[-1])
    return jnp.where(inside, counted - 1, -1).astype(jnp.int32)

def rounded(values):
    return lax.optimization_barrier(values.astype(jnp.bfloat16)).astype(jnp.float32)

def group_pass(layer_input, query_heads, key_heads, value_heads, out_weight, conv_kernel, record_sizes, upstream_grad):
    half_width = (KW - 1) // 2
    block_rows = math.gcd(CTXLEN, 512)
    block_count = CTXLEN // block_rows
    frame_labels = frame_ids(jnp.arange(CTXLEN, dtype=jnp.int32), record_sizes)
    query_all = query_heads.astype(jnp.float32).reshape(CTXLEN, H, E)
    key_all = key_heads.astype(jnp.float32).reshape(CTXLEN, H, E)
    value_all = value_heads.astype(jnp.float32).reshape(CTXLEN, H, E)
    kernel_f32 = conv_kernel.astype(jnp.float32)

    def forward_block(block_index):
        begin_row = (block_index * block_rows).astype(jnp.int32)
        query_block = lax.dynamic_slice_in_dim(query_all, begin_row, block_rows, 0)
        label_block = lax.dynamic_slice_in_dim(frame_labels, begin_row, block_rows, 0)
        scores = jnp.einsum('qhe,khe->hqk', query_block, key_all) * SCORE_SCALE
        same_record = (label_block[:, None] == frame_labels[None, :])[None]
        scores = jnp.where(same_record, scores, MASKED_SCORE)
        row_max = lax.optimization_barrier(jnp.max(scores, axis=2))
        row_sum = lax.optimization_barrier(jnp.sum(jnp.where(same_record, jnp.exp(scores - row_max[:, :, None]), 0.0), axis=2))
        log_norm = row_max + jnp.log(row_sum)
        probs = jnp.where(same_record, jnp.exp(scores - log_norm[:, :, None]), 0.0)
        attended = jnp.einsum('hqk,khe->qhe', probs, value_all)
        return (attended.astype(jnp.bfloat16).reshape(block_rows, H * E), log_norm)
    attended_blocks, norm_blocks = lax.map(forward_block, jnp.arange(block_count, dtype=jnp.int32))
    attended = attended_blocks.reshape(CTXLEN, H * E)
    log_norm = jnp.transpose(norm_blocks, (1, 0, 2)).reshape(H, CTXLEN)
    mixed_frames = (layer_input.astype(jnp.float32) + jnp.dot(attended, out_weight.T, preferred_element_type=jnp.float32)).astype(jnp.bfloat16)
    padded = jnp.pad(mixed_frames, ((half_width, half_width), (0, 0)))
    edge_labels = jnp.pad(frame_labels, (half_width, half_width), constant_values=-1).astype(jnp.int32)

    def conv_tap(tap_index, running):
        tap_index = jnp.asarray(tap_index).astype(jnp.int32)
        shifted = lax.dynamic_slice_in_dim(padded, tap_index, CTXLEN, 0).astype(jnp.float32)
        same_record = (lax.dynamic_slice_in_dim(edge_labels, tap_index, CTXLEN, 0) == frame_labels)[:, None]
        tap_weight = lax.dynamic_slice_in_dim(kernel_f32, tap_index, 1, 1)[:, 0]
        return running + jnp.where(same_record, shifted * tap_weight[None, :], 0.0)
    conv_out = lax.fori_loop(0, KW, conv_tap, jnp.zeros((CTXLEN, D), jnp.float32))
    sigmoid_gate = jax.nn.sigmoid(conv_out)
    layer_output = (mixed_frames.astype(jnp.float32) + conv_out * sigmoid_gate).astype(jnp.bfloat16)
    conv_grad = (upstream_grad.astype(jnp.float32) * sigmoid_gate * (1.0 + conv_out * (1.0 - sigmoid_gate))).astype(jnp.bfloat16)
    grad_padded = jnp.pad(conv_grad, ((half_width, half_width), (0, 0)))
    conv_grad_f32 = conv_grad.astype(jnp.float32)

    def back_tap(tap_index, carried):
        running, kernel_rows = carried
        tap_index = jnp.asarray(tap_index).astype(jnp.int32)
        mirror = (KW - 1 - tap_index).astype(jnp.int32)
        shifted = lax.dynamic_slice_in_dim(grad_padded, mirror, CTXLEN, 0).astype(jnp.float32)
        same_back = (lax.dynamic_slice_in_dim(edge_labels, mirror, CTXLEN, 0) == frame_labels)[:, None]
        tap_weight = lax.dynamic_slice_in_dim(kernel_f32, tap_index, 1, 1)[:, 0]
        running = running + jnp.where(same_back, shifted * tap_weight[None, :], 0.0)
        forward_rows = lax.dynamic_slice_in_dim(padded, tap_index, CTXLEN, 0).astype(jnp.float32)
        same_fore = (lax.dynamic_slice_in_dim(edge_labels, tap_index, CTXLEN, 0) == frame_labels)[:, None]
        kernel_column = lax.optimization_barrier(jnp.sum(jnp.where(same_fore, conv_grad_f32 * forward_rows, 0.0), axis=0))
        kernel_rows = lax.dynamic_update_slice_in_dim(kernel_rows, kernel_column[:, None], tap_index, 1)
        return (running, kernel_rows)
    back_sum, kernel_grad = lax.fori_loop(0, KW, back_tap, (jnp.zeros((CTXLEN, D), jnp.float32), jnp.zeros((D, KW), jnp.float32)))
    input_grad = (upstream_grad.astype(jnp.float32) + back_sum).astype(jnp.bfloat16)
    weight_grad = jnp.dot(input_grad.T, attended, preferred_element_type=jnp.float32)
    attended_grad = jnp.dot(input_grad, out_weight, preferred_element_type=jnp.float32).astype(jnp.bfloat16)
    grad_all = attended_grad.astype(jnp.float32).reshape(CTXLEN, H, E)
    row_dots = jnp.transpose(lax.optimization_barrier(jnp.sum(grad_all * attended.astype(jnp.float32).reshape(CTXLEN, H, E), axis=2)))

    def query_block_grad(block_index):
        begin_row = (block_index * block_rows).astype(jnp.int32)
        query_block = lax.dynamic_slice_in_dim(query_all, begin_row, block_rows, 0)
        grad_block = lax.dynamic_slice_in_dim(grad_all, begin_row, block_rows, 0)
        label_block = lax.dynamic_slice_in_dim(frame_labels, begin_row, block_rows, 0)
        norm_block = lax.dynamic_slice_in_dim(log_norm, begin_row, block_rows, 1)
        dots_block = lax.dynamic_slice_in_dim(row_dots, begin_row, block_rows, 1)
        scores = jnp.einsum('qhe,khe->hqk', query_block, key_all) * SCORE_SCALE
        same_record = (label_block[:, None] == frame_labels[None, :])[None]
        probs = jnp.where(same_record, jnp.exp(jnp.where(same_record, scores, MASKED_SCORE) - norm_block[:, :, None]), 0.0)
        grad_dots = jnp.einsum('qhe,khe->hqk', grad_block, value_all)
        score_grad = rounded(probs * (grad_dots - dots_block[:, :, None]))
        query_part = jnp.einsum('hqk,khe->qhe', score_grad, key_all) * SCORE_SCALE
        return query_part.astype(jnp.bfloat16).reshape(block_rows, H * E)

    def key_block_grad(block_index):
        begin_row = (block_index * block_rows).astype(jnp.int32)
        key_block = lax.dynamic_slice_in_dim(key_all, begin_row, block_rows, 0)
        value_block = lax.dynamic_slice_in_dim(value_all, begin_row, block_rows, 0)
        label_block = lax.dynamic_slice_in_dim(frame_labels, begin_row, block_rows, 0)
        scores = jnp.einsum('qhe,khe->hqk', query_all, key_block) * SCORE_SCALE
        same_record = (frame_labels[:, None] == label_block[None, :])[None]
        probs = jnp.where(same_record, jnp.exp(jnp.where(same_record, scores, MASKED_SCORE) - log_norm[:, :, None]), 0.0)
        grad_dots = jnp.einsum('qhe,khe->hqk', grad_all, value_block)
        score_grad = rounded(probs * (grad_dots - row_dots[:, :, None]))
        key_part = jnp.einsum('hqk,qhe->khe', score_grad, query_all) * SCORE_SCALE
        value_part = jnp.einsum('hqk,qhe->khe', rounded(probs), grad_all)
        return (key_part.astype(jnp.bfloat16).reshape(block_rows, H * E), value_part.astype(jnp.bfloat16).reshape(block_rows, H * E))
    query_grad = lax.map(query_block_grad, jnp.arange(block_count, dtype=jnp.int32)).reshape(CTXLEN, H * E)
    key_blocks, value_blocks = lax.map(key_block_grad, jnp.arange(block_count, dtype=jnp.int32))
    key_grad = key_blocks.reshape(CTXLEN, H * E)
    value_grad = value_blocks.reshape(CTXLEN, H * E)
    return (layer_output, input_grad, query_grad, key_grad, value_grad, weight_grad, kernel_grad)

def reference(layer_input, query_heads, key_heads, value_heads, out_weight, conv_kernel, record_lengths, upstream_grad):
    outputs_list = []
    weight_total = jnp.zeros((D, H * E), jnp.float32)
    kernel_total = jnp.zeros((D, KW), jnp.float32)
    for group_index in range(GROUPS):
        lower = group_index * CTXLEN
        upper = lower + CTXLEN
        results = group_pass(layer_input[lower:upper], query_heads[lower:upper], key_heads[lower:upper], value_heads[lower:upper], out_weight, conv_kernel, record_lengths[group_index], upstream_grad[lower:upper])
        outputs_list.append(results[:5])
        weight_total = weight_total + results[5]
        kernel_total = kernel_total + results[6]
    layer_output = jnp.concatenate([entry[0] for entry in outputs_list], axis=0)
    input_grad = jnp.concatenate([entry[1] for entry in outputs_list], axis=0)
    query_grad = jnp.concatenate([entry[2] for entry in outputs_list], axis=0)
    key_grad = jnp.concatenate([entry[3] for entry in outputs_list], axis=0)
    value_grad = jnp.concatenate([entry[4] for entry in outputs_list], axis=0)
    return (layer_output, input_grad, query_grad, key_grad, value_grad, weight_total, kernel_total)
```

```python
import functools

import jax
import jax.numpy as jnp
from jax import lax
from jax.experimental import pallas as pl
from jax.experimental.pallas import tpu as pltpu
from jax.sharding import PartitionSpec as P

MESH = pl.DeviceIdType.MESH
BF = jnp.bfloat16
F32 = jnp.float32
H = 8
E = 64
SCALE = 0.125
NEG = -1e30
T = 128
KB = 256
NB = 4096 // KB


def vm(n):
    return [pl.BlockSpec(memory_space=pltpu.VMEM)] * n


def params(cid):
    return pltpu.CompilerParams(collective_id=cid, has_side_effects=True)


def meet_plane(me):
    barrier = pltpu.get_barrier_semaphore()

    def hello(d, _):
        pl.semaphore_signal(barrier, inc=1, device_id={"ctx": (me + 4 * d) % 32}, device_id_type=MESH)
        return 0

    lax.fori_loop(1, 8, hello, 0)
    pl.semaphore_wait(barrier, 7)


def meet_group(me):
    barrier = pltpu.get_barrier_semaphore()

    def hello(d, _):
        pl.semaphore_signal(barrier, inc=1, device_id={"ctx": (me + d) % 32}, device_id_type=MESH)
        return 0

    lax.fori_loop(1, 32, hello, 0)
    pl.semaphore_wait(barrier, 31)


def plane_copy(me, d, src, dst, send_sem, recv_sem):
    other = (me + 4 * d) % 32
    return pltpu.make_async_remote_copy(
        src_ref=src.at[other // 4],
        dst_ref=dst.at[me // 4],
        send_sem=send_sem.at[d],
        recv_sem=recv_sem.at[d],
        device_id={"ctx": other},
        device_id_type=MESH,
    )


def group_copy(me, d, src, dst, send_sem, recv_sem, by_head):
    other = (me + d) % 32
    return pltpu.make_async_remote_copy(
        src_ref=src.at[other // 4] if by_head else src.at[other],
        dst_ref=dst.at[me],
        send_sem=send_sem.at[d],
        recv_sem=recv_sem.at[d],
        device_id={"ctx": other},
        device_id_type=MESH,
    )


def gather_kernel(q_ref, k_ref, v_ref, kv_out, q_out, kvs, qs, ks, kr, qsnd, qrcv, own):
    me = lax.axis_index("ctx")
    for h in range(H):
        cols = slice(h * E, (h + 1) * E)
        kvs[h] = jnp.concatenate([k_ref[:, cols], v_ref[:, cols]], axis=1)
    qt = (q_ref[...].astype(F32) * SCALE).T.astype(BF)
    for h in range(H):
        qs[h] = qt[h * E : (h + 1) * E, :]
    meet_group(me)

    def start(d, _):
        group_copy(me, d, kvs, kv_out, ks, kr, True).start()
        return 0

    def start_q(d, _):
        plane_copy(me, d, qs, q_out, qsnd, qrcv).start()
        return 0

    lax.fori_loop(1, 8, start_q, 0)
    lax.fori_loop(1, 32, start, 0)
    a = pltpu.make_async_copy(kvs.at[me // 4], kv_out.at[me], own.at[0])
    b = pltpu.make_async_copy(qs.at[me // 4], q_out.at[me // 4], own.at[1])
    a.start()
    b.start()
    a.wait()
    b.wait()

    def done(d, _):
        group_copy(me, d, kvs, kv_out, ks, kr, True).wait()
        return 0

    def done_q(d, _):
        plane_copy(me, d, qs, q_out, qsnd, qrcv).wait()
        return 0

    lax.fori_loop(1, 8, done_q, 0)
    lax.fori_loop(1, 32, done, 0)


def gather_qkv(q, k, v):
    return pl.pallas_call(
        gather_kernel,
        name="gather_qkv",
        out_shape=(
            jax.ShapeDtypeStruct((32, T, 2 * E), BF),
            jax.ShapeDtypeStruct((H, E, T), BF),
        ),
        in_specs=vm(3),
        out_specs=tuple(vm(2)),
        scratch_shapes=[
            pltpu.VMEM((H, T, 2 * E), BF),
            pltpu.VMEM((H, E, T), BF),
            pltpu.SemaphoreType.DMA((32,)),
            pltpu.SemaphoreType.DMA((32,)),
            pltpu.SemaphoreType.DMA((8,)),
            pltpu.SemaphoreType.DMA((8,)),
            pltpu.SemaphoreType.DMA((2,)),
        ],
        compiler_params=params(0),
    )(q, k, v)


def plane_kernel(x_ref, y_ref, snd, rcv, own):
    me = lax.axis_index("ctx")
    meet_plane(me)

    def start(d, _):
        plane_copy(me, d, x_ref, y_ref, snd, rcv).start()
        return 0

    lax.fori_loop(1, 8, start, 0)
    a = pltpu.make_async_copy(x_ref.at[me // 4], y_ref.at[me // 4], own)
    a.start()
    a.wait()

    def done(d, _):
        plane_copy(me, d, x_ref, y_ref, snd, rcv).wait()
        return 0

    lax.fori_loop(1, 8, done, 0)


def plane_exchange(x, cid, name):
    return pl.pallas_call(
        plane_kernel,
        name=name,
        out_shape=jax.ShapeDtypeStruct(x.shape, x.dtype),
        in_specs=vm(1),
        out_specs=vm(1)[0],
        scratch_shapes=[
            pltpu.SemaphoreType.DMA((8,)),
            pltpu.SemaphoreType.DMA((8,)),
            pltpu.SemaphoreType.DMA,
        ],
        compiler_params=params(cid),
    )(x)


def spread_kernel(dq_ref, dkv_ref, dq_out, dkv_out, ks, kr, qsnd, qrcv, own):
    me = lax.axis_index("ctx")
    meet_group(me)

    def start(d, _):
        group_copy(me, d, dkv_ref, dkv_out, ks, kr, False).start()
        return 0

    def start_q(d, _):
        plane_copy(me, d, dq_ref, dq_out, qsnd, qrcv).start()
        return 0

    lax.fori_loop(1, 32, start, 0)
    lax.fori_loop(1, 8, start_q, 0)
    a = pltpu.make_async_copy(dkv_ref.at[me], dkv_out.at[me], own.at[0])
    b = pltpu.make_async_copy(dq_ref.at[me // 4], dq_out.at[me // 4], own.at[1])
    a.start()
    b.start()
    a.wait()
    b.wait()

    def done(d, _):
        group_copy(me, d, dkv_ref, dkv_out, ks, kr, False).wait()
        return 0

    def done_q(d, _):
        plane_copy(me, d, dq_ref, dq_out, qsnd, qrcv).wait()
        return 0

    lax.fori_loop(1, 8, done_q, 0)
    lax.fori_loop(1, 32, done, 0)


def finish_kernel(dq_ref, dkv_ref, dq_out, dk_out, dv_out):
    dq = (dq_ref[...].astype(F32).reshape(H * E, T) * SCALE).T
    dq_out[...] = dq.astype(BF)
    for h in range(H):
        total = dkv_ref[4 * h].astype(F32)
        for p in range(1, 4):
            total = total + dkv_ref[4 * h + p].astype(F32)
        cols = slice(h * E, (h + 1) * E)
        dk_out[:, cols] = total[:, :E].astype(BF)
        dv_out[:, cols] = total[:, E:].astype(BF)


def spread_grads(dq, dkv):
    dq_all, dkv_all = pl.pallas_call(
        spread_kernel,
        name="spread_grads",
        out_shape=(
            jax.ShapeDtypeStruct((H, E, T), BF),
            jax.ShapeDtypeStruct((32, T, 2 * E), BF),
        ),
        in_specs=vm(2),
        out_specs=tuple(vm(2)),
        scratch_shapes=[
            pltpu.SemaphoreType.DMA((32,)),
            pltpu.SemaphoreType.DMA((32,)),
            pltpu.SemaphoreType.DMA((8,)),
            pltpu.SemaphoreType.DMA((8,)),
            pltpu.SemaphoreType.DMA((2,)),
        ],
        compiler_params=params(3),
    )(dq, dkv)
    return pl.pallas_call(
        finish_kernel,
        name="finish_grads",
        out_shape=(jax.ShapeDtypeStruct((T, H * E), BF),) * 3,
        in_specs=vm(2),
        out_specs=tuple(vm(3)),
    )(dq_all, dkv_all)


def record_bounds(len_ref):
    g = lax.axis_index("dp")
    s1 = len_ref[g, 0]
    s2 = s1 + len_ref[g, 1]
    s3 = s2 + len_ref[g, 2]
    return s1, s2, s3, s3 + len_ref[g, 3]


def low_of(pos, b):
    return jnp.where(pos >= b[2], b[2], jnp.where(pos >= b[1], b[1], jnp.where(pos >= b[0], b[0], 0)))


def high_of(pos, b):
    return jnp.where(pos < b[0], b[0], jnp.where(pos < b[1], b[1], jnp.where(pos < b[2], b[2], b[3])))


def block_span(i, part, b):
    f0 = (i * 4 + part) * T
    pos = f0 + lax.broadcasted_iota(jnp.int32, (1, T), 1)
    lo, hi = low_of(pos, b), high_of(pos, b)
    first_lo, first_hi = low_of(f0, b), high_of(f0, b)
    last_hi = high_of(f0 + T - 1, b)
    kb0 = first_lo // KB
    kb1 = (last_hi + KB - 1) // KB
    same = first_hi == last_hi
    in0 = jnp.where(same, (first_lo + KB - 1) // KB, kb1)
    in1 = jnp.where(same, first_hi // KB, kb1)
    in0 = jnp.minimum(in0, kb1)
    in1 = jnp.maximum(in1, in0)
    return lo, hi, kb0, in0, in1, kb1


def fold(x, op):
    r = x.reshape(x.shape[0] // 8, 8, x.shape[1])
    return op(r, axis=0)


def forward_kernel(len_ref, kv_ref, q_ref, att_ref, lse_ref, kvt_ref, st):
    part = lax.axis_index("ctx") % 4
    b = record_bounds(len_ref)

    def turn(j, _):
        kvt_ref[j] = kv_ref[j].astype(F32).T.astype(BF)
        return 0

    lax.fori_loop(0, NB, turn, 0)

    def block(i, _):
        lo, hi, kb0, in0, in1, kb1 = block_span(i, part, b)
        qz = jnp.concatenate([q_ref[i], jnp.zeros((E, T), BF)], axis=0)

        def score(masked):
            def step(j, m):
                s = jnp.dot(kv_ref[j], qz, preferred_element_type=F32)
                if masked:
                    kpos = j * KB + lax.broadcasted_iota(jnp.int32, (KB, T), 0)
                    s = jnp.where((kpos >= lo) & (kpos < hi), s, NEG)
                st[j] = s
                return jnp.maximum(m, fold(s, jnp.max))

            return step

        m = jnp.full((8, T), NEG, F32)
        m = lax.fori_loop(kb0, in0, score(True), m)
        m = lax.fori_loop(in0, in1, score(False), m)
        m = lax.fori_loop(in1, kb1, score(True), m)
        m = jnp.max(m, axis=0, keepdims=True)

        def weigh(j, carry):
            l, acc = carry
            p = jnp.exp(st[j] - m)
            l = l + fold(p, jnp.sum)
            acc = acc + jnp.dot(kvt_ref[j], p.astype(BF), preferred_element_type=F32)
            return l, acc

        l, acc = lax.fori_loop(kb0, kb1, weigh, (jnp.zeros((8, T), F32), jnp.zeros((2 * E, T), F32)))
        l = jnp.sum(l, axis=0, keepdims=True)
        att_ref[i] = (acc[E:] / l).astype(BF)
        lse_ref[i] = m + jnp.log(l)
        return 0

    lax.fori_loop(0, H, block, 0)


def forward(lens, kv, q):
    return pl.pallas_call(
        forward_kernel,
        name="attention_forward",
        out_shape=(
            jax.ShapeDtypeStruct((H, E, T), BF),
            jax.ShapeDtypeStruct((H, 1, T), F32),
            jax.ShapeDtypeStruct((NB, 2 * E, KB), BF),
        ),
        in_specs=[pl.BlockSpec(memory_space=pltpu.SMEM)] + vm(2),
        out_specs=tuple(vm(3)),
        scratch_shapes=[pltpu.VMEM((NB, KB, T), F32)],
    )(lens, kv.reshape(NB, KB, 2 * E), q)


def backward_kernel(len_ref, kv_ref, kvt_ref, q_ref, do_ref, att_ref, lse_ref, dq_ref, dkv_ref, acc_ref):
    part = lax.axis_index("ctx") % 4
    b = record_bounds(len_ref)

    def clear(j, _):
        acc_ref[j] = jnp.zeros((KB, 2 * E), F32)
        return 0

    lax.fori_loop(0, NB, clear, 0)

    def block(i, _):
        lo, hi, kb0, in0, in1, kb1 = block_span(i, part, b)
        qt, dot = q_ref[i], do_ref[i]
        rows = jnp.sum(dot.astype(F32) * att_ref[i].astype(F32), axis=0, keepdims=True)
        lse = lse_ref[i]
        zero = jnp.zeros((E, T), BF)
        both = jnp.concatenate(
            [jnp.concatenate([qt, zero], axis=0), jnp.concatenate([zero, dot], axis=0)], axis=1
        )
        back = both.astype(F32).T.astype(BF)

        def step(masked):
            def body(j, dq):
                sd = jnp.dot(kv_ref[j], both, preferred_element_type=F32)
                p = jnp.exp(sd[:, :T] - lse)
                if masked:
                    kpos = j * KB + lax.broadcasted_iota(jnp.int32, (KB, T), 0)
                    p = jnp.where((kpos >= lo) & (kpos < hi), p, 0.0)
                ds = (p * (sd[:, T:] - rows)).astype(BF)
                dq = dq + jnp.dot(kvt_ref[j], ds, preferred_element_type=F32)
                acc_ref[j] += jnp.dot(
                    jnp.concatenate([ds, p.astype(BF)], axis=1), back, preferred_element_type=F32
                )
                return dq

            return body

        dq = jnp.zeros((2 * E, T), F32)
        dq = lax.fori_loop(kb0, in0, step(True), dq)
        dq = lax.fori_loop(in0, in1, step(False), dq)
        dq = lax.fori_loop(in1, kb1, step(True), dq)
        dq_ref[i] = dq[:E].astype(BF)
        return 0

    lax.fori_loop(0, H, block, 0)

    def put(j, _):
        dkv_ref[j] = acc_ref[j].astype(BF)
        return 0

    lax.fori_loop(0, NB, put, 0)


def backward(lens, kv, kvt, q, do, att, lse):
    dq, dkv = pl.pallas_call(
        backward_kernel,
        name="attention_backward",
        out_shape=(
            jax.ShapeDtypeStruct((H, E, T), BF),
            jax.ShapeDtypeStruct((NB, KB, 2 * E), BF),
        ),
        in_specs=[pl.BlockSpec(memory_space=pltpu.SMEM)] + vm(6),
        out_specs=tuple(vm(2)),
        scratch_shapes=[pltpu.VMEM((NB, KB, 2 * E), F32)],
    )(lens, kv.reshape(NB, KB, 2 * E), kvt, q, do, att, lse)
    return dq, dkv.reshape(32, T, 2 * E)


def everyone(me, d):
    other = (me + d) % 128
    return other, {"dp": other // 32, "ctx": other % 32}


def weight_kernel(w_ref, o_ref, ws, got, snd, rcv):
    me = lax.axis_index("dp") * 32 + lax.axis_index("ctx")
    barrier = pltpu.get_barrier_semaphore()

    def hello(d, _):
        _, where = everyone(me, d)
        pl.semaphore_signal(barrier, inc=1, device_id=where, device_id_type=MESH)
        return 0

    lax.fori_loop(1, 128, hello, 0)
    ws[...] = w_ref[...].astype(BF)
    pl.semaphore_wait(barrier, 127)

    def copy(d):
        other, where = everyone(me, d)
        return pltpu.make_async_remote_copy(
            src_ref=ws.at[other],
            dst_ref=got.at[d],
            send_sem=snd.at[d],
            recv_sem=rcv.at[d],
            device_id=where,
            device_id_type=MESH,
        )

    def start(d, _):
        copy(d).start()
        return 0

    lax.fori_loop(1, 128, start, 0)
    total = w_ref[me]

    def done(d, total):
        copy(d).wait()
        return total + got[d].astype(F32)

    o_ref[...] = lax.fori_loop(1, 128, done, total)


def weight_scatter(w):
    return pl.pallas_call(
        weight_kernel,
        name="weight_scatter",
        out_shape=jax.ShapeDtypeStruct((8, 512), F32),
        in_specs=vm(1),
        out_specs=vm(1)[0],
        scratch_shapes=[
            pltpu.VMEM((128, 8, 512), BF),
            pltpu.VMEM((128, 8, 512), BF),
            pltpu.SemaphoreType.DMA((128,)),
            pltpu.SemaphoreType.DMA((128,)),
        ],
        compiler_params=params(4),
    )(w.reshape(128, 8, 512))


def with_sides(x, width):
    n = 32
    up = [(i, i + 1) for i in range(n - 1)]
    down = [(j, i) for i, j in up]
    before = lax.ppermute(x[-width:], "ctx", up)
    after = lax.ppermute(x[:width], "ctx", down)
    return jnp.concatenate([before, x, after], axis=0)


def frame_ids(positions, sizes):
    ends = jnp.cumsum(sizes)
    counted = jnp.sum((positions[:, None] >= (ends - sizes)[None, :]).astype(jnp.int32), axis=1)
    inside = (positions >= 0) & (positions < ends[-1])
    return jnp.where(inside, counted - 1, -1)


def body(x, q, k, v, w, ck, lens, g):
    n, taps, half = T, 9, 4
    kv, qs = gather_qkv(q, k, v)
    att_t, lse, kvt = forward(lens, kv, qs)
    att_own = plane_exchange(att_t, 1, "attended_home")
    attended = att_own.reshape(H * E, T).T
    mixed = (
        x.astype(F32)
        + lax.dot_general(attended, w, (((1,), (1,)), ((), ())), preferred_element_type=F32)
    ).astype(BF)
    sizes = lax.dynamic_index_in_dim(lens, lax.axis_index("dp"), 0, keepdims=False)
    first = lax.axis_index("ctx") * n
    ids = frame_ids(first - half + jnp.arange(n + 2 * half, dtype=jnp.int32), sizes)
    own = ids[half : half + n]
    padded = with_sides(mixed, half).astype(F32)
    kf = ck.astype(F32).T
    conv = jnp.zeros((n, 1024), F32)
    for j in range(taps):
        same = (ids[j : j + n] == own)[:, None]
        conv = conv + jnp.where(same, padded[j : j + n] * kf[j][None], 0.0)
    gate = jax.nn.sigmoid(conv)
    layer_output = (mixed.astype(F32) + conv * gate).astype(BF)
    cg = (g.astype(F32) * gate * (1.0 + conv * (1.0 - gate))).astype(BF)
    cgf = cg.astype(F32)
    gp = with_sides(cg, half).astype(F32)
    back = jnp.zeros((n, 1024), F32)
    rows = []
    for j in range(taps):
        mirror = taps - 1 - j
        same = (ids[mirror : mirror + n] == own)[:, None]
        back = back + jnp.where(same, gp[mirror : mirror + n] * kf[j][None], 0.0)
        fore = (ids[j : j + n] == own)[:, None]
        rows.append(jnp.sum(jnp.where(fore, cgf * padded[j : j + n], 0.0), axis=0))
    input_grad = (g.astype(F32) + back).astype(BF)
    kernel_grad = lax.psum(jnp.stack(rows), ("dp", "ctx")).T
    wg = lax.dot_general(
        input_grad, attended, (((0,), (0,)), ((), ())), preferred_element_type=F32
    )
    ag_t = lax.dot_general(w, input_grad, (((0,), (1,)), ((), ())), preferred_element_type=F32).astype(BF)
    do = plane_exchange(ag_t.reshape(H, E, T), 2, "grad_out")
    dq, dkv = backward(lens, kv, kvt, qs, do, att_t, lse)
    dq, dk, dv = spread_grads(dq, dkv)
    return layer_output, input_grad, dq, dk, dv, weight_scatter(wg), kernel_grad


def solution(mesh):
    row = P(("dp", "ctx"), None)
    return jax.shard_map(
        body,
        mesh=mesh,
        in_specs=(row, row, row, row, P(), P(), P(), row),
        out_specs=(row, row, row, row, row, row, P()),
        check_vma=False,
    )
```

```python
import functools

import jax
import jax.numpy as jnp
from jax import lax
from jax.experimental import pallas as pl
from jax.experimental.pallas import tpu as pltpu
from jax.sharding import PartitionSpec as P

MESH = pl.DeviceIdType.MESH
BF = jnp.bfloat16
F32 = jnp.float32
H = 8
E = 64
SCALE = 0.125
NEG = -1e30
T = 128
KB = 256
NB = 4096 // KB


def vm(n):
    return [pl.BlockSpec(memory_space=pltpu.VMEM)] * n


def params(cid):
    return pltpu.CompilerParams(collective_id=cid, has_side_effects=True)


def barrier_hello(me):
    barrier = pltpu.get_barrier_semaphore()

    def hello(d, _):
        pl.semaphore_signal(barrier, inc=1, device_id={"ctx": (me + d) % 32}, device_id_type=MESH)
        return 0

    lax.fori_loop(1, 32, hello, 0)


def barrier_wait():
    pl.semaphore_wait(pltpu.get_barrier_semaphore(), 31)


def plane_copy(me, d, src, dst, send_sem, recv_sem):
    other = (me + 4 * d) % 32
    return pltpu.make_async_remote_copy(
        src_ref=src.at[other // 4],
        dst_ref=dst.at[me // 4],
        send_sem=send_sem.at[d],
        recv_sem=recv_sem.at[d],
        device_id={"ctx": other},
        device_id_type=MESH,
    )


def group_copy(me, d, src, dst, send_sem, recv_sem, by_head):
    other = (me + d) % 32
    return pltpu.make_async_remote_copy(
        src_ref=src.at[other // 4] if by_head else src.at[other],
        dst_ref=dst.at[me],
        send_sem=send_sem.at[d],
        recv_sem=recv_sem.at[d],
        device_id={"ctx": other},
        device_id_type=MESH,
    )


def gather_kernel(q_ref, k_ref, v_ref, x_ref, g_ref, kv_out, q_out, halo, kvs, qs, ks, kr, qsnd, qrcv, own, hsnd, hrcv):
    me = lax.axis_index("ctx")
    barrier_hello(me)
    for h in range(H):
        cols = slice(h * E, (h + 1) * E)
        kvs[h] = jnp.concatenate([k_ref[:, cols], v_ref[:, cols]], axis=1)
    qt = (q_ref[...].astype(F32) * SCALE).T.astype(BF)
    for h in range(H):
        qs[h] = qt[h * E : (h + 1) * E, :]
    barrier_wait()

    def start(d, _):
        group_copy(me, d, kvs, kv_out, ks, kr, True).start()
        return 0

    def start_q(d, _):
        plane_copy(me, d, qs, q_out, qsnd, qrcv).start()
        return 0

    def side(a, up):
        ref = (x_ref, g_ref)[a]
        return pltpu.make_async_remote_copy(
            src_ref=ref.at[pl.ds(T - 8, 8)] if up else ref.at[pl.ds(0, 8)],
            dst_ref=halo.at[a, 0 if up else 1],
            send_sem=hsnd.at[a, 0 if up else 1],
            recv_sem=hrcv.at[a, 0 if up else 1],
            device_id={"ctx": (me + (1 if up else 31)) % 32},
            device_id_type=MESH,
        )

    lax.fori_loop(1, 8, start_q, 0)
    lax.fori_loop(1, 32, start, 0)
    sides = [side(a, up) for a in range(2) for up in (True, False)]
    for c in sides:
        c.start()
    a = pltpu.make_async_copy(kvs.at[me // 4], kv_out.at[me], own.at[0])
    b = pltpu.make_async_copy(qs.at[me // 4], q_out.at[me // 4], own.at[1])
    a.start()
    b.start()
    a.wait()
    b.wait()

    def done(d, _):
        group_copy(me, d, kvs, kv_out, ks, kr, True).wait()
        return 0

    def done_q(d, _):
        plane_copy(me, d, qs, q_out, qsnd, qrcv).wait()
        return 0

    lax.fori_loop(1, 8, done_q, 0)
    lax.fori_loop(1, 32, done, 0)
    for c in sides:
        c.wait()


def gather_qkv(q, k, v, x, g):
    return pl.pallas_call(
        gather_kernel,
        name="gather_qkv",
        out_shape=(
            jax.ShapeDtypeStruct((32, T, 2 * E), BF),
            jax.ShapeDtypeStruct((H, E, T), BF),
            jax.ShapeDtypeStruct((2, 2, 8, 1024), BF),
        ),
        in_specs=vm(5),
        out_specs=tuple(vm(3)),
        scratch_shapes=[
            pltpu.VMEM((H, T, 2 * E), BF),
            pltpu.VMEM((H, E, T), BF),
            pltpu.SemaphoreType.DMA((32,)),
            pltpu.SemaphoreType.DMA((32,)),
            pltpu.SemaphoreType.DMA((8,)),
            pltpu.SemaphoreType.DMA((8,)),
            pltpu.SemaphoreType.DMA((2,)),
            pltpu.SemaphoreType.DMA((2, 2)),
            pltpu.SemaphoreType.DMA((2, 2)),
        ],
        compiler_params=params(0),
    )(q, k, v, x, g)


def mid_kernel(
    len_ref, att_ref, edge_ref, x_ref, g_ref, halo, w_ref, ck_ref,
    lo_ref, ig_ref, do_ref, wg_ref, kg_ref,
    at_in, eb, am, ap, igs, igp, dos, mx, ge, cs, mk,
    asnd, arcv, esnd, ercv, dsnd, drcv, psnd, prcv, own,
):
    dp, me = lax.axis_index("dp"), lax.axis_index("ctx")
    core, part, plane = dp % 2, me % 4, me // 4
    partner = {"dp": dp - core + (1 - core)}
    barrier = pltpu.get_barrier_semaphore()

    def signal(where):
        pl.semaphore_signal(barrier, inc=1, device_id=where, device_id_type=MESH)

    signal(partner)

    def hello(d, _):
        signal({"ctx": (me + 4 * d) % 32})
        return 0

    def hello_edge(i, _):
        signal({"ctx": (4 * i + part + 1) % 32})
        signal({"ctx": (4 * i + part + 31) % 32})
        return 0

    lax.fori_loop(1, 8, hello, 0)
    lax.fori_loop(0, 8, hello_edge, 0)

    s1, s2, s3, s4 = record_bounds(len_ref)

    def label(pos):
        one = lambda s: jnp.where(pos >= s, 1, 0)
        n = one(s1) + one(s2) + one(s3)
        return jnp.where((pos >= 0) & (pos < s4), n, -1)

    pos = me * T - 4 + lax.broadcasted_iota(jnp.int32, (136, 128), 0)
    mine = label(pos)
    for j in range(9):
        mk[j] = jnp.where(label(pos + (j - 4)) == mine, 1.0, 0.0)
    ge[0:8] = halo[1, 0].astype(F32)
    ge[8:136] = g_ref[...].astype(F32)
    ge[136:144] = halo[1, 1].astype(F32)

    pl.semaphore_wait(barrier, 24)

    def att_copy(d):
        return plane_copy(me, d, att_ref, at_in, asnd, arcv)

    def edge_copy(i, late):
        other = (4 * i + part + (1 if late else 31)) % 32
        return pltpu.make_async_remote_copy(
            src_ref=edge_ref.at[i, 1 if late else 0],
            dst_ref=eb.at[0 if late else 1, plane],
            send_sem=esnd.at[1 if late else 0, i],
            recv_sem=ercv.at[0 if late else 1, plane],
            device_id={"ctx": other},
            device_id_type=MESH,
        )

    def edge_arrival(h, side):
        return pltpu.make_async_remote_copy(
            src_ref=edge_ref.at[0, 0],
            dst_ref=eb.at[side, h],
            send_sem=esnd.at[0, 0],
            recv_sem=ercv.at[side, h],
            device_id=partner,
            device_id_type=MESH,
        )

    def start_att(d, _):
        att_copy(d).start()
        return 0

    def start_edge(i, _):
        edge_copy(i, True).start()
        edge_copy(i, False).start()
        return 0

    lax.fori_loop(1, 8, start_att, 0)
    lax.fori_loop(0, 8, start_edge, 0)
    a = pltpu.make_async_copy(att_ref.at[plane], at_in.at[plane], own.at[0])
    a.start()
    a.wait()

    def wait_att(d, _):
        att_copy(d).wait()
        return 0

    def wait_edge(i, _):
        edge_copy(i, True).wait_send()
        edge_copy(i, False).wait_send()
        edge_arrival(i, 0).wait_recv()
        edge_arrival(i, 1).wait_recv()
        return 0

    lax.fori_loop(1, 8, wait_att, 0)
    lax.fori_loop(0, 8, wait_edge, 0)
    am[...] = at_in[...].astype(F32).reshape(H * E, T).T.astype(BF)

    def pair(src, dst, n):
        return pltpu.make_async_remote_copy(
            src_ref=src,
            dst_ref=dst,
            send_sem=psnd.at[n],
            recv_sem=prcv.at[n],
            device_id=partner,
            device_id_type=MESH,
        )

    send_att = pair(am, ap, 0)
    send_att.start()
    sides = jnp.concatenate(
        [jnp.concatenate([eb[s, h][:, :E] for h in range(H)], axis=1) for s in range(2)], axis=0
    )

    NT = (((1,), (1,)), ((), ()))

    def chunk(c, _):
        cols = pl.ds(pl.multiple_of(c * 128, 128), 128)
        wc = w_ref[cols, :]
        main = lax.dot_general(am[...], wc, NT, preferred_element_type=F32)
        rim = lax.dot_general(sides, wc, NT, preferred_element_type=F32)
        rnd = lambda y: y.astype(BF).astype(F32)
        mx[8:136] = rnd(x_ref[:, cols].astype(F32) + main)
        mx[0:8] = rnd(halo[0, 0, :, cols].astype(F32) + rim[0:8])
        mx[136:144] = rnd(halo[0, 1, :, cols].astype(F32) + rim[8:16])
        conv = jnp.zeros((136, 128), F32)
        for j in range(9):
            conv = conv + mx[pl.ds(j, 136)] * mk[j] * ck_ref[j : j + 1, cols]
        gate = jax.nn.sigmoid(conv)
        cg = ge[pl.ds(4, 136), cols] * gate * (1.0 + conv * (1.0 - gate))
        cs[...] = rnd(cg)
        silu = conv * gate
        lo_ref[:, cols] = (mx[8:136] + silu[4:132]).astype(BF)
        back = ge[8:136, cols]
        for j in range(9):
            back = back + cs[pl.ds(8 - j, 128)] * mk[8 - j, pl.ds(4, 128)] * ck_ref[j : j + 1, cols]
        ig = back.astype(BF)
        ig_ref[:, cols] = ig
        igs[c // 2, :, pl.ds(pl.multiple_of((c % 2) * 128, 128), 128)] = ig
        cg_own = cs[pl.ds(4, 128)]
        rows = []
        for j in range(9):
            rows.append(
                jnp.sum(cg_own * mx[pl.ds(4 + j, 128)] * mk[j, pl.ds(4, 128)], axis=0, keepdims=True)
            )
        rows.append(jnp.zeros((7, 128), F32))
        kg_ref[c] = jnp.concatenate(rows, axis=0)
        return 0

    lax.fori_loop(0, 8, chunk, 0)
    send_ig = [pair(igs.at[2 * z + 1 - core], igp.at[z], 1 + z) for z in range(2)]
    for c in send_ig:
        c.start()
    ag = jnp.zeros((T, H * E), F32)
    for z in range(4):
        ag = ag + jnp.dot(igs[z], w_ref[z * 256 : (z + 1) * 256, :], preferred_element_type=F32)
    dos[...] = ag.astype(BF).astype(F32).T.astype(BF).reshape(H, E, T)

    def do_copy(d):
        return plane_copy(me, d, dos, do_ref, dsnd, drcv)

    def start_do(d, _):
        do_copy(d).start()
        return 0

    lax.fori_loop(1, 8, start_do, 0)
    b = pltpu.make_async_copy(dos.at[plane], do_ref.at[plane], own.at[1])
    b.start()
    send_att.wait()
    for c in send_ig:
        c.wait()
    TN = (((0,), (0,)), ((), ()))
    for z in range(2):
        wg = lax.dot_general(igs[2 * z + core], am[...], TN, preferred_element_type=F32)
        wg = wg + lax.dot_general(igp[z], ap[...], TN, preferred_element_type=F32)
        wg_ref[z * 32 : (z + 1) * 32] = wg.reshape(32, 8, H * E).astype(BF)
    b.wait()

    def wait_do(d, _):
        do_copy(d).wait()
        return 0

    lax.fori_loop(1, 8, wait_do, 0)


def middle(lens, att, edge, x, g, halo, w, ck):
    sem = pltpu.SemaphoreType.DMA
    return pl.pallas_call(
        mid_kernel,
        name="middle",
        out_shape=(
            jax.ShapeDtypeStruct((T, 1024), BF),
            jax.ShapeDtypeStruct((T, 1024), BF),
            jax.ShapeDtypeStruct((H, E, T), BF),
            jax.ShapeDtypeStruct((64, 8, H * E), BF),
            jax.ShapeDtypeStruct((8, 16, 128), F32),
        ),
        in_specs=[pl.BlockSpec(memory_space=pltpu.SMEM)] + vm(7),
        out_specs=tuple(vm(5)),
        scratch_shapes=[
            pltpu.VMEM((H, E, T), BF),
            pltpu.VMEM((2, H, 8, 128), BF),
            pltpu.VMEM((T, H * E), BF),
            pltpu.VMEM((T, H * E), BF),
            pltpu.VMEM((4, T, 256), BF),
            pltpu.VMEM((2, T, 256), BF),
            pltpu.VMEM((H, E, T), BF),
            pltpu.VMEM((144, 128), F32),
            pltpu.VMEM((144, 1024), F32),
            pltpu.VMEM((136, 128), F32),
            pltpu.VMEM((9, 136, 128), F32),
            sem((8,)),
            sem((8,)),
            sem((2, 8)),
            sem((2, 8)),
            sem((8,)),
            sem((8,)),
            sem((3,)),
            sem((3,)),
            sem((2,)),
        ],
        compiler_params=params(1),
    )(lens, att, edge, x, g, halo, w, ck)


def spread_kernel(
    dq_ref, dkv_ref, wg_ref, kg_ref, dq_out, dk_out, dv_out, wo_ref, ko_ref,
    dq_in, dkv_in, wg_in, k1, k2, ksum, kall,
    ks, kr, qsnd, qrcv, wsnd, wrcv, s1, r1, s2, r2, s3, r3, own,
):
    dp, me = lax.axis_index("dp"), lax.axis_index("ctx")
    core, part, plane = dp % 2, me % 4, me // 4
    chip = (dp // 2) * 32 + me
    barrier = pltpu.get_barrier_semaphore()

    def chip_at(d):
        other = (chip + d) % 64
        return other, {"dp": (other // 32) * 2 + core, "ctx": other % 32}

    def column_at(d):
        other = (dp * 4 + part + d) % 16
        return {"dp": other // 4, "ctx": plane * 4 + other % 4}

    def hello(d, _):
        pl.semaphore_signal(barrier, inc=1, device_id=chip_at(d)[1], device_id_type=MESH)
        return 0

    def hello_column(d, _):
        where = {"dp": (d // 4) * 2 + 1 - core, "ctx": plane * 4 + d % 4}
        pl.semaphore_signal(barrier, inc=1, device_id=where, device_id_type=MESH)
        return 0

    lax.fori_loop(1, 64, hello, 0)
    lax.fori_loop(0, 8, hello_column, 0)
    pl.semaphore_wait(barrier, 71)

    def loop(n, f):
        def step(d, _):
            f(d)
            return 0

        lax.fori_loop(1, n, step, 0)

    def w_copy(d):
        other, where = chip_at(d)
        return pltpu.make_async_remote_copy(
            src_ref=wg_ref.at[other],
            dst_ref=wg_in.at[d],
            send_sem=wsnd.at[d],
            recv_sem=wrcv.at[d],
            device_id=where,
            device_id_type=MESH,
        )

    def column_copy(d):
        return pltpu.make_async_remote_copy(
            src_ref=ksum.at[0],
            dst_ref=k2.at[dp * 4 + part],
            send_sem=s2.at[d],
            recv_sem=r2.at[d],
            device_id=column_at(d),
            device_id_type=MESH,
        )

    def back_copy(d):
        return pltpu.make_async_remote_copy(
            src_ref=ksum.at[1],
            dst_ref=kall.at[plane],
            send_sem=s3.at[d],
            recv_sem=r3.at[d],
            device_id={"ctx": (me + 4 * d) % 32},
            device_id_type=MESH,
        )

    rows = lambda d: plane_copy(me, d, kg_ref, k1, s1, r1)
    grads = lambda d: group_copy(me, d, dkv_ref, dkv_in, ks, kr, False)
    queries = lambda d: plane_copy(me, d, dq_ref, dq_in, qsnd, qrcv)
    loop(8, lambda d: rows(d).start())
    loop(32, lambda d: grads(d).start())
    loop(8, lambda d: queries(d).start())
    loop(64, lambda d: w_copy(d).start())
    a = pltpu.make_async_copy(dkv_ref.at[me], dkv_in.at[me], own.at[0])
    b = pltpu.make_async_copy(dq_ref.at[plane], dq_in.at[plane], own.at[1])
    c = pltpu.make_async_copy(kg_ref.at[plane], k1.at[plane], own.at[2])
    for copy in (a, b, c):
        copy.start()
    for copy in (a, b, c):
        copy.wait()
    loop(8, lambda d: rows(d).wait())
    ksum[0] = jnp.sum(k1[...], axis=0)
    k2[dp * 4 + part] = ksum[0]
    loop(16, lambda d: column_copy(d).start())
    loop(16, lambda d: column_copy(d).wait())
    ksum[1] = jnp.sum(k2[...], axis=0)
    kall[plane] = ksum[1]
    loop(8, lambda d: back_copy(d).start())
    loop(8, lambda d: queries(d).wait())
    dq_out[...] = (dq_in[...].astype(F32).reshape(H * E, T) * SCALE).T.astype(BF)
    loop(32, lambda d: grads(d).wait())
    for h in range(H):
        total = dkv_in[4 * h].astype(F32)
        for p in range(1, 4):
            total = total + dkv_in[4 * h + p].astype(F32)
        cols = slice(h * E, (h + 1) * E)
        dk_out[:, cols] = total[:, :E].astype(BF)
        dv_out[:, cols] = total[:, E:].astype(BF)

    def add(d, total):
        w_copy(d).wait()
        return total + wg_in[d].astype(F32)

    wo_ref[...] = lax.fori_loop(1, 64, add, wg_ref[chip].astype(F32))
    loop(8, lambda d: back_copy(d).wait())
    ko_ref[...] = kall[...]


def spread_grads(dq, dkv, wg, kg):
    sem = pltpu.SemaphoreType.DMA
    return pl.pallas_call(
        spread_kernel,
        name="spread_grads",
        out_shape=(jax.ShapeDtypeStruct((T, H * E), BF),) * 3
        + (jax.ShapeDtypeStruct((8, H * E), F32), jax.ShapeDtypeStruct((8, 16, 128), F32)),
        in_specs=vm(4),
        out_specs=tuple(vm(5)),
        scratch_shapes=[
            pltpu.VMEM((H, E, T), BF),
            pltpu.VMEM((32, T, 2 * E), BF),
            pltpu.VMEM((64, 8, H * E), BF),
            pltpu.VMEM((8, 16, 128), F32),
            pltpu.VMEM((16, 16, 128), F32),
            pltpu.VMEM((2, 16, 128), F32),
            pltpu.VMEM((8, 16, 128), F32),
            sem((32,)),
            sem((32,)),
            sem((8,)),
            sem((8,)),
            sem((64,)),
            sem((64,)),
            sem((8,)),
            sem((8,)),
            sem((16,)),
            sem((16,)),
            sem((8,)),
            sem((8,)),
            sem((3,)),
        ],
        compiler_params=params(2),
    )(dq, dkv, wg, kg)


def record_bounds(len_ref):
    g = lax.axis_index("dp")
    s1 = len_ref[g, 0]
    s2 = s1 + len_ref[g, 1]
    s3 = s2 + len_ref[g, 2]
    return s1, s2, s3, s3 + len_ref[g, 3]


def low_of(pos, b):
    return jnp.where(pos >= b[2], b[2], jnp.where(pos >= b[1], b[1], jnp.where(pos >= b[0], b[0], 0)))


def high_of(pos, b):
    return jnp.where(pos < b[0], b[0], jnp.where(pos < b[1], b[1], jnp.where(pos < b[2], b[2], b[3])))


def block_span(i, part, b):
    f0 = (i * 4 + part) * T
    pos = f0 + lax.broadcasted_iota(jnp.int32, (1, T), 1)
    lo, hi = low_of(pos, b), high_of(pos, b)
    first_lo, first_hi = low_of(f0, b), high_of(f0, b)
    last_hi = high_of(f0 + T - 1, b)
    kb0 = first_lo // KB
    kb1 = (last_hi + KB - 1) // KB
    same = first_hi == last_hi
    in0 = jnp.where(same, (first_lo + KB - 1) // KB, kb1)
    in1 = jnp.where(same, first_hi // KB, kb1)
    in0 = jnp.minimum(in0, kb1)
    in1 = jnp.maximum(in1, in0)
    return lo, hi, kb0, in0, in1, kb1


def fold(x, op):
    r = x.reshape(x.shape[0] // 8, 8, x.shape[1])
    return op(r, axis=0)


def forward_kernel(len_ref, kv_ref, q_ref, att_ref, edge_ref, lse_ref, kvt_ref, st):
    part = lax.axis_index("ctx") % 4
    b = record_bounds(len_ref)

    def turn(j, _):
        kvt_ref[j] = kv_ref[j].astype(F32).T.astype(BF)
        return 0

    lax.fori_loop(0, NB, turn, 0)

    def block(i, _):
        lo, hi, kb0, in0, in1, kb1 = block_span(i, part, b)
        qz = jnp.concatenate([q_ref[i], jnp.zeros((E, T), BF)], axis=0)

        def score(masked):
            def step(j, m):
                s = jnp.dot(kv_ref[j], qz, preferred_element_type=F32)
                if masked:
                    kpos = j * KB + lax.broadcasted_iota(jnp.int32, (KB, T), 0)
                    s = jnp.where((kpos >= lo) & (kpos < hi), s, NEG)
                st[j] = s
                return jnp.maximum(m, fold(s, jnp.max))

            return step

        m = jnp.full((8, T), NEG, F32)
        m = lax.fori_loop(kb0, in0, score(True), m)
        m = lax.fori_loop(in0, in1, score(False), m)
        m = lax.fori_loop(in1, kb1, score(True), m)
        m = jnp.max(m, axis=0, keepdims=True)

        def weigh(j, carry):
            l, acc = carry
            p = jnp.exp(st[j] - m)
            l = l + fold(p, jnp.sum)
            acc = acc + jnp.dot(kvt_ref[j], p.astype(BF), preferred_element_type=F32)
            return l, acc

        l, acc = lax.fori_loop(kb0, kb1, weigh, (jnp.zeros((8, T), F32), jnp.zeros((2 * E, T), F32)))
        l = jnp.sum(l, axis=0, keepdims=True)
        out = acc[E:] / l
        att_ref[i] = out.astype(BF)
        wide = jnp.concatenate([out, jnp.zeros((E, T), F32)], axis=0).T
        edge_ref[i, 0] = wide[:8].astype(BF)
        edge_ref[i, 1] = wide[T - 8 :].astype(BF)
        lse_ref[i] = m + jnp.log(l)
        return 0

    lax.fori_loop(0, H, block, 0)


def forward(lens, kv, q):
    return pl.pallas_call(
        forward_kernel,
        name="attention_forward",
        out_shape=(
            jax.ShapeDtypeStruct((H, E, T), BF),
            jax.ShapeDtypeStruct((H, 2, 8, 2 * E), BF),
            jax.ShapeDtypeStruct((H, 1, T), F32),
            jax.ShapeDtypeStruct((NB, 2 * E, KB), BF),
        ),
        in_specs=[pl.BlockSpec(memory_space=pltpu.SMEM)] + vm(2),
        out_specs=tuple(vm(4)),
        scratch_shapes=[pltpu.VMEM((NB, KB, T), F32)],
    )(lens, kv.reshape(NB, KB, 2 * E), q)


def backward_kernel(len_ref, kv_ref, kvt_ref, q_ref, do_ref, att_ref, lse_ref, dq_ref, dkv_ref, acc_ref):
    part = lax.axis_index("ctx") % 4
    b = record_bounds(len_ref)

    def clear(j, _):
        acc_ref[j] = jnp.zeros((KB, 2 * E), F32)
        return 0

    lax.fori_loop(0, NB, clear, 0)

    def block(i, _):
        lo, hi, kb0, in0, in1, kb1 = block_span(i, part, b)
        qt, dot = q_ref[i], do_ref[i]
        rows = jnp.sum(dot.astype(F32) * att_ref[i].astype(F32), axis=0, keepdims=True)
        lse = lse_ref[i]
        zero = jnp.zeros((E, T), BF)
        both = jnp.concatenate(
            [jnp.concatenate([qt, zero], axis=0), jnp.concatenate([zero, dot], axis=0)], axis=1
        )
        back = both.astype(F32).T.astype(BF)

        def step(masked):
            def body(j, dq):
                sd = jnp.dot(kv_ref[j], both, preferred_element_type=F32)
                p = jnp.exp(sd[:, :T] - lse)
                if masked:
                    kpos = j * KB + lax.broadcasted_iota(jnp.int32, (KB, T), 0)
                    p = jnp.where((kpos >= lo) & (kpos < hi), p, 0.0)
                ds = (p * (sd[:, T:] - rows)).astype(BF)
                dq = dq + jnp.dot(kvt_ref[j], ds, preferred_element_type=F32)
                acc_ref[j] += jnp.dot(
                    jnp.concatenate([ds, p.astype(BF)], axis=1), back, preferred_element_type=F32
                )
                return dq

            return body

        dq = jnp.zeros((2 * E, T), F32)
        dq = lax.fori_loop(kb0, in0, step(True), dq)
        dq = lax.fori_loop(in0, in1, step(False), dq)
        dq = lax.fori_loop(in1, kb1, step(True), dq)
        dq_ref[i] = dq[:E].astype(BF)
        return 0

    lax.fori_loop(0, H, block, 0)

    def put(j, _):
        dkv_ref[j] = acc_ref[j].astype(BF)
        return 0

    lax.fori_loop(0, NB, put, 0)


def backward(lens, kv, kvt, q, do, att, lse):
    dq, dkv = pl.pallas_call(
        backward_kernel,
        name="attention_backward",
        out_shape=(
            jax.ShapeDtypeStruct((H, E, T), BF),
            jax.ShapeDtypeStruct((NB, KB, 2 * E), BF),
        ),
        in_specs=[pl.BlockSpec(memory_space=pltpu.SMEM)] + vm(6),
        out_specs=tuple(vm(2)),
        scratch_shapes=[pltpu.VMEM((NB, KB, 2 * E), F32)],
    )(lens, kv.reshape(NB, KB, 2 * E), kvt, q, do, att, lse)
    return dq, dkv.reshape(32, T, 2 * E)


def body(x, q, k, v, w, ck, lens, g):
    kv, qs, halo = gather_qkv(q, k, v, x, g)
    att, edge, lse, kvt = forward(lens, kv, qs)
    layer_output, input_grad, do, wg, kg = middle(lens, att, edge, x, g, halo, w, ck.astype(F32).T)
    dq, dkv = backward(lens, kv, kvt, qs, do, att, lse)
    dq, dk, dv, out_weight_grad, kg = spread_grads(dq, dkv, wg, kg)
    kernel_grad = jnp.transpose(kg[:, :9], (0, 2, 1)).reshape(1024, 9)
    return layer_output, input_grad, dq, dk, dv, out_weight_grad, kernel_grad


def solution(mesh):
    row = P(("dp", "ctx"), None)
    return jax.shard_map(
        body,
        mesh=mesh,
        in_specs=(row, row, row, row, P(), P(), P(), row),
        out_specs=(row, row, row, row, row, row, P()),
        check_vma=False,
    )
```

```python
import functools

import jax
import jax.numpy as jnp
from jax import lax
from jax.experimental import pallas as pl
from jax.experimental.pallas import tpu as pltpu
from jax.sharding import PartitionSpec as P

MESH = pl.DeviceIdType.MESH
BF = jnp.bfloat16
F32 = jnp.float32
H = 8
E = 64
SCALE = 0.125
NEG = -1e30
T = 128
KB = 256
NB = 4096 // KB
U = 4


def vm(n):
    return [pl.BlockSpec(memory_space=pltpu.VMEM)] * n


def params(cid):
    return pltpu.CompilerParams(collective_id=cid, has_side_effects=True)


def barrier_hello(me):
    barrier = pltpu.get_barrier_semaphore()

    def hello(d, _):
        pl.semaphore_signal(barrier, inc=1, device_id={"ctx": (me + d) % 32}, device_id_type=MESH)
        return 0

    lax.fori_loop(1, 32, hello, 0)


def barrier_wait():
    pl.semaphore_wait(pltpu.get_barrier_semaphore(), 31)


def plane_copy(me, d, src, dst, send_sem, recv_sem):
    other = (me + 4 * d) % 32
    return pltpu.make_async_remote_copy(
        src_ref=src.at[other // 4],
        dst_ref=dst.at[me // 4],
        send_sem=send_sem.at[d],
        recv_sem=recv_sem.at[d],
        device_id={"ctx": other},
        device_id_type=MESH,
    )


def group_copy(me, d, src, dst, send_sem, recv_sem, by_head):
    other = (me + d) % 32
    return pltpu.make_async_remote_copy(
        src_ref=src.at[other // 4] if by_head else src.at[other],
        dst_ref=dst.at[me],
        send_sem=send_sem.at[d],
        recv_sem=recv_sem.at[d],
        device_id={"ctx": other},
        device_id_type=MESH,
    )


def gather_kernel(q_ref, k_ref, v_ref, x_ref, g_ref, kv_out, q_out, halo, kvs, qs, ks, kr, qsnd, qrcv, own, hsnd, hrcv):
    me = lax.axis_index("ctx")
    barrier_hello(me)
    for h in range(H):
        cols = slice(h * E, (h + 1) * E)
        kvs[h] = jnp.concatenate([k_ref[:, cols], v_ref[:, cols]], axis=1)
    qt = (q_ref[...].astype(F32) * SCALE).T.astype(BF)
    for h in range(H):
        qs[h] = qt[h * E : (h + 1) * E, :]
    barrier_wait()

    def start(d, _):
        group_copy(me, d, kvs, kv_out, ks, kr, True).start()
        return 0

    def start_q(d, _):
        plane_copy(me, d, qs, q_out, qsnd, qrcv).start()
        return 0

    def side(a, up):
        ref = (x_ref, g_ref)[a]
        return pltpu.make_async_remote_copy(
            src_ref=ref.at[pl.ds(T - 8, 8)] if up else ref.at[pl.ds(0, 8)],
            dst_ref=halo.at[a, 0 if up else 1],
            send_sem=hsnd.at[a, 0 if up else 1],
            recv_sem=hrcv.at[a, 0 if up else 1],
            device_id={"ctx": (me + (1 if up else 31)) % 32},
            device_id_type=MESH,
        )

    lax.fori_loop(1, 8, start_q, 0)
    lax.fori_loop(1, 32, start, 0)
    sides = [side(a, up) for a in range(2) for up in (True, False)]
    for c in sides:
        c.start()
    a = pltpu.make_async_copy(kvs.at[me // 4], kv_out.at[me], own.at[0])
    b = pltpu.make_async_copy(qs.at[me // 4], q_out.at[me // 4], own.at[1])
    a.start()
    b.start()
    a.wait()
    b.wait()

    def done(d, _):
        group_copy(me, d, kvs, kv_out, ks, kr, True).wait()
        return 0

    def done_q(d, _):
        plane_copy(me, d, qs, q_out, qsnd, qrcv).wait()
        return 0

    lax.fori_loop(1, 8, done_q, 0)
    lax.fori_loop(1, 32, done, 0)
    for c in sides:
        c.wait()


def gather_qkv(q, k, v, x, g):
    return pl.pallas_call(
        gather_kernel,
        name="gather_qkv",
        out_shape=(
            jax.ShapeDtypeStruct((32, T, 2 * E), BF),
            jax.ShapeDtypeStruct((H, E, T), BF),
            jax.ShapeDtypeStruct((2, 2, 8, 1024), BF),
        ),
        in_specs=vm(5),
        out_specs=tuple(vm(3)),
        scratch_shapes=[
            pltpu.VMEM((H, T, 2 * E), BF),
            pltpu.VMEM((H, E, T), BF),
            pltpu.SemaphoreType.DMA((32,)),
            pltpu.SemaphoreType.DMA((32,)),
            pltpu.SemaphoreType.DMA((8,)),
            pltpu.SemaphoreType.DMA((8,)),
            pltpu.SemaphoreType.DMA((2,)),
            pltpu.SemaphoreType.DMA((2, 2)),
            pltpu.SemaphoreType.DMA((2, 2)),
        ],
        compiler_params=params(0),
    )(q, k, v, x, g)


def mid_kernel(
    len_ref, att_ref, edge_ref, x_ref, g_ref, halo, w_ref, ck_ref,
    lo_ref, ig_ref, do_ref, wg_ref, kg_ref,
    at_in, eb, am, ap, igs, igp, dos, mx, ge, cs, mk,
    asnd, arcv, esnd, ercv, dsnd, drcv, psnd, prcv, own,
):
    dp, me = lax.axis_index("dp"), lax.axis_index("ctx")
    core, part, plane = dp % 2, me % 4, me // 4
    partner = {"dp": dp - core + (1 - core)}
    barrier = pltpu.get_barrier_semaphore()

    def signal(where):
        pl.semaphore_signal(barrier, inc=1, device_id=where, device_id_type=MESH)

    signal(partner)

    def hello(d, _):
        signal({"ctx": (me + 4 * d) % 32})
        return 0

    def hello_edge(i, _):
        signal({"ctx": (4 * i + part + 1) % 32})
        signal({"ctx": (4 * i + part + 31) % 32})
        return 0

    lax.fori_loop(1, 8, hello, 0)
    lax.fori_loop(0, 8, hello_edge, 0)

    s1, s2, s3, s4 = record_bounds(len_ref)

    def label(pos):
        one = lambda s: jnp.where(pos >= s, 1, 0)
        n = one(s1) + one(s2) + one(s3)
        return jnp.where((pos >= 0) & (pos < s4), n, -1)

    pos = me * T - 4 + lax.broadcasted_iota(jnp.int32, (136, 128), 0)
    mine = label(pos)
    for j in range(9):
        mk[j] = jnp.where(label(pos + (j - 4)) == mine, 1.0, 0.0)
    ge[0:8] = halo[1, 0].astype(F32)
    ge[8:136] = g_ref[...].astype(F32)
    ge[136:144] = halo[1, 1].astype(F32)

    pl.semaphore_wait(barrier, 24)

    def att_copy(d):
        return plane_copy(me, d, att_ref, at_in, asnd, arcv)

    def edge_copy(i, late):
        other = (4 * i + part + (1 if late else 31)) % 32
        return pltpu.make_async_remote_copy(
            src_ref=edge_ref.at[i, 1 if late else 0],
            dst_ref=eb.at[0 if late else 1, plane],
            send_sem=esnd.at[1 if late else 0, i],
            recv_sem=ercv.at[0 if late else 1, plane],
            device_id={"ctx": other},
            device_id_type=MESH,
        )

    def edge_arrival(h, side):
        return pltpu.make_async_remote_copy(
            src_ref=edge_ref.at[0, 0],
            dst_ref=eb.at[side, h],
            send_sem=esnd.at[0, 0],
            recv_sem=ercv.at[side, h],
            device_id=partner,
            device_id_type=MESH,
        )

    def start_att(d, _):
        att_copy(d).start()
        return 0

    def start_edge(i, _):
        edge_copy(i, True).start()
        edge_copy(i, False).start()
        return 0

    lax.fori_loop(1, 8, start_att, 0)
    lax.fori_loop(0, 8, start_edge, 0)
    a = pltpu.make_async_copy(att_ref.at[plane], at_in.at[plane], own.at[0])
    a.start()
    a.wait()

    def wait_att(d, _):
        att_copy(d).wait()
        return 0

    def wait_edge(i, _):
        edge_copy(i, True).wait_send()
        edge_copy(i, False).wait_send()
        edge_arrival(i, 0).wait_recv()
        edge_arrival(i, 1).wait_recv()
        return 0

    lax.fori_loop(1, 8, wait_att, 0)
    lax.fori_loop(0, 8, wait_edge, 0)
    am[...] = at_in[...].astype(F32).reshape(H * E, T).T.astype(BF)

    def pair(src, dst, n):
        return pltpu.make_async_remote_copy(
            src_ref=src,
            dst_ref=dst,
            send_sem=psnd.at[n],
            recv_sem=prcv.at[n],
            device_id=partner,
            device_id_type=MESH,
        )

    send_att = pair(am, ap, 0)
    send_att.start()
    sides = jnp.concatenate(
        [jnp.concatenate([eb[s, h][:, :E] for h in range(H)], axis=1) for s in range(2)], axis=0
    )

    NT = (((1,), (1,)), ((), ()))

    def chunk(c, _):
        cols = pl.ds(pl.multiple_of(c * 128, 128), 128)
        wc = w_ref[cols, :]
        main = lax.dot_general(am[...], wc, NT, preferred_element_type=F32)
        rim = lax.dot_general(sides, wc, NT, preferred_element_type=F32)
        rnd = lambda y: y.astype(BF).astype(F32)
        mx[8:136] = rnd(x_ref[:, cols].astype(F32) + main)
        mx[0:8] = rnd(halo[0, 0, :, cols].astype(F32) + rim[0:8])
        mx[136:144] = rnd(halo[0, 1, :, cols].astype(F32) + rim[8:16])
        conv = jnp.zeros((136, 128), F32)
        for j in range(9):
            conv = conv + mx[pl.ds(j, 136)] * mk[j] * ck_ref[j : j + 1, cols]
        gate = jax.nn.sigmoid(conv)
        cg = ge[pl.ds(4, 136), cols] * gate * (1.0 + conv * (1.0 - gate))
        cs[...] = rnd(cg)
        silu = conv * gate
        lo_ref[:, cols] = (mx[8:136] + silu[4:132]).astype(BF)
        back = ge[8:136, cols]
        for j in range(9):
            back = back + cs[pl.ds(8 - j, 128)] * mk[8 - j, pl.ds(4, 128)] * ck_ref[j : j + 1, cols]
        ig = back.astype(BF)
        ig_ref[:, cols] = ig
        igs[c // 2, :, pl.ds(pl.multiple_of((c % 2) * 128, 128), 128)] = ig
        cg_own = cs[pl.ds(4, 128)]
        rows = []
        for j in range(9):
            rows.append(
                jnp.sum(cg_own * mx[pl.ds(4 + j, 128)] * mk[j, pl.ds(4, 128)], axis=0, keepdims=True)
            )
        rows.append(jnp.zeros((7, 128), F32))
        kg_ref[c] = jnp.concatenate(rows, axis=0)
        return 0

    lax.fori_loop(0, 8, chunk, 0)
    send_ig = [pair(igs.at[2 * z + 1 - core], igp.at[z], 1 + z) for z in range(2)]
    for c in send_ig:
        c.start()
    ag = jnp.zeros((T, H * E), F32)
    for z in range(4):
        ag = ag + jnp.dot(igs[z], w_ref[z * 256 : (z + 1) * 256, :], preferred_element_type=F32)
    dos[...] = ag.astype(BF).astype(F32).T.astype(BF).reshape(H, E, T)

    def do_copy(d):
        return plane_copy(me, d, dos, do_ref, dsnd, drcv)

    def start_do(d, _):
        do_copy(d).start()
        return 0

    lax.fori_loop(1, 8, start_do, 0)
    b = pltpu.make_async_copy(dos.at[plane], do_ref.at[plane], own.at[1])
    b.start()
    send_att.wait()
    for c in send_ig:
        c.wait()
    TN = (((0,), (0,)), ((), ()))
    for z in range(2):
        wg = lax.dot_general(igs[2 * z + core], am[...], TN, preferred_element_type=F32)
        wg = wg + lax.dot_general(igp[z], ap[...], TN, preferred_element_type=F32)
        wg_ref[z * 32 : (z + 1) * 32] = wg.reshape(32, 8, H * E).astype(BF)
    b.wait()

    def wait_do(d, _):
        do_copy(d).wait()
        return 0

    lax.fori_loop(1, 8, wait_do, 0)


def middle(lens, att, edge, x, g, halo, w, ck):
    sem = pltpu.SemaphoreType.DMA
    return pl.pallas_call(
        mid_kernel,
        name="middle",
        out_shape=(
            jax.ShapeDtypeStruct((T, 1024), BF),
            jax.ShapeDtypeStruct((T, 1024), BF),
            jax.ShapeDtypeStruct((H, E, T), BF),
            jax.ShapeDtypeStruct((64, 8, H * E), BF),
            jax.ShapeDtypeStruct((8, 16, 128), F32),
        ),
        in_specs=[pl.BlockSpec(memory_space=pltpu.SMEM)] + vm(7),
        out_specs=tuple(vm(5)),
        scratch_shapes=[
            pltpu.VMEM((H, E, T), BF),
            pltpu.VMEM((2, H, 8, 128), BF),
            pltpu.VMEM((T, H * E), BF),
            pltpu.VMEM((T, H * E), BF),
            pltpu.VMEM((4, T, 256), BF),
            pltpu.VMEM((2, T, 256), BF),
            pltpu.VMEM((H, E, T), BF),
            pltpu.VMEM((144, 128), F32),
            pltpu.VMEM((144, 1024), F32),
            pltpu.VMEM((136, 128), F32),
            pltpu.VMEM((9, 136, 128), F32),
            sem((8,)),
            sem((8,)),
            sem((2, 8)),
            sem((2, 8)),
            sem((8,)),
            sem((8,)),
            sem((3,)),
            sem((3,)),
            sem((2,)),
        ],
        compiler_params=params(1),
    )(lens, att, edge, x, g, halo, w, ck)


def spread_kernel(
    dq_ref, dkv_ref, wg_ref, kg_ref, dq_out, dk_out, dv_out, wo_ref, ko_ref,
    dq_in, dkv_in, wg_in, k1, k2, ksum, kall,
    ks, kr, qsnd, qrcv, wsnd, wrcv, s1, r1, s2, r2, s3, r3, own,
):
    dp, me = lax.axis_index("dp"), lax.axis_index("ctx")
    core, part, plane = dp % 2, me % 4, me // 4
    chip = (dp // 2) * 32 + me
    barrier = pltpu.get_barrier_semaphore()

    def chip_at(d):
        other = (chip + d) % 64
        return other, {"dp": (other // 32) * 2 + core, "ctx": other % 32}

    def column_at(d):
        other = (dp * 4 + part + d) % 16
        return {"dp": other // 4, "ctx": plane * 4 + other % 4}

    def hello(d, _):
        pl.semaphore_signal(barrier, inc=1, device_id=chip_at(d)[1], device_id_type=MESH)
        return 0

    def hello_column(d, _):
        where = {"dp": (d // 4) * 2 + 1 - core, "ctx": plane * 4 + d % 4}
        pl.semaphore_signal(barrier, inc=1, device_id=where, device_id_type=MESH)
        return 0

    lax.fori_loop(1, 64, hello, 0)
    lax.fori_loop(0, 8, hello_column, 0)
    pl.semaphore_wait(barrier, 71)

    def loop(n, f):
        def step(d, _):
            f(d)
            return 0

        lax.fori_loop(1, n, step, 0)

    def w_copy(d):
        other, where = chip_at(d)
        return pltpu.make_async_remote_copy(
            src_ref=wg_ref.at[other],
            dst_ref=wg_in.at[d],
            send_sem=wsnd.at[d],
            recv_sem=wrcv.at[d],
            device_id=where,
            device_id_type=MESH,
        )

    def column_copy(d):
        return pltpu.make_async_remote_copy(
            src_ref=ksum.at[0],
            dst_ref=k2.at[dp * 4 + part],
            send_sem=s2.at[d],
            recv_sem=r2.at[d],
            device_id=column_at(d),
            device_id_type=MESH,
        )

    def back_copy(d):
        return pltpu.make_async_remote_copy(
            src_ref=ksum.at[1],
            dst_ref=kall.at[plane],
            send_sem=s3.at[d],
            recv_sem=r3.at[d],
            device_id={"ctx": (me + 4 * d) % 32},
            device_id_type=MESH,
        )

    rows = lambda d: plane_copy(me, d, kg_ref, k1, s1, r1)
    grads = lambda d: group_copy(me, d, dkv_ref, dkv_in, ks, kr, False)
    queries = lambda d: plane_copy(me, d, dq_ref, dq_in, qsnd, qrcv)
    loop(8, lambda d: rows(d).start())
    loop(32, lambda d: grads(d).start())
    loop(8, lambda d: queries(d).start())
    loop(64, lambda d: w_copy(d).start())
    a = pltpu.make_async_copy(dkv_ref.at[me], dkv_in.at[me], own.at[0])
    b = pltpu.make_async_copy(dq_ref.at[plane], dq_in.at[plane], own.at[1])
    c = pltpu.make_async_copy(kg_ref.at[plane], k1.at[plane], own.at[2])
    for copy in (a, b, c):
        copy.start()
    for copy in (a, b, c):
        copy.wait()
    loop(8, lambda d: rows(d).wait())
    ksum[0] = jnp.sum(k1[...], axis=0)
    k2[dp * 4 + part] = ksum[0]
    loop(16, lambda d: column_copy(d).start())
    loop(16, lambda d: column_copy(d).wait())
    ksum[1] = jnp.sum(k2[...], axis=0)
    kall[plane] = ksum[1]
    loop(8, lambda d: back_copy(d).start())
    loop(8, lambda d: queries(d).wait())
    dq_out[...] = (dq_in[...].astype(F32).reshape(H * E, T) * SCALE).T.astype(BF)
    loop(32, lambda d: grads(d).wait())
    for h in range(H):
        total = dkv_in[4 * h].astype(F32)
        for p in range(1, 4):
            total = total + dkv_in[4 * h + p].astype(F32)
        cols = slice(h * E, (h + 1) * E)
        dk_out[:, cols] = total[:, :E].astype(BF)
        dv_out[:, cols] = total[:, E:].astype(BF)

    def add(d, total):
        w_copy(d).wait()
        return total + wg_in[d].astype(F32)

    wo_ref[...] = lax.fori_loop(1, 64, add, wg_ref[chip].astype(F32))
    loop(8, lambda d: back_copy(d).wait())
    ko_ref[...] = kall[...]


def spread_grads(dq, dkv, wg, kg):
    sem = pltpu.SemaphoreType.DMA
    return pl.pallas_call(
        spread_kernel,
        name="spread_grads",
        out_shape=(jax.ShapeDtypeStruct((T, H * E), BF),) * 3
        + (jax.ShapeDtypeStruct((8, H * E), F32), jax.ShapeDtypeStruct((8, 16, 128), F32)),
        in_specs=vm(4),
        out_specs=tuple(vm(5)),
        scratch_shapes=[
            pltpu.VMEM((H, E, T), BF),
            pltpu.VMEM((32, T, 2 * E), BF),
            pltpu.VMEM((64, 8, H * E), BF),
            pltpu.VMEM((8, 16, 128), F32),
            pltpu.VMEM((16, 16, 128), F32),
            pltpu.VMEM((2, 16, 128), F32),
            pltpu.VMEM((8, 16, 128), F32),
            sem((32,)),
            sem((32,)),
            sem((8,)),
            sem((8,)),
            sem((64,)),
            sem((64,)),
            sem((8,)),
            sem((8,)),
            sem((16,)),
            sem((16,)),
            sem((8,)),
            sem((8,)),
            sem((3,)),
        ],
        compiler_params=params(2),
    )(dq, dkv, wg, kg)


def record_bounds(len_ref):
    g = lax.axis_index("dp")
    s1 = len_ref[g, 0]
    s2 = s1 + len_ref[g, 1]
    s3 = s2 + len_ref[g, 2]
    return s1, s2, s3, s3 + len_ref[g, 3]


def record_of(pos, b):
    one = lambda s: jnp.where(pos >= s, 1, 0)
    return one(b[0]) + one(b[1]) + one(b[2])


def prepare_keys(b, kv_ref, kx, kt):
    def turn(j, _):
        kv = kv_ref[j]
        kt[j] = kv.astype(F32).T.astype(BF)
        kx[j, :, : 2 * E] = kv
        pos = j * KB + lax.broadcasted_iota(jnp.int32, (KB, 2 * E), 0)
        lane = lax.broadcasted_iota(jnp.int32, (KB, 2 * E), 1)
        kx[j, :, 2 * E :] = jnp.where(record_of(pos, b) == lane, 1.0, 0.0).astype(BF)
        return 0

    lax.fori_loop(0, NB, turn, 0)


def other_records(i, part, b):
    pos = (i * 4 + part) * T + lax.broadcasted_iota(jnp.int32, (2 * E, T), 1)
    row = lax.broadcasted_iota(jnp.int32, (2 * E, T), 0)
    return jnp.where((row < 4) & (record_of(pos, b) != row), NEG, 0.0).astype(BF)


def plan_blocks(part, b, first, last):
    count = jnp.int32(0)
    for i in range(H):
        f0 = (i * 4 + part) * T
        f1 = f0 + T - 1
        lo = jnp.where(f0 >= b[2], b[2], jnp.where(f0 >= b[1], b[1], jnp.where(f0 >= b[0], b[0], 0)))
        hi = jnp.where(f1 < b[0], b[0], jnp.where(f1 < b[1], b[1], jnp.where(f1 < b[2], b[2], b[3])))
        first[i] = lo // KB
        last[i] = (hi + KB - 1) // KB
        count = count + last[i] - first[i]
    first[H] = jnp.int32(0)
    last[H] = jnp.int32(1 << 20)
    return count


def run_items(count, first, last, item):
    def step(t, carry):
        i, kb = carry
        for u in range(U):
            item(t * U + u, i, kb)
            more = kb + 1 < last[i]
            after = jnp.minimum(i + 1, H)
            kb = jnp.where(more, kb + 1, first[after])
            i = jnp.where(more, i, after)
        return i, kb

    lax.fori_loop(0, (count + U - 1) // U, step, (jnp.int32(0), first[0]))


def fold(x, op):
    r = x.reshape(x.shape[0] // 8, 8, x.shape[1])
    return op(r, axis=0)


def forward_kernel(len_ref, kv_ref, q_ref, att_ref, edge_ref, lse_ref, kx, kt, qa, st, m8, m1, l8, acc, first, last):
    part = lax.axis_index("ctx") % 4
    b = record_bounds(len_ref)
    count = plan_blocks(part, b, first, last)
    prepare_keys(b, kv_ref, kx, kt)
    for i in range(H):
        qa[i, :E] = q_ref[i]
        qa[i, E : 2 * E] = jnp.zeros((E, T), BF)
        qa[i, 2 * E :] = other_records(i, part, b)
    qa[H] = jnp.zeros((4 * E, T), BF)
    m8[...] = jnp.full((H + 1, 8, T), NEG, F32)
    l8[...] = jnp.zeros((H + 1, 8, T), F32)
    acc[...] = jnp.zeros((H + 1, 2 * E, T), F32)

    def score(t, i, kb):
        s = jnp.dot(kx[kb], qa[i], preferred_element_type=F32)
        st[t] = s
        m8[i] = jnp.maximum(m8[i], fold(s, jnp.max))

    run_items(count, first, last, score)
    m1[...] = jnp.max(m8[...], axis=1, keepdims=True)

    def weigh(t, i, kb):
        p = jnp.exp(st[t] - m1[i])
        l8[i] += fold(p, jnp.sum)
        acc[i] += jnp.dot(kt[kb], p.astype(BF), preferred_element_type=F32)

    run_items(count, first, last, weigh)
    l1 = jnp.sum(l8[...], axis=1, keepdims=True)
    lse_ref[...] = m1[:H] + jnp.log(l1[:H])
    for i in range(H):
        out = acc[i, E:] / l1[i]
        att_ref[i] = out.astype(BF)
        wide = jnp.concatenate([out, jnp.zeros((E, T), F32)], axis=0).T
        edge_ref[i, 0] = wide[:8].astype(BF)
        edge_ref[i, 1] = wide[T - 8 :].astype(BF)


def forward(lens, kv, q):
    return pl.pallas_call(
        forward_kernel,
        name="attention_forward",
        out_shape=(
            jax.ShapeDtypeStruct((H, E, T), BF),
            jax.ShapeDtypeStruct((H, 2, 8, 2 * E), BF),
            jax.ShapeDtypeStruct((H, 1, T), F32),
        ),
        in_specs=[pl.BlockSpec(memory_space=pltpu.SMEM)] + vm(2),
        out_specs=tuple(vm(3)),
        scratch_shapes=[
            pltpu.VMEM((NB, KB, 4 * E), BF),
            pltpu.VMEM((NB, 2 * E, KB), BF),
            pltpu.VMEM((H + 1, 4 * E, T), BF),
            pltpu.VMEM((H * NB + U, KB, T), F32),
            pltpu.VMEM((H + 1, 8, T), F32),
            pltpu.VMEM((H + 1, 1, T), F32),
            pltpu.VMEM((H + 1, 8, T), F32),
            pltpu.VMEM((H + 1, 2 * E, T), F32),
            pltpu.SMEM((H + 1,), jnp.int32),
            pltpu.SMEM((H + 1,), jnp.int32),
        ],
    )(lens, kv.reshape(NB, KB, 2 * E), q)


def backward_kernel(
    len_ref, kv_ref, q_ref, do_ref, att_ref, lse_ref, dq_ref, dkv_ref,
    kx, kt, both, back, lse, rows, dq, acc, first, last,
):
    part = lax.axis_index("ctx") % 4
    b = record_bounds(len_ref)
    count = plan_blocks(part, b, first, last)
    prepare_keys(b, kv_ref, kx, kt)
    acc[...] = jnp.zeros((NB, KB, 2 * E), F32)
    dq[...] = jnp.zeros((H + 1, 2 * E, T), F32)
    zero = jnp.zeros((E, T), BF)
    for i in range(H):
        qt, dot = q_ref[i], do_ref[i]
        rows[i] = jnp.sum(dot.astype(F32) * att_ref[i].astype(F32), axis=0, keepdims=True)
        lse[i] = lse_ref[i]
        pair = jnp.concatenate(
            [jnp.concatenate([qt, zero], axis=0), jnp.concatenate([zero, dot], axis=0)], axis=1
        )
        both[i, : 2 * E] = pair
        both[i, 2 * E :, :T] = other_records(i, part, b)
        both[i, 2 * E :, T:] = jnp.zeros((2 * E, T), BF)
        back[i] = pair.astype(F32).T.astype(BF)
    rows[H] = jnp.zeros((1, T), F32)
    lse[H] = jnp.zeros((1, T), F32)
    both[H] = jnp.zeros((4 * E, 2 * T), BF)
    back[H] = jnp.zeros((2 * T, 2 * E), BF)

    def item(t, i, kb):
        sd = jnp.dot(kx[kb], both[i], preferred_element_type=F32)
        p = jnp.exp(sd[:, :T] - lse[i])
        ds = (p * (sd[:, T:] - rows[i])).astype(BF)
        dq[i] += jnp.dot(kt[kb], ds, preferred_element_type=F32)
        acc[kb] += jnp.dot(
            jnp.concatenate([ds, p.astype(BF)], axis=1), back[i], preferred_element_type=F32
        )

    run_items(count, first, last, item)
    for i in range(H):
        dq_ref[i] = dq[i, :E].astype(BF)

    def put(j, _):
        dkv_ref[j] = acc[j].astype(BF)
        return 0

    lax.fori_loop(0, NB, put, 0)


def backward(lens, kv, q, do, att, lse):
    dq, dkv = pl.pallas_call(
        backward_kernel,
        name="attention_backward",
        out_shape=(
            jax.ShapeDtypeStruct((H, E, T), BF),
            jax.ShapeDtypeStruct((NB, KB, 2 * E), BF),
        ),
        in_specs=[pl.BlockSpec(memory_space=pltpu.SMEM)] + vm(5),
        out_specs=tuple(vm(2)),
        scratch_shapes=[
            pltpu.VMEM((NB, KB, 4 * E), BF),
            pltpu.VMEM((NB, 2 * E, KB), BF),
            pltpu.VMEM((H + 1, 4 * E, 2 * T), BF),
            pltpu.VMEM((H + 1, 2 * T, 2 * E), BF),
            pltpu.VMEM((H + 1, 1, T), F32),
            pltpu.VMEM((H + 1, 1, T), F32),
            pltpu.VMEM((H + 1, 2 * E, T), F32),
            pltpu.VMEM((NB, KB, 2 * E), F32),
            pltpu.SMEM((H + 1,), jnp.int32),
            pltpu.SMEM((H + 1,), jnp.int32),
        ],
    )(lens, kv.reshape(NB, KB, 2 * E), q, do, att, lse)
    return dq, dkv.reshape(32, T, 2 * E)


def body(x, q, k, v, w, ck, lens, g):
    kv, qs, halo = gather_qkv(q, k, v, x, g)
    att, edge, lse = forward(lens, kv, qs)
    layer_output, input_grad, do, wg, kg = middle(lens, att, edge, x, g, halo, w, ck.astype(F32).T)
    dq, dkv = backward(lens, kv, qs, do, att, lse)
    dq, dk, dv, out_weight_grad, kg = spread_grads(dq, dkv, wg, kg)
    kernel_grad = jnp.transpose(kg[:, :9], (0, 2, 1)).reshape(1024, 9)
    return layer_output, input_grad, dq, dk, dv, out_weight_grad, kernel_grad


def solution(mesh):
    row = P(("dp", "ctx"), None)
    return jax.shard_map(
        body,
        mesh=mesh,
        in_specs=(row, row, row, row, P(), P(), P(), row),
        out_specs=(row, row, row, row, row, row, P()),
        check_vma=False,
    )
```

```python
import jax
import jax.numpy as jnp
from jax import lax
from jax.experimental import pallas as pl
from jax.experimental.pallas import tpu as pltpu
from jax.sharding import PartitionSpec as P

MESH = pl.DeviceIdType.MESH
BF = jnp.bfloat16
F32 = jnp.float32
H = 8
E = 64
C = 1024
SCALE = 0.125
NEG = -1e30
T = 128
KB = 256
NB = 16
NT = (((1,), (1,)), ((), ()))
TN = (((0,), (0,)), ((), ()))


def vm(n):
    return [pl.BlockSpec(memory_space=pltpu.VMEM)] * n


def loop(a, b, f):
    def step(d, _):
        f(d)
        return 0

    lax.fori_loop(a, b, step, 0)


def fold(x, op):
    return op(x.reshape(x.shape[0] // 8, 8, x.shape[1]), axis=0)


def remote(src, dst, snd, rcv, where):
    return pltpu.make_async_remote_copy(
        src_ref=src, dst_ref=dst, send_sem=snd, recv_sem=rcv, device_id=where, device_id_type=MESH
    )


def layer_kernel(
    len_ref, q_ref, k_ref, v_ref, x_ref, g_ref, w_ref, ck_ref,
    lo_ref, ig_ref, dq_ref, dk_ref, dv_ref, wo_ref, ko_ref,
    kvs, qs, kv_in, q_in, halo, kx, kt, both, back, m1, l8, acc, lse, rows, att, edge,
    at_in, eb, am, ap, igs, igp, dos, do_in, mx, ge, cs, mk, cf, wg, wg_in,
    kg, k1, k2, ksum, kall, dsp, dqa, dks, dkv_in, dqs, dq_in,
    kv_s, kv_r, q_s, q_r, h_s, h_r, a_s, a_r, e_s, e_r, d_s, d_r, p_s, p_r,
    w_s, w_r, k1_s, k1_r, k2_s, k2_r, k3_s, k3_r, g_s, g_r, y_s, y_r,
):
    dp, me = lax.axis_index("dp"), lax.axis_index("ctx")
    core, part, plane = dp % 2, me % 4, me // 4
    partner = {"dp": dp - core + (1 - core)}
    chip = (dp // 2) * 32 + me

    def plane_at(d):
        return {"ctx": (me + 4 * d) % 32}

    def chip_at(d):
        other = (chip + d) % 64
        return {"dp": (other // 32) * 2 + core, "ctx": other % 32}

    def column_at(d):
        other = (dp * 4 + part + d) % 16
        return {"dp": other // 4, "ctx": plane * 4 + other % 4}

    barrier = pltpu.get_barrier_semaphore()

    def signal(where):
        pl.semaphore_signal(barrier, inc=1, device_id=where, device_id_type=MESH)

    loop(1, 64, lambda d: signal(chip_at(d)))
    loop(0, 8, lambda d: signal({"dp": (d // 4) * 2 + 1 - core, "ctx": plane * 4 + d % 4}))

    for h in range(H):
        cols = slice(h * E, (h + 1) * E)
        kvs[h] = jnp.concatenate([k_ref[:, cols], v_ref[:, cols]], axis=1)
    qt = (q_ref[...].astype(F32) * SCALE).T.astype(BF)
    for h in range(H):
        qs[h] = qt[h * E : (h + 1) * E, :]
    kv_in[0] = kvs[plane]
    q_in[0] = qs[plane]

    s1 = len_ref[dp, 0]
    s2 = s1 + len_ref[dp, 1]
    s3 = s2 + len_ref[dp, 2]
    s4 = s3 + len_ref[dp, 3]

    def record_of(pos):
        one = lambda s: jnp.where(pos >= s, 1, 0)
        return one(s1) + one(s2) + one(s3)

    pl.semaphore_wait(barrier, 71)

    q_copy = lambda d: remote(qs.at[(plane + d) % 8], q_in.at[d], q_s.at[d], q_r.at[d], plane_at(d))
    kv_copy = lambda d: remote(
        kvs.at[((me + d) % 32) // 4], kv_in.at[d], kv_s.at[d], kv_r.at[d], {"ctx": (me + d) % 32}
    )

    def halo_copy(a, up):
        ref, s = (x_ref, g_ref)[a], 0 if up else 1
        return remote(
            ref.at[pl.ds(T - 8, 8)] if up else ref.at[pl.ds(0, 8)],
            halo.at[a, s],
            h_s.at[a, s],
            h_r.at[a, s],
            {"ctx": (me + (1 if up else 31)) % 32},
        )

    halos = [halo_copy(a, up) for a in range(2) for up in (True, False)]
    loop(1, 8, lambda d: q_copy(d).start())
    loop(1, 32, lambda d: kv_copy(d).start())
    for c in halos:
        c.start()

    m1[...] = jnp.full((H, 1, T), NEG, F32)
    l8[...] = jnp.zeros((H, 8, T), F32)
    acc[...] = jnp.zeros((H, E, T), F32)
    lane = lax.broadcasted_iota(jnp.int32, (1, 2 * E), 1)
    pick = lambda a, b, c, d, e: jnp.where(
        lane == 0, a, jnp.where(lane == 1, b, jnp.where(lane == 2, c, jnp.where(lane == 3, d, e)))
    )
    begin, end = pick(0, s1, s2, s3, s4), pick(s1, s2, s3, s4, s4)

    for i in range(H):
        pos = (i * 4 + part) * T + lax.broadcasted_iota(jnp.int32, (2 * E, T), 1)
        row = lax.broadcasted_iota(jnp.int32, (2 * E, T), 0)
        both[i, : 2 * E] = jnp.zeros((2 * E, 2 * T), BF)
        both[i, 2 * E :, :T] = jnp.where((row < 4) & (record_of(pos) != row), NEG, 0.0).astype(BF)
        both[i, 2 * E :, T:] = jnp.zeros((2 * E, T), BF)

    pos = me * T - 4 + lax.broadcasted_iota(jnp.int32, (136, 128), 0)
    label = lambda p: jnp.where((p >= 0) & (p < s4), record_of(p), -1)
    mine = label(pos)
    for j in range(9):
        mk[j] = jnp.where(label(pos + (j - 4)) == mine, 1.0, 0.0)
    cf[0:9] = ck_ref[...].astype(F32)
    ge[8:136] = g_ref[...].astype(F32)

    loop(1, 8, lambda d: q_copy(d).wait_recv())
    for i in range(H):
        both[i, :E, :T] = q_in[(plane - i + 8) % 8]

    def arrive(d):
        kv_copy(d).wait_recv()

    def forward_step(t):
        @pl.when(t > 0)
        def _():
            arrive(2 * t)

        arrive(2 * t + 1)
        for u in range(2):
            kv = kv_in[2 * t + u]
            kt[t, :, u * T : (u + 1) * T] = kv.astype(F32).T.astype(BF)
            at = slice(u * T, (u + 1) * T)
            kx[t, at, : 2 * E] = kv
            p = (me - 2 * t - u + 32) % 32 * T + lax.broadcasted_iota(jnp.int32, (T, 2 * E), 0)
            kx[t, at, 2 * E :] = jnp.where((p >= begin) & (p < end), 1.0, 0.0).astype(BF)
        for i in range(H):
            s = jnp.dot(kx[t], both[i, :, :T], preferred_element_type=F32)
            old = m1[i]
            new = jnp.maximum(old, jnp.max(fold(s, jnp.max), axis=0, keepdims=True))
            p = jnp.exp(s - new)
            scale = jnp.exp(old - new)
            m1[i] = new
            l8[i] = l8[i] * scale + fold(p, jnp.sum)
            acc[i] = acc[i] * scale + jnp.dot(kt[t, E:], p.astype(BF), preferred_element_type=F32)

    loop(0, NB, forward_step)
    for i in range(H):
        total = jnp.sum(l8[i], axis=0, keepdims=True)
        lse[i] = m1[i] + jnp.log(total)
        out = acc[i] / total
        att[i] = out.astype(BF)
        wide = jnp.concatenate([out, jnp.zeros((E, T), F32)], axis=0).T
        edge[i, 0] = wide[:8].astype(BF)
        edge[i, 1] = wide[T - 8 :].astype(BF)

    a_copy = lambda d: remote(att.at[(plane + d) % 8], at_in.at[plane], a_s.at[d], a_r.at[d], plane_at(d))

    def e_copy(i, late):
        other = (4 * i + part + (1 if late else 31)) % 32
        u = 1 if late else 0
        return remote(
            edge.at[i, u], eb.at[1 - u, plane], e_s.at[u, i], e_r.at[1 - u, plane], {"ctx": other}
        )

    e_arrival = lambda h, s: remote(edge.at[0, 0], eb.at[s, h], e_s.at[0, 0], e_r.at[s, h], partner)
    loop(1, 8, lambda d: a_copy(d).start())

    def edge_start(i):
        e_copy(i, True).start()
        e_copy(i, False).start()

    loop(0, 8, edge_start)
    at_in[plane] = att[plane]
    for c in halos:
        c.wait()
    ge[0:8] = halo[1, 0].astype(F32)
    ge[136:144] = halo[1, 1].astype(F32)
    loop(1, 8, lambda d: q_copy(d).wait_send())
    loop(1, 32, lambda d: kv_copy(d).wait_send())
    loop(1, 8, lambda d: a_copy(d).wait())

    def edge_wait(i):
        e_copy(i, True).wait_send()
        e_copy(i, False).wait_send()
        e_arrival(i, 0).wait_recv()
        e_arrival(i, 1).wait_recv()

    loop(0, 8, edge_wait)

    am[...] = at_in[...].astype(F32).reshape(H * E, T).T.astype(BF)
    pair = lambda src, dst, n: remote(src, dst, p_s.at[n], p_r.at[n], partner)
    send_att = pair(am, ap, 0)
    send_att.start()
    sides = jnp.concatenate(
        [jnp.concatenate([eb[s, h][:, :E] for h in range(H)], axis=1) for s in range(2)], axis=0
    )

    def chunk(c):
        cols = pl.ds(pl.multiple_of(c * 128, 128), 128)
        wc = w_ref[cols, :]
        main = lax.dot_general(am[...], wc, NT, preferred_element_type=F32)
        rim = lax.dot_general(sides, wc, NT, preferred_element_type=F32)
        rnd = lambda y: y.astype(BF).astype(F32)
        mx[8:136] = rnd(x_ref[:, cols].astype(F32) + main)
        mx[0:8] = rnd(halo[0, 0, :, cols].astype(F32) + rim[0:8])
        mx[136:144] = rnd(halo[0, 1, :, cols].astype(F32) + rim[8:16])
        conv = jnp.zeros((136, 128), F32)
        for j in range(9):
            conv = conv + mx[pl.ds(j, 136)] * mk[j] * cf[j : j + 1, cols]
        gate = jax.nn.sigmoid(conv)
        cg = ge[pl.ds(4, 136), cols] * gate * (1.0 + conv * (1.0 - gate))
        cs[...] = rnd(cg)
        silu = conv * gate
        lo_ref[:, cols] = (mx[8:136] + silu[4:132]).astype(BF)
        deep = ge[8:136, cols]
        for j in range(9):
            deep = deep + cs[pl.ds(8 - j, 128)] * mk[8 - j, pl.ds(4, 128)] * cf[j : j + 1, cols]
        ig = deep.astype(BF)
        ig_ref[:, cols] = ig
        igs[c // 2, :, pl.ds(pl.multiple_of((c % 2) * 128, 128), 128)] = ig
        cg_own = cs[pl.ds(4, 128)]
        sums = []
        for j in range(9):
            sums.append(
                jnp.sum(cg_own * mx[pl.ds(4 + j, 128)] * mk[j, pl.ds(4, 128)], axis=0, keepdims=True)
            )
        sums.append(jnp.zeros((7, 128), F32))
        kg[c] = jnp.concatenate(sums, axis=0)

    loop(0, 8, chunk)
    send_ig = [pair(igs.at[2 * z + 1 - core], igp.at[z], 1 + z) for z in range(2)]
    for c in send_ig:
        c.start()
    ag = jnp.zeros((T, H * E), F32)
    for z in range(4):
        ag = ag + jnp.dot(igs[z], w_ref[z * 256 : (z + 1) * 256, :], preferred_element_type=F32)
    dos[...] = ag.astype(BF).astype(F32).T.astype(BF).reshape(H, E, T)
    d_copy = lambda d: remote(dos.at[(plane + d) % 8], do_in.at[plane], d_s.at[d], d_r.at[d], plane_at(d))
    loop(1, 8, lambda d: d_copy(d).start())
    do_in[plane] = dos[plane]

    k1_copy = lambda d: remote(kg.at[(plane + d) % 8], k1.at[plane], k1_s.at[d], k1_r.at[d], plane_at(d))
    k2_copy = lambda d: remote(ksum.at[0], k2.at[dp * 4 + part], k2_s.at[d], k2_r.at[d], column_at(d))
    k3_copy = lambda d: remote(ksum.at[1], kall.at[plane], k3_s.at[d], k3_r.at[d], plane_at(d))
    loop(1, 8, lambda d: k1_copy(d).start())
    k1[plane] = kg[plane]

    w_copy = lambda d: remote(wg.at[(chip + d) % 64], wg_in.at[d], w_s.at[d], w_r.at[d], chip_at(d))
    send_att.wait()
    for c in send_ig:
        c.wait()
    for z in range(2):
        part_sum = lax.dot_general(igs[2 * z + core], am[...], TN, preferred_element_type=F32)
        part_sum = part_sum + lax.dot_general(igp[z], ap[...], TN, preferred_element_type=F32)
        wg[z * 32 : (z + 1) * 32] = part_sum.reshape(32, 8, H * E).astype(BF)
    loop(1, 64, lambda d: w_copy(d).start())

    dqa[...] = jnp.zeros((H, E, T), F32)
    zero = jnp.zeros((E, T), BF)
    loop(1, 8, lambda d: d_copy(d).wait())
    for i in range(H):
        dot = do_in[i]
        rows[i] = jnp.sum(dot.astype(F32) * att[i].astype(F32), axis=0, keepdims=True)
        both[i, E : 2 * E, T:] = dot
        pair_t = jnp.concatenate(
            [
                jnp.concatenate([both[i, :E, :T], zero], axis=0),
                jnp.concatenate([zero, dot], axis=0),
            ],
            axis=1,
        )
        back[i * 2 * T : (i + 1) * 2 * T] = pair_t.astype(F32).T.astype(BF)
    loop(1, 8, lambda d: k1_copy(d).wait())
    ksum[0] = jnp.sum(k1[...], axis=0)
    k2[dp * 4 + part] = ksum[0]
    loop(1, 16, lambda d: k2_copy(d).start())

    g_copy = lambda d: remote(
        dks.at[d], dkv_in.at[d], g_s.at[d], g_r.at[d], {"ctx": (me - d + 32) % 32}
    )

    def backward_step(t):
        for i in range(H):
            sd = jnp.dot(kx[t], both[i], preferred_element_type=F32)
            p = jnp.exp(sd[:, :T] - lse[i])
            ds = (p * (sd[:, T:] - rows[i])).astype(BF)
            dsp[:, i * 2 * T : i * 2 * T + T] = ds
            dsp[:, i * 2 * T + T : (i + 1) * 2 * T] = p.astype(BF)
            dqa[i] += jnp.dot(kt[t, :E], ds, preferred_element_type=F32)
        dkv = jnp.dot(dsp[...], back[...], preferred_element_type=F32).astype(BF)
        dks[2 * t] = dkv[:T]
        dks[2 * t + 1] = dkv[T:]

        @pl.when(t > 0)
        def _():
            g_copy(2 * t).start()

        g_copy(2 * t + 1).start()

    loop(0, NB // 2, backward_step)
    loop(1, 16, lambda d: k2_copy(d).wait())
    ksum[1] = jnp.sum(k2[...], axis=0)
    kall[plane] = ksum[1]
    loop(1, 8, lambda d: k3_copy(d).start())
    loop(NB // 2, NB, backward_step)
    for i in range(H):
        dqs[i] = dqa[i].astype(BF)
    y_copy = lambda d: remote(dqs.at[(plane + d) % 8], dq_in.at[plane], y_s.at[d], y_r.at[d], plane_at(d))
    loop(1, 8, lambda d: y_copy(d).start())
    dq_in[plane] = dqs[plane]
    dkv_in[0] = dks[0]

    loop(1, 8, lambda d: k3_copy(d).wait())
    ko_ref[...] = kall[...]

    def add(d, total):
        w_copy(d).wait()
        return total + wg_in[d].astype(F32)

    wo_ref[...] = lax.fori_loop(1, 64, add, wg[chip].astype(F32))
    loop(1, 8, lambda d: y_copy(d).wait())
    dq_ref[...] = (dq_in[...].astype(F32).reshape(H * E, T) * SCALE).T.astype(BF)
    loop(1, 32, lambda d: g_copy(d).wait())
    for h in range(H):
        parts = [dkv_in[(4 * h + p - me + 32) % 32].astype(F32) for p in range(4)]
        total = (parts[0] + parts[1]) + (parts[2] + parts[3])
        cols = slice(h * E, (h + 1) * E)
        dk_ref[:, cols] = total[:, :E].astype(BF)
        dv_ref[:, cols] = total[:, E:].astype(BF)


def layer(lens, q, k, v, x, g, w, ck):
    dma = pltpu.SemaphoreType.DMA
    V = pltpu.VMEM
    return pl.pallas_call(
        layer_kernel,
        name="layer",
        out_shape=(
            jax.ShapeDtypeStruct((T, C), BF),
            jax.ShapeDtypeStruct((T, C), BF),
            jax.ShapeDtypeStruct((T, H * E), BF),
            jax.ShapeDtypeStruct((T, H * E), BF),
            jax.ShapeDtypeStruct((T, H * E), BF),
            jax.ShapeDtypeStruct((8, H * E), F32),
            jax.ShapeDtypeStruct((8, 16, 128), F32),
        ),
        in_specs=[pl.BlockSpec(memory_space=pltpu.SMEM)] + vm(7),
        out_specs=tuple(vm(7)),
        scratch_shapes=[
            V((H, T, 2 * E), BF),
            V((H, E, T), BF),
            V((32, T, 2 * E), BF),
            V((H, E, T), BF),
            V((2, 2, 8, C), BF),
            V((NB, KB, 4 * E), BF),
            V((NB, 2 * E, KB), BF),
            V((H, 4 * E, 2 * T), BF),
            V((H * 2 * T, 2 * E), BF),
            V((H, 1, T), F32),
            V((H, 8, T), F32),
            V((H, E, T), F32),
            V((H, 1, T), F32),
            V((H, 1, T), F32),
            V((H, E, T), BF),
            V((H, 2, 8, 128), BF),
            V((H, E, T), BF),
            V((2, H, 8, 128), BF),
            V((T, H * E), BF),
            V((T, H * E), BF),
            V((4, T, 256), BF),
            V((2, T, 256), BF),
            V((H, E, T), BF),
            V((H, E, T), BF),
            V((144, 128), F32),
            V((144, C), F32),
            V((136, 128), F32),
            V((9, 136, 128), F32),
            V((16, C), F32),
            V((64, 8, H * E), BF),
            V((64, 8, H * E), BF),
            V((8, 16, 128), F32),
            V((8, 16, 128), F32),
            V((16, 16, 128), F32),
            V((2, 16, 128), F32),
            V((8, 16, 128), F32),
            V((KB, H * 2 * T), BF),
            V((H, E, T), F32),
            V((32, T, 2 * E), BF),
            V((32, T, 2 * E), BF),
            V((H, E, T), BF),
            V((H, E, T), BF),
        ]
        + [dma((n,)) for n in (32, 32, 8, 8)]
        + [dma((2, 2))] * 2
        + [dma((8,))] * 2
        + [dma((2, 8))] * 2
        + [dma((n,)) for n in (8, 8, 3, 3, 64, 64, 8, 8, 16, 16, 8, 8, 32, 32, 8, 8)],
        compiler_params=pltpu.CompilerParams(collective_id=0, has_side_effects=True),
    )(lens, q, k, v, x, g, w, ck)


def hand_on_kernel(a, b, c, d, e, f, k, ao, bo, co, do, eo, fo, ko):
    for src, dst in ((a, ao), (b, bo), (c, co), (d, do), (e, eo), (f, fo)):
        dst[...] = src[...]
    for h in range(8):
        ko[:, h * 128 : (h + 1) * 128] = k[h, :9]


def hand_on(*xs):
    shapes = [jax.ShapeDtypeStruct(x.shape, x.dtype) for x in xs[:6]]
    return pl.pallas_call(
        hand_on_kernel,
        name="hand_on",
        out_shape=tuple(shapes) + (jax.ShapeDtypeStruct((9, C), F32),),
        in_specs=vm(7),
        out_specs=tuple(vm(7)),
    )(*xs)


def body(x, q, k, v, w, ck, lens, g):
    outs = hand_on(*layer(lens, q, k, v, x, g, w, ck.T))
    return outs[:6] + (outs[6].T,)


def solution(mesh):
    row = P(("dp", "ctx"), None)
    return jax.shard_map(
        body,
        mesh=mesh,
        in_specs=(row, row, row, row, P(), P(), P(), row),
        out_specs=(row, row, row, row, row, row, P()),
        check_vma=False,
    )
```

```python
import jax
import jax.numpy as jnp
from jax import lax
from jax.experimental import pallas as pl
from jax.experimental.pallas import tpu as pltpu
from jax.sharding import PartitionSpec as P

MESH = pl.DeviceIdType.MESH
BF = jnp.bfloat16
F32 = jnp.float32
H = 8
E = 64
C = 1024
SCALE = 0.125
NEG = -1e30
T = 128
KB = 256
NB = 16
NT = (((1,), (1,)), ((), ()))
TN = (((0,), (0,)), ((), ()))


def vm(n):
    return [pl.BlockSpec(memory_space=pltpu.VMEM)] * n


def loop(a, b, f):
    def step(d, _):
        f(d)
        return 0

    lax.fori_loop(a, b, step, 0)


def fold(x, op):
    return op(x.reshape(x.shape[0] // 8, 8, x.shape[1]), axis=0)


def remote(src, dst, snd, rcv, where):
    return pltpu.make_async_remote_copy(
        src_ref=src, dst_ref=dst, send_sem=snd, recv_sem=rcv, device_id=where, device_id_type=MESH
    )


def layer_kernel(
    len_ref, q_ref, k_ref, v_ref, x_ref, g_ref, w_ref, ck_ref,
    lo_ref, ig_ref, dq_ref, dk_ref, dv_ref, wo_ref, ko_ref,
    kvs, qs, kv_in, q_in, halo, kx, kt, both, back, m1, l8, acc, lse, rows, att, edge,
    at_in, eb, am, ap, igs, igp, dos, do_in, mx, ge, cs, mk, cf, wg, wg_in,
    kg, k1, k2, ksum, kall, st_a, st_b, sd_a, sd_b, pt_a, pt_b, ds_a, ds_b, top, dqa, dks, dkv_in, dqs, dq_in,
    kv_s, kv_r, q_s, q_r, h_s, h_r, a_s, a_r, e_s, e_r, d_s, d_r, p_s, p_r,
    w_s, w_r, k1_s, k1_r, k2_s, k2_r, k3_s, k3_r, g_s, g_r, y_s, y_r,
):
    dp, me = lax.axis_index("dp"), lax.axis_index("ctx")
    core, part, plane = dp % 2, me % 4, me // 4
    partner = {"dp": dp - core + (1 - core)}
    chip = (dp // 2) * 32 + me

    def plane_at(d):
        return {"ctx": (me + 4 * d) % 32}

    def chip_at(d):
        other = (chip + d) % 64
        return {"dp": (other // 32) * 2 + core, "ctx": other % 32}

    def column_at(d):
        other = (dp * 4 + part + d) % 16
        return {"dp": other // 4, "ctx": plane * 4 + other % 4}

    barrier = pltpu.get_barrier_semaphore()

    def signal(where):
        pl.semaphore_signal(barrier, inc=1, device_id=where, device_id_type=MESH)

    loop(1, 64, lambda d: signal(chip_at(d)))
    loop(0, 8, lambda d: signal({"dp": (d // 4) * 2 + 1 - core, "ctx": plane * 4 + d % 4}))

    for h in range(H):
        cols = slice(h * E, (h + 1) * E)
        kvs[h] = jnp.concatenate([k_ref[:, cols], v_ref[:, cols]], axis=1)
    qt = (q_ref[...].astype(F32) * SCALE).T.astype(BF)
    for h in range(H):
        qs[h] = qt[h * E : (h + 1) * E, :]
    kv_in[0] = kvs[plane]
    q_in[0] = qs[plane]

    s1 = len_ref[dp, 0]
    s2 = s1 + len_ref[dp, 1]
    s3 = s2 + len_ref[dp, 2]
    s4 = s3 + len_ref[dp, 3]

    def record_of(pos):
        one = lambda s: jnp.where(pos >= s, 1, 0)
        return one(s1) + one(s2) + one(s3)

    pl.semaphore_wait(barrier, 71)

    q_copy = lambda d: remote(qs.at[(plane + d) % 8], q_in.at[d], q_s.at[d], q_r.at[d], plane_at(d))
    kv_copy = lambda d: remote(
        kvs.at[((me + d) % 32) // 4], kv_in.at[d], kv_s.at[d], kv_r.at[d], {"ctx": (me + d) % 32}
    )

    def halo_copy(a, up):
        ref, s = (x_ref, g_ref)[a], 0 if up else 1
        return remote(
            ref.at[pl.ds(T - 8, 8)] if up else ref.at[pl.ds(0, 8)],
            halo.at[a, s],
            h_s.at[a, s],
            h_r.at[a, s],
            {"ctx": (me + (1 if up else 31)) % 32},
        )

    halos = [halo_copy(a, up) for a in range(2) for up in (True, False)]
    loop(1, 8, lambda d: q_copy(d).start())
    loop(1, 32, lambda d: kv_copy(d).start())
    for c in halos:
        c.start()

    m1[...] = jnp.full((1, H * T), NEG, F32)
    l8[...] = jnp.zeros((8, H * T), F32)
    acc[...] = jnp.zeros((E, H * T), F32)
    lane = lax.broadcasted_iota(jnp.int32, (1, 2 * E), 1)
    pick = lambda a, b, c, d, e: jnp.where(
        lane == 0, a, jnp.where(lane == 1, b, jnp.where(lane == 2, c, jnp.where(lane == 3, d, e)))
    )
    begin, end = pick(0, s1, s2, s3, s4), pick(s1, s2, s3, s4, s4)

    for i in range(H):
        pos = (i * 4 + part) * T + lax.broadcasted_iota(jnp.int32, (2 * E, T), 1)
        row = lax.broadcasted_iota(jnp.int32, (2 * E, T), 0)
        both[i, : 2 * E] = jnp.zeros((2 * E, 2 * T), BF)
        both[i, 2 * E :, :T] = jnp.where((row < 4) & (record_of(pos) != row), NEG, 0.0).astype(BF)
        both[i, 2 * E :, T:] = jnp.zeros((2 * E, T), BF)

    pos = me * T - 4 + lax.broadcasted_iota(jnp.int32, (136, 128), 0)
    label = lambda p: jnp.where((p >= 0) & (p < s4), record_of(p), -1)
    mine = label(pos)
    for j in range(9):
        mk[j] = jnp.where(label(pos + (j - 4)) == mine, 1.0, 0.0)
    cf[0:9] = ck_ref[...].astype(F32)
    ge[8:136] = g_ref[...].astype(F32)

    loop(1, 8, lambda d: q_copy(d).wait_recv())
    for i in range(H):
        both[i, :E, :T] = q_in[(plane - i + 8) % 8]

    def build(t):
        for u in range(2):
            kv = kv_in[2 * t + u]
            at = slice(u * T, (u + 1) * T)
            kt[t, :, at] = kv.astype(F32).T.astype(BF)
            kx[t, at, : 2 * E] = kv
            p = (me - 2 * t - u + 32) % 32 * T + lax.broadcasted_iota(jnp.int32, (T, 2 * E), 0)
            kx[t, at, 2 * E :] = jnp.where((p >= begin) & (p < end), 1.0, 0.0).astype(BF)

    def score(t, st):
        for i in range(H):
            s = jnp.dot(kx[t], both[i, :, :T], preferred_element_type=F32)
            st[i] = s
            top[:, i * T : (i + 1) * T] = fold(s, jnp.max)

    def weigh(t, st, pt):
        old = m1[...]
        new = jnp.maximum(old, jnp.max(top[...], axis=0, keepdims=True))
        scale = jnp.exp(old - new)
        m1[...] = new
        return new, scale

    def spread(t, st, pt, new, scale):
        for i in range(H):
            cols = slice(i * T, (i + 1) * T)
            p = jnp.exp(st[i] - new[:, cols])
            l8[:, cols] = l8[:, cols] * scale[:, cols] + fold(p, jnp.sum)
            pt[:, cols] = p.astype(BF)
        for i in range(0, H, 2):
            cols = slice(i * T, (i + 2) * T)
            acc[:, cols] = acc[:, cols] * scale[:, cols] + jnp.dot(
                kt[t, E:], pt[:, cols], preferred_element_type=F32
            )

    kv_copy(1).wait_recv()
    build(0)
    score(0, st_a)

    def forward_step(u):
        t = 2 * u
        kv_copy(2 * t + 2).wait_recv()
        kv_copy(2 * t + 3).wait_recv()

        @pl.when(u < NB // 2 - 1)
        def _():
            kv_copy(2 * t + 4).wait_recv()
            kv_copy(2 * t + 5).wait_recv()

        later = jnp.minimum(t + 2, NB - 1)
        build(t + 1)
        build(later)
        w = weigh(t, st_a, pt_a)
        score(t + 1, st_b)
        spread(t, st_a, pt_a, *w)
        w = weigh(t + 1, st_b, pt_b)
        score(later, st_a)
        spread(t + 1, st_b, pt_b, *w)

    loop(0, NB // 2, forward_step)
    for i in range(H):
        cols = slice(i * T, (i + 1) * T)
        total = jnp.sum(l8[:, cols], axis=0, keepdims=True)
        lse[:, cols] = m1[:, cols] + jnp.log(total)
        out = acc[:, cols] / total
        att[i] = out.astype(BF)
        wide = jnp.concatenate([out, jnp.zeros((E, T), F32)], axis=0).T
        edge[i, 0] = wide[:8].astype(BF)
        edge[i, 1] = wide[T - 8 :].astype(BF)

    a_copy = lambda d: remote(att.at[(plane + d) % 8], at_in.at[plane], a_s.at[d], a_r.at[d], plane_at(d))

    def e_copy(i, late):
        other = (4 * i + part + (1 if late else 31)) % 32
        u = 1 if late else 0
        return remote(
            edge.at[i, u], eb.at[1 - u, plane], e_s.at[u, i], e_r.at[1 - u, plane], {"ctx": other}
        )

    e_arrival = lambda h, s: remote(edge.at[0, 0], eb.at[s, h], e_s.at[0, 0], e_r.at[s, h], partner)
    loop(1, 8, lambda d: a_copy(d).start())

    def edge_start(i):
        e_copy(i, True).start()
        e_copy(i, False).start()

    loop(0, 8, edge_start)
    at_in[plane] = att[plane]
    for c in halos:
        c.wait()
    ge[0:8] = halo[1, 0].astype(F32)
    ge[136:144] = halo[1, 1].astype(F32)
    loop(1, 8, lambda d: q_copy(d).wait_send())
    loop(1, 32, lambda d: kv_copy(d).wait_send())
    loop(1, 8, lambda d: a_copy(d).wait())

    def edge_wait(i):
        e_copy(i, True).wait_send()
        e_copy(i, False).wait_send()
        e_arrival(i, 0).wait_recv()
        e_arrival(i, 1).wait_recv()

    loop(0, 8, edge_wait)

    am[...] = at_in[...].astype(F32).reshape(H * E, T).T.astype(BF)
    pair = lambda src, dst, n: remote(src, dst, p_s.at[n], p_r.at[n], partner)
    send_att = pair(am, ap, 0)
    send_att.start()
    sides = jnp.concatenate(
        [jnp.concatenate([eb[s, h][:, :E] for h in range(H)], axis=1) for s in range(2)], axis=0
    )

    def chunk(c):
        cols = pl.ds(pl.multiple_of(c * 128, 128), 128)
        wc = w_ref[cols, :]
        main = lax.dot_general(am[...], wc, NT, preferred_element_type=F32)
        rim = lax.dot_general(sides, wc, NT, preferred_element_type=F32)
        rnd = lambda y: y.astype(BF).astype(F32)
        mx[8:136] = rnd(x_ref[:, cols].astype(F32) + main)
        mx[0:8] = rnd(halo[0, 0, :, cols].astype(F32) + rim[0:8])
        mx[136:144] = rnd(halo[0, 1, :, cols].astype(F32) + rim[8:16])
        conv = jnp.zeros((136, 128), F32)
        for j in range(9):
            conv = conv + mx[pl.ds(j, 136)] * mk[j] * cf[j : j + 1, cols]
        gate = jax.nn.sigmoid(conv)
        cg = ge[pl.ds(4, 136), cols] * gate * (1.0 + conv * (1.0 - gate))
        cs[...] = rnd(cg)
        silu = conv * gate
        lo_ref[:, cols] = (mx[8:136] + silu[4:132]).astype(BF)
        deep = ge[8:136, cols]
        for j in range(9):
            deep = deep + cs[pl.ds(8 - j, 128)] * mk[8 - j, pl.ds(4, 128)] * cf[j : j + 1, cols]
        ig = deep.astype(BF)
        ig_ref[:, cols] = ig
        igs[c // 2, :, pl.ds(pl.multiple_of((c % 2) * 128, 128), 128)] = ig
        cg_own = cs[pl.ds(4, 128)]
        sums = []
        for j in range(9):
            sums.append(
                jnp.sum(cg_own * mx[pl.ds(4 + j, 128)] * mk[j, pl.ds(4, 128)], axis=0, keepdims=True)
            )
        sums.append(jnp.zeros((7, 128), F32))
        kg[c] = jnp.concatenate(sums, axis=0)

    loop(0, 8, chunk)
    send_ig = [pair(igs.at[2 * z + 1 - core], igp.at[z], 1 + z) for z in range(2)]
    for c in send_ig:
        c.start()
    ag = jnp.zeros((T, H * E), F32)
    for z in range(4):
        ag = ag + jnp.dot(igs[z], w_ref[z * 256 : (z + 1) * 256, :], preferred_element_type=F32)
    dos[...] = ag.astype(BF).astype(F32).T.astype(BF).reshape(H, E, T)
    d_copy = lambda d: remote(dos.at[(plane + d) % 8], do_in.at[plane], d_s.at[d], d_r.at[d], plane_at(d))
    loop(1, 8, lambda d: d_copy(d).start())
    do_in[plane] = dos[plane]

    k1_copy = lambda d: remote(kg.at[(plane + d) % 8], k1.at[plane], k1_s.at[d], k1_r.at[d], plane_at(d))
    k2_copy = lambda d: remote(ksum.at[0], k2.at[dp * 4 + part], k2_s.at[d], k2_r.at[d], column_at(d))
    k3_copy = lambda d: remote(ksum.at[1], kall.at[plane], k3_s.at[d], k3_r.at[d], plane_at(d))
    loop(1, 8, lambda d: k1_copy(d).start())
    k1[plane] = kg[plane]

    w_copy = lambda d: remote(wg.at[(chip + d) % 64], wg_in.at[d], w_s.at[d], w_r.at[d], chip_at(d))
    send_att.wait()
    for c in send_ig:
        c.wait()
    for z in range(2):
        part_sum = lax.dot_general(igs[2 * z + core], am[...], TN, preferred_element_type=F32)
        part_sum = part_sum + lax.dot_general(igp[z], ap[...], TN, preferred_element_type=F32)
        wg[z * 32 : (z + 1) * 32] = part_sum.reshape(32, 8, H * E).astype(BF)
    loop(1, 64, lambda d: w_copy(d).start())

    dqa[...] = jnp.zeros((E, H * T), F32)
    zero = jnp.zeros((E, T), BF)
    loop(1, 8, lambda d: d_copy(d).wait())
    for i in range(H):
        dot = do_in[i]
        rows[i] = jnp.sum(dot.astype(F32) * att[i].astype(F32), axis=0, keepdims=True)
        both[i, E : 2 * E, T:] = dot
        pair_t = jnp.concatenate(
            [
                jnp.concatenate([both[i, :E, :T], zero], axis=0),
                jnp.concatenate([zero, dot], axis=0),
            ],
            axis=1,
        )
        turned = pair_t.astype(F32).T.astype(BF)
        back[i * T : (i + 1) * T] = turned[:T]
        back[(H + i) * T : (H + i + 1) * T] = turned[T:]
    loop(1, 8, lambda d: k1_copy(d).wait())
    ksum[0] = jnp.sum(k1[...], axis=0)
    k2[dp * 4 + part] = ksum[0]
    loop(1, 16, lambda d: k2_copy(d).start())

    g_copy = lambda d: remote(
        dks.at[d], dkv_in.at[d], g_s.at[d], g_r.at[d], {"ctx": (me - d + 32) % 32}
    )

    def product(t, sd):
        for i in range(H):
            sd[i] = jnp.dot(kx[t], both[i], preferred_element_type=F32)

    def backward_part(t, sd, pt, dst):
        for i in range(H):
            cols = slice(i * T, (i + 1) * T)
            p = jnp.exp(sd[i, :, :T] - lse[:, cols])
            ds = (p * (sd[i, :, T:] - rows[i])).astype(BF)
            dst[:, cols] = ds
            pt[:, cols] = p.astype(BF)
        for i in range(0, H, 2):
            cols = slice(i * T, (i + 2) * T)
            dqa[:, cols] += jnp.dot(kt[t, :E], dst[:, cols], preferred_element_type=F32)
        dkv = jnp.dot(dst[...], back[: H * T], preferred_element_type=F32)
        dkv = dkv + jnp.dot(pt[...], back[H * T :], preferred_element_type=F32)
        dkv = dkv.astype(BF)
        dks[2 * t] = dkv[:T]
        dks[2 * t + 1] = dkv[T:]

    def backward_step(u):
        t = 2 * u
        product(t + 1, sd_b)
        backward_part(t, sd_a, pt_a, ds_a)
        product(jnp.minimum(t + 2, NB - 1), sd_a)
        backward_part(t + 1, sd_b, pt_b, ds_b)

        @pl.when(u > 0)
        def _():
            g_copy(2 * t).start()

        g_copy(2 * t + 1).start()
        g_copy(2 * t + 2).start()
        g_copy(2 * t + 3).start()

    product(0, sd_a)
    loop(0, NB // 4, backward_step)
    loop(1, 16, lambda d: k2_copy(d).wait())
    ksum[1] = jnp.sum(k2[...], axis=0)
    kall[plane] = ksum[1]
    loop(1, 8, lambda d: k3_copy(d).start())
    loop(NB // 4, NB // 2, backward_step)
    for i in range(H):
        dqs[i] = dqa[:, i * T : (i + 1) * T].astype(BF)
    y_copy = lambda d: remote(dqs.at[(plane + d) % 8], dq_in.at[plane], y_s.at[d], y_r.at[d], plane_at(d))
    loop(1, 8, lambda d: y_copy(d).start())
    dq_in[plane] = dqs[plane]
    dkv_in[0] = dks[0]

    loop(1, 8, lambda d: k3_copy(d).wait())
    ko_ref[...] = kall[...]

    def add(d, total):
        w_copy(d).wait()
        return total + wg_in[d].astype(F32)

    wo_ref[...] = lax.fori_loop(1, 64, add, wg[chip].astype(F32))
    loop(1, 8, lambda d: y_copy(d).wait())
    dq_ref[...] = (dq_in[...].astype(F32).reshape(H * E, T) * SCALE).T.astype(BF)
    loop(1, 32, lambda d: g_copy(d).wait())
    for h in range(H):
        parts = [dkv_in[(4 * h + p - me + 32) % 32].astype(F32) for p in range(4)]
        total = (parts[0] + parts[1]) + (parts[2] + parts[3])
        cols = slice(h * E, (h + 1) * E)
        dk_ref[:, cols] = total[:, :E].astype(BF)
        dv_ref[:, cols] = total[:, E:].astype(BF)


def layer(lens, q, k, v, x, g, w, ck):
    dma = pltpu.SemaphoreType.DMA
    V = pltpu.VMEM
    return pl.pallas_call(
        layer_kernel,
        name="layer",
        out_shape=(
            jax.ShapeDtypeStruct((T, C), BF),
            jax.ShapeDtypeStruct((T, C), BF),
            jax.ShapeDtypeStruct((T, H * E), BF),
            jax.ShapeDtypeStruct((T, H * E), BF),
            jax.ShapeDtypeStruct((T, H * E), BF),
            jax.ShapeDtypeStruct((8, H * E), F32),
            jax.ShapeDtypeStruct((8, 16, 128), F32),
        ),
        in_specs=[pl.BlockSpec(memory_space=pltpu.SMEM)] + vm(7),
        out_specs=tuple(vm(7)),
        scratch_shapes=[
            V((H, T, 2 * E), BF),
            V((H, E, T), BF),
            V((32, T, 2 * E), BF),
            V((H, E, T), BF),
            V((2, 2, 8, C), BF),
            V((NB, KB, 4 * E), BF),
            V((NB, 2 * E, KB), BF),
            V((H, 4 * E, 2 * T), BF),
            V((H * 2 * T, 2 * E), BF),
            V((1, H * T), F32),
            V((8, H * T), F32),
            V((E, H * T), F32),
            V((1, H * T), F32),
            V((H, 1, T), F32),
            V((H, E, T), BF),
            V((H, 2, 8, 128), BF),
            V((H, E, T), BF),
            V((2, H, 8, 128), BF),
            V((T, H * E), BF),
            V((T, H * E), BF),
            V((4, T, 256), BF),
            V((2, T, 256), BF),
            V((H, E, T), BF),
            V((H, E, T), BF),
            V((144, 128), F32),
            V((144, C), F32),
            V((136, 128), F32),
            V((9, 136, 128), F32),
            V((16, C), F32),
            V((64, 8, H * E), BF),
            V((64, 8, H * E), BF),
            V((8, 16, 128), F32),
            V((8, 16, 128), F32),
            V((16, 16, 128), F32),
            V((2, 16, 128), F32),
            V((8, 16, 128), F32),
            V((H, KB, T), F32),
            V((H, KB, T), F32),
            V((H, KB, 2 * T), F32),
            V((H, KB, 2 * T), F32),
            V((KB, H * T), BF),
            V((KB, H * T), BF),
            V((KB, H * T), BF),
            V((KB, H * T), BF),
            V((8, H * T), F32),
            V((E, H * T), F32),
            V((32, T, 2 * E), BF),
            V((32, T, 2 * E), BF),
            V((H, E, T), BF),
            V((H, E, T), BF),
        ]
        + [dma((n,)) for n in (32, 32, 8, 8)]
        + [dma((2, 2))] * 2
        + [dma((8,))] * 2
        + [dma((2, 8))] * 2
        + [dma((n,)) for n in (8, 8, 3, 3, 64, 64, 8, 8, 16, 16, 8, 8, 32, 32, 8, 8)],
        compiler_params=pltpu.CompilerParams(collective_id=0, has_side_effects=True),
    )(lens, q, k, v, x, g, w, ck)


def hand_on_kernel(a, b, c, d, e, f, k, ao, bo, co, do, eo, fo, ko):
    for src, dst in ((a, ao), (b, bo), (c, co), (d, do), (e, eo), (f, fo)):
        dst[...] = src[...]
    for h in range(8):
        ko[:, h * 128 : (h + 1) * 128] = k[h, :9]


def hand_on(*xs):
    shapes = [jax.ShapeDtypeStruct(x.shape, x.dtype) for x in xs[:6]]
    return pl.pallas_call(
        hand_on_kernel,
        name="hand_on",
        out_shape=tuple(shapes) + (jax.ShapeDtypeStruct((9, C), F32),),
        in_specs=vm(7),
        out_specs=tuple(vm(7)),
    )(*xs)


def body(x, q, k, v, w, ck, lens, g):
    outs = hand_on(*layer(lens, q, k, v, x, g, w, ck.T))
    return outs[:6] + (outs[6].T,)


def solution(mesh):
    row = P(("dp", "ctx"), None)
    return jax.shard_map(
        body,
        mesh=mesh,
        in_specs=(row, row, row, row, P(), P(), P(), row),
        out_specs=(row, row, row, row, row, row, P()),
        check_vma=False,
    )
```

```python
import jax
import jax.numpy as jnp
from jax import lax
from jax.experimental import pallas as pl
from jax.experimental.pallas import tpu as pltpu
from jax.sharding import PartitionSpec as P

MESH = pl.DeviceIdType.MESH
BF = jnp.bfloat16
F32 = jnp.float32
H = 8
E = 64
C = 1024
SCALE = 0.125
NEG = -1e30
T = 128
KB = 256
NB = 16
NT = (((1,), (1,)), ((), ()))
TN = (((0,), (0,)), ((), ()))


def vm(n):
    return [pl.BlockSpec(memory_space=pltpu.VMEM)] * n


def loop(a, b, f):
    def step(d, _):
        f(d)
        return 0

    lax.fori_loop(a, b, step, 0)


def fold(x, op):
    return op(x.reshape(x.shape[0] // 8, 8, x.shape[1]), axis=0)


def remote(src, dst, snd, rcv, where):
    return pltpu.make_async_remote_copy(
        src_ref=src, dst_ref=dst, send_sem=snd, recv_sem=rcv, device_id=where, device_id_type=MESH
    )


def layer_kernel(
    len_ref, q_ref, k_ref, v_ref, x_ref, g_ref, w_ref, ck_ref,
    lo_ref, ig_ref, dq_ref, dk_ref, dv_ref, wo_ref, ko_ref,
    kvs, qs, kv_in, q_in, halo, kx, kt, both, back, m1, l8, acc, lse, rows, att, edge,
    at_in, eb, am, ap, igs, igp, dos, do_in, mx, ge, cs, mk, cf, wg, wg_in,
    kg, k1, k2, ksum, kall, st_a, st_b, sd_a, sd_b, pt_a, pt_b, ds_a, ds_b, top, dqa, dks, dkv_in, dqs, dq_in,
    kv_s, kv_r, q_s, q_r, h_s, h_r, a_s, a_r, e_s, e_r, d_s, d_r, p_s, p_r,
    f_s, f_r, r_s, r_r, w_s, w_r, k1_s, k1_r, k2_s, k2_r, k3_s, k3_r, g_s, g_r, y_s, y_r,
):
    dp, me = lax.axis_index("dp"), lax.axis_index("ctx")
    core, part, plane = dp % 2, me % 4, me // 4
    partner = {"dp": dp - core + (1 - core)}
    chip = (dp // 2) * 32 + me

    def plane_at(d):
        return {"ctx": (me + 4 * d) % 32}

    def chip_at(d):
        other = (chip + d) % 64
        return {"dp": (other // 32) * 2 + core, "ctx": other % 32}

    def column_at(d):
        other = (dp * 4 + part + d) % 16
        return {"dp": other // 4, "ctx": plane * 4 + other % 4}

    barrier = pltpu.get_barrier_semaphore()

    def signal(where):
        pl.semaphore_signal(barrier, inc=1, device_id=where, device_id_type=MESH)

    loop(1, 64, lambda d: signal(chip_at(d)))
    loop(0, 8, lambda d: signal({"dp": (d // 4) * 2 + 1 - core, "ctx": plane * 4 + d % 4}))

    for h in range(H):
        cols = slice(h * E, (h + 1) * E)
        kvs[h] = jnp.concatenate([k_ref[:, cols], v_ref[:, cols]], axis=1)
    qt = (q_ref[...].astype(F32) * SCALE).T.astype(BF)
    for h in range(H):
        qs[h] = qt[h * E : (h + 1) * E, :]
    kv_in[0] = kvs[plane]
    q_in[0] = qs[plane]

    s1 = len_ref[dp, 0]
    s2 = s1 + len_ref[dp, 1]
    s3 = s2 + len_ref[dp, 2]
    s4 = s3 + len_ref[dp, 3]

    def record_of(pos):
        one = lambda s: jnp.where(pos >= s, 1, 0)
        return one(s1) + one(s2) + one(s3)

    pl.semaphore_wait(barrier, 71)

    q_copy = lambda d: remote(qs.at[(plane + d) % 8], q_in.at[d], q_s.at[d], q_r.at[d], plane_at(d))
    slot = lambda e, f: f // 2 * 16 + 2 * e + f % 2
    owner = lambda n: (plane - n // 2 % 8 + 8) % 8 * 4 + (part - n // 16 * 2 - n % 2 + 4) % 4
    kv_copy = lambda e: remote(
        kvs.at[(plane + e) % 8], kv_in.at[slot(e, 0)], kv_s.at[e], kv_r.at[e], plane_at(e)
    )
    up, down = {"ctx": plane * 4 + (part + 1) % 4}, {"ctx": plane * 4 + (part + 3) % 4}

    def pass_on(e, n):
        return remote(
            kv_in.at[slot(e, 0)], kv_in.at[slot(e, (3, 1)[n])], f_s.at[n, e], f_r.at[n, e], (down, up)[n]
        )

    def relay(e, n):
        half = pl.ds((1 - n) * 64, 64)
        return remote(
            kv_in.at[slot(e, (3, 1)[n]), half],
            kv_in.at[slot(e, 2), half],
            r_s.at[n, e],
            r_r.at[n, e],
            (down, up)[n],
        )

    def stage_pass(e):
        pass_on(e, 0).start()
        pass_on(e, 1).start()

    def stage_relay(e):
        for n in range(2):
            pass_on(e, n).wait_recv()
            relay(e, n).start()

    def stage_last(e):
        relay(e, 0).wait_recv()
        relay(e, 1).wait_recv()

    def stage_first(e):
        kv_copy(e).wait_recv()
        stage_pass(e)

    def halo_copy(a, up):
        ref, s = (x_ref, g_ref)[a], 0 if up else 1
        return remote(
            ref.at[pl.ds(T - 8, 8)] if up else ref.at[pl.ds(0, 8)],
            halo.at[a, s],
            h_s.at[a, s],
            h_r.at[a, s],
            {"ctx": (me + (1 if up else 31)) % 32},
        )

    halos = [halo_copy(a, up) for a in range(2) for up in (True, False)]
    loop(1, 8, lambda d: q_copy(d).start())
    loop(1, 8, lambda e: kv_copy(e).start())
    stage_pass(0)
    for c in halos:
        c.start()

    m1[...] = jnp.full((1, H * T), NEG, F32)
    l8[...] = jnp.zeros((8, H * T), F32)
    acc[...] = jnp.zeros((E, H * T), F32)
    lane = lax.broadcasted_iota(jnp.int32, (1, 2 * E), 1)
    pick = lambda a, b, c, d, e: jnp.where(
        lane == 0, a, jnp.where(lane == 1, b, jnp.where(lane == 2, c, jnp.where(lane == 3, d, e)))
    )
    begin, end = pick(0, s1, s2, s3, s4), pick(s1, s2, s3, s4, s4)

    for i in range(H):
        pos = (i * 4 + part) * T + lax.broadcasted_iota(jnp.int32, (2 * E, T), 1)
        row = lax.broadcasted_iota(jnp.int32, (2 * E, T), 0)
        both[i, : 2 * E] = jnp.zeros((2 * E, 2 * T), BF)
        both[i, 2 * E :, :T] = jnp.where((row < 4) & (record_of(pos) != row), NEG, 0.0).astype(BF)
        both[i, 2 * E :, T:] = jnp.zeros((2 * E, T), BF)

    pos = me * T - 4 + lax.broadcasted_iota(jnp.int32, (136, 128), 0)
    label = lambda p: jnp.where((p >= 0) & (p < s4), record_of(p), -1)
    mine = label(pos)
    for j in range(9):
        mk[j] = jnp.where(label(pos + (j - 4)) == mine, 1.0, 0.0)
    cf[0:9] = ck_ref[...].astype(F32)
    ge[8:136] = g_ref[...].astype(F32)

    loop(1, 8, lambda d: q_copy(d).wait_recv())
    for i in range(H):
        both[i, :E, :T] = q_in[(plane - i + 8) % 8]

    def build(t):
        for u in range(2):
            kv = kv_in[2 * t + u]
            at = slice(u * T, (u + 1) * T)
            kt[t, :, at] = kv.astype(F32).T.astype(BF)
            kx[t, at, : 2 * E] = kv
            p = owner(2 * t + u) * T + lax.broadcasted_iota(jnp.int32, (T, 2 * E), 0)
            kx[t, at, 2 * E :] = jnp.where((p >= begin) & (p < end), 1.0, 0.0).astype(BF)

    def score(t, st):
        for i in range(H):
            s = jnp.dot(kx[t], both[i, :, :T], preferred_element_type=F32)
            st[i] = s
            top[:, i * T : (i + 1) * T] = fold(s, jnp.max)

    def weigh(t, st, pt):
        old = m1[...]
        new = jnp.maximum(old, jnp.max(top[...], axis=0, keepdims=True))
        scale = jnp.exp(old - new)
        m1[...] = new
        return new, scale

    def spread(t, st, pt, new, scale):
        for i in range(H):
            cols = slice(i * T, (i + 1) * T)
            p = jnp.exp(st[i] - new[:, cols])
            l8[:, cols] = l8[:, cols] * scale[:, cols] + fold(p, jnp.sum)
            pt[:, cols] = p.astype(BF)
        for i in range(0, H, 2):
            cols = slice(i * T, (i + 2) * T)
            acc[:, cols] = acc[:, cols] * scale[:, cols] + jnp.dot(
                kt[t, E:], pt[:, cols], preferred_element_type=F32
            )

    loop(1, 8, stage_first)
    stage_relay(0)
    build(0)
    score(0, st_a)

    def forward_step(u):
        t = 2 * u

        @pl.when(u < 4)
        def _():
            stage_relay(2 * u + 1)

        @pl.when(u < 3)
        def _():
            stage_relay(2 * u + 2)

        @pl.when(u > 3)
        def _():
            stage_last(2 * u - 7)

        @pl.when((u > 2) & (u < 7))
        def _():
            stage_last(2 * u - 6)

        later = jnp.minimum(t + 2, NB - 1)
        build(t + 1)
        build(later)
        w = weigh(t, st_a, pt_a)
        score(t + 1, st_b)
        spread(t, st_a, pt_a, *w)
        w = weigh(t + 1, st_b, pt_b)
        score(later, st_a)
        spread(t + 1, st_b, pt_b, *w)

    loop(0, NB // 2, forward_step)
    for i in range(H):
        cols = slice(i * T, (i + 1) * T)
        total = jnp.sum(l8[:, cols], axis=0, keepdims=True)
        lse[:, cols] = m1[:, cols] + jnp.log(total)
        out = acc[:, cols] / total
        att[i] = out.astype(BF)
        wide = jnp.concatenate([out, jnp.zeros((E, T), F32)], axis=0).T
        edge[i, 0] = wide[:8].astype(BF)
        edge[i, 1] = wide[T - 8 :].astype(BF)

    a_copy = lambda d: remote(att.at[(plane + d) % 8], at_in.at[plane], a_s.at[d], a_r.at[d], plane_at(d))

    def e_copy(i, late):
        other = (4 * i + part + (1 if late else 31)) % 32
        u = 1 if late else 0
        return remote(
            edge.at[i, u], eb.at[1 - u, plane], e_s.at[u, i], e_r.at[1 - u, plane], {"ctx": other}
        )

    e_arrival = lambda h, s: remote(edge.at[0, 0], eb.at[s, h], e_s.at[0, 0], e_r.at[s, h], partner)
    loop(1, 8, lambda d: a_copy(d).start())

    def edge_start(i):
        e_copy(i, True).start()
        e_copy(i, False).start()

    loop(0, 8, edge_start)
    at_in[plane] = att[plane]
    for c in halos:
        c.wait()
    ge[0:8] = halo[1, 0].astype(F32)
    ge[136:144] = halo[1, 1].astype(F32)
    loop(1, 8, lambda d: q_copy(d).wait_send())
    loop(1, 8, lambda e: kv_copy(e).wait_send())

    def sent(e):
        for n in range(2):
            pass_on(e, n).wait_send()
            relay(e, n).wait_send()

    loop(0, 8, sent)
    loop(1, 8, lambda d: a_copy(d).wait())

    def edge_wait(i):
        e_copy(i, True).wait_send()
        e_copy(i, False).wait_send()
        e_arrival(i, 0).wait_recv()
        e_arrival(i, 1).wait_recv()

    loop(0, 8, edge_wait)

    am[...] = at_in[...].astype(F32).reshape(H * E, T).T.astype(BF)
    pair = lambda src, dst, n: remote(src, dst, p_s.at[n], p_r.at[n], partner)
    send_att = pair(am, ap, 0)
    send_att.start()
    sides = jnp.concatenate(
        [jnp.concatenate([eb[s, h][:, :E] for h in range(H)], axis=1) for s in range(2)], axis=0
    )

    def chunk(c):
        cols = pl.ds(pl.multiple_of(c * 128, 128), 128)
        wc = w_ref[cols, :]
        main = lax.dot_general(am[...], wc, NT, preferred_element_type=F32)
        rim = lax.dot_general(sides, wc, NT, preferred_element_type=F32)
        rnd = lambda y: y.astype(BF).astype(F32)
        mx[8:136] = rnd(x_ref[:, cols].astype(F32) + main)
        mx[0:8] = rnd(halo[0, 0, :, cols].astype(F32) + rim[0:8])
        mx[136:144] = rnd(halo[0, 1, :, cols].astype(F32) + rim[8:16])
        conv = jnp.zeros((136, 128), F32)
        for j in range(9):
            conv = conv + mx[pl.ds(j, 136)] * mk[j] * cf[j : j + 1, cols]
        gate = jax.nn.sigmoid(conv)
        cg = ge[pl.ds(4, 136), cols] * gate * (1.0 + conv * (1.0 - gate))
        cs[...] = rnd(cg)
        silu = conv * gate
        lo_ref[:, cols] = (mx[8:136] + silu[4:132]).astype(BF)
        deep = ge[8:136, cols]
        for j in range(9):
            deep = deep + cs[pl.ds(8 - j, 128)] * mk[8 - j, pl.ds(4, 128)] * cf[j : j + 1, cols]
        ig = deep.astype(BF)
        ig_ref[:, cols] = ig
        igs[c // 2, :, pl.ds(pl.multiple_of((c % 2) * 128, 128), 128)] = ig
        cg_own = cs[pl.ds(4, 128)]
        sums = []
        for j in range(9):
            sums.append(
                jnp.sum(cg_own * mx[pl.ds(4 + j, 128)] * mk[j, pl.ds(4, 128)], axis=0, keepdims=True)
            )
        sums.append(jnp.zeros((7, 128), F32))
        kg[c] = jnp.concatenate(sums, axis=0)

    loop(0, 8, chunk)
    send_ig = [pair(igs.at[2 * z + 1 - core], igp.at[z], 1 + z) for z in range(2)]
    for c in send_ig:
        c.start()
    ag = jnp.zeros((T, H * E), F32)
    for z in range(4):
        ag = ag + jnp.dot(igs[z], w_ref[z * 256 : (z + 1) * 256, :], preferred_element_type=F32)
    dos[...] = ag.astype(BF).astype(F32).T.astype(BF).reshape(H, E, T)
    d_copy = lambda d: remote(dos.at[(plane + d) % 8], do_in.at[plane], d_s.at[d], d_r.at[d], plane_at(d))
    loop(1, 8, lambda d: d_copy(d).start())
    do_in[plane] = dos[plane]

    k1_copy = lambda d: remote(kg.at[(plane + d) % 8], k1.at[plane], k1_s.at[d], k1_r.at[d], plane_at(d))
    k2_copy = lambda d: remote(ksum.at[0], k2.at[dp * 4 + part], k2_s.at[d], k2_r.at[d], column_at(d))
    k3_copy = lambda d: remote(ksum.at[1], kall.at[plane], k3_s.at[d], k3_r.at[d], plane_at(d))
    loop(1, 8, lambda d: k1_copy(d).start())
    k1[plane] = kg[plane]

    w_copy = lambda d: remote(wg.at[(chip + d) % 64], wg_in.at[d], w_s.at[d], w_r.at[d], chip_at(d))
    send_att.wait()
    for c in send_ig:
        c.wait()
    for z in range(2):
        part_sum = lax.dot_general(igs[2 * z + core], am[...], TN, preferred_element_type=F32)
        part_sum = part_sum + lax.dot_general(igp[z], ap[...], TN, preferred_element_type=F32)
        wg[z * 32 : (z + 1) * 32] = part_sum.reshape(32, 8, H * E).astype(BF)
    loop(1, 64, lambda d: w_copy(d).start())

    dqa[...] = jnp.zeros((E, H * T), F32)
    zero = jnp.zeros((E, T), BF)
    loop(1, 8, lambda d: d_copy(d).wait())
    for i in range(H):
        dot = do_in[i]
        rows[i] = jnp.sum(dot.astype(F32) * att[i].astype(F32), axis=0, keepdims=True)
        both[i, E : 2 * E, T:] = dot
        pair_t = jnp.concatenate(
            [
                jnp.concatenate([both[i, :E, :T], zero], axis=0),
                jnp.concatenate([zero, dot], axis=0),
            ],
            axis=1,
        )
        turned = pair_t.astype(F32).T.astype(BF)
        back[i * T : (i + 1) * T] = turned[:T]
        back[(H + i) * T : (H + i + 1) * T] = turned[T:]
    loop(1, 8, lambda d: k1_copy(d).wait())
    ksum[0] = jnp.sum(k1[...], axis=0)
    k2[dp * 4 + part] = ksum[0]
    loop(1, 16, lambda d: k2_copy(d).start())

    g_copy = lambda n: remote(
        dks.at[n],
        dkv_in.at[n],
        g_s.at[n],
        g_r.at[n],
        {"ctx": owner(n)},
    )

    def product(t, sd):
        for i in range(H):
            sd[i] = jnp.dot(kx[t], both[i], preferred_element_type=F32)

    def backward_part(t, sd, pt, dst):
        for i in range(H):
            cols = slice(i * T, (i + 1) * T)
            p = jnp.exp(sd[i, :, :T] - lse[:, cols])
            ds = (p * (sd[i, :, T:] - rows[i])).astype(BF)
            dst[:, cols] = ds
            pt[:, cols] = p.astype(BF)
        for i in range(0, H, 2):
            cols = slice(i * T, (i + 2) * T)
            dqa[:, cols] += jnp.dot(kt[t, :E], dst[:, cols], preferred_element_type=F32)
        dkv = jnp.dot(dst[...], back[: H * T], preferred_element_type=F32)
        dkv = dkv + jnp.dot(pt[...], back[H * T :], preferred_element_type=F32)
        dkv = dkv.astype(BF)
        dks[2 * t] = dkv[:T]
        dks[2 * t + 1] = dkv[T:]

    def backward_step(u):
        t = 2 * u
        product(t + 1, sd_b)
        backward_part(t, sd_a, pt_a, ds_a)
        product(jnp.minimum(t + 2, NB - 1), sd_a)
        backward_part(t + 1, sd_b, pt_b, ds_b)

        @pl.when(u > 0)
        def _():
            g_copy(2 * t).start()

        g_copy(2 * t + 1).start()
        g_copy(2 * t + 2).start()
        g_copy(2 * t + 3).start()

    product(0, sd_a)
    loop(0, NB // 4, backward_step)
    loop(1, 16, lambda d: k2_copy(d).wait())
    ksum[1] = jnp.sum(k2[...], axis=0)
    kall[plane] = ksum[1]
    loop(1, 8, lambda d: k3_copy(d).start())
    loop(NB // 4, NB // 2, backward_step)
    for i in range(H):
        dqs[i] = dqa[:, i * T : (i + 1) * T].astype(BF)
    y_copy = lambda d: remote(dqs.at[(plane + d) % 8], dq_in.at[plane], y_s.at[d], y_r.at[d], plane_at(d))
    loop(1, 8, lambda d: y_copy(d).start())
    dq_in[plane] = dqs[plane]
    dkv_in[0] = dks[0]

    loop(1, 8, lambda d: k3_copy(d).wait())
    ko_ref[...] = kall[...]

    def add(d, total):
        w_copy(d).wait()
        return total + wg_in[d].astype(F32)

    wo_ref[...] = lax.fori_loop(1, 64, add, wg[chip].astype(F32))
    loop(1, 8, lambda d: y_copy(d).wait())
    dq_ref[...] = (dq_in[...].astype(F32).reshape(H * E, T) * SCALE).T.astype(BF)
    loop(1, 32, lambda d: g_copy(d).wait())
    for h in range(H):
        parts = [dkv_in[slot((h - plane + 8) % 8, f)].astype(F32) for f in range(4)]
        total = (parts[0] + parts[1]) + (parts[2] + parts[3])
        cols = slice(h * E, (h + 1) * E)
        dk_ref[:, cols] = total[:, :E].astype(BF)
        dv_ref[:, cols] = total[:, E:].astype(BF)


def layer(lens, q, k, v, x, g, w, ck):
    dma = pltpu.SemaphoreType.DMA
    V = pltpu.VMEM
    return pl.pallas_call(
        layer_kernel,
        name="layer",
        out_shape=(
            jax.ShapeDtypeStruct((T, C), BF),
            jax.ShapeDtypeStruct((T, C), BF),
            jax.ShapeDtypeStruct((T, H * E), BF),
            jax.ShapeDtypeStruct((T, H * E), BF),
            jax.ShapeDtypeStruct((T, H * E), BF),
            jax.ShapeDtypeStruct((8, H * E), F32),
            jax.ShapeDtypeStruct((8, 16, 128), F32),
        ),
        in_specs=[pl.BlockSpec(memory_space=pltpu.SMEM)] + vm(7),
        out_specs=tuple(vm(7)),
        scratch_shapes=[
            V((H, T, 2 * E), BF),
            V((H, E, T), BF),
            V((32, T, 2 * E), BF),
            V((H, E, T), BF),
            V((2, 2, 8, C), BF),
            V((NB, KB, 4 * E), BF),
            V((NB, 2 * E, KB), BF),
            V((H, 4 * E, 2 * T), BF),
            V((H * 2 * T, 2 * E), BF),
            V((1, H * T), F32),
            V((8, H * T), F32),
            V((E, H * T), F32),
            V((1, H * T), F32),
            V((H, 1, T), F32),
            V((H, E, T), BF),
            V((H, 2, 8, 128), BF),
            V((H, E, T), BF),
            V((2, H, 8, 128), BF),
            V((T, H * E), BF),
            V((T, H * E), BF),
            V((4, T, 256), BF),
            V((2, T, 256), BF),
            V((H, E, T), BF),
            V((H, E, T), BF),
            V((144, 128), F32),
            V((144, C), F32),
            V((136, 128), F32),
            V((9, 136, 128), F32),
            V((16, C), F32),
            V((64, 8, H * E), BF),
            V((64, 8, H * E), BF),
            V((8, 16, 128), F32),
            V((8, 16, 128), F32),
            V((16, 16, 128), F32),
            V((2, 16, 128), F32),
            V((8, 16, 128), F32),
            V((H, KB, T), F32),
            V((H, KB, T), F32),
            V((H, KB, 2 * T), F32),
            V((H, KB, 2 * T), F32),
            V((KB, H * T), BF),
            V((KB, H * T), BF),
            V((KB, H * T), BF),
            V((KB, H * T), BF),
            V((8, H * T), F32),
            V((E, H * T), F32),
            V((32, T, 2 * E), BF),
            V((32, T, 2 * E), BF),
            V((H, E, T), BF),
            V((H, E, T), BF),
        ]
        + [dma((n,)) for n in (8, 8, 8, 8)]
        + [dma((2, 2))] * 2
        + [dma((8,))] * 2
        + [dma((2, 8))] * 2
        + [dma((n,)) for n in (8, 8, 3, 3)]
        + [dma((2, 8))] * 4
        + [dma((n,)) for n in (64, 64, 8, 8, 16, 16, 8, 8, 32, 32, 8, 8)],
        compiler_params=pltpu.CompilerParams(collective_id=0, has_side_effects=True),
    )(lens, q, k, v, x, g, w, ck)


def hand_on_kernel(a, b, c, d, e, f, k, ao, bo, co, do, eo, fo, ko):
    for src, dst in ((a, ao), (b, bo), (c, co), (d, do), (e, eo), (f, fo)):
        dst[...] = src[...]
    for h in range(8):
        ko[:, h * 128 : (h + 1) * 128] = k[h, :9]


def hand_on(*xs):
    shapes = [jax.ShapeDtypeStruct(x.shape, x.dtype) for x in xs[:6]]
    return pl.pallas_call(
        hand_on_kernel,
        name="hand_on",
        out_shape=tuple(shapes) + (jax.ShapeDtypeStruct((9, C), F32),),
        in_specs=vm(7),
        out_specs=tuple(vm(7)),
    )(*xs)


def body(x, q, k, v, w, ck, lens, g):
    outs = hand_on(*layer(lens, q, k, v, x, g, w, ck.T))
    return outs[:6] + (outs[6].T,)


def solution(mesh):
    row = P(("dp", "ctx"), None)
    return jax.shard_map(
        body,
        mesh=mesh,
        in_specs=(row, row, row, row, P(), P(), P(), row),
        out_specs=(row, row, row, row, row, row, P()),
        check_vma=False,
    )
```

```python
import jax
import jax.numpy as jnp
from jax import lax
from jax.experimental import pallas as pl
from jax.experimental.pallas import tpu as pltpu
from jax.sharding import PartitionSpec as P

MESH = pl.DeviceIdType.MESH
BF = jnp.bfloat16
F32 = jnp.float32
H = 8
E = 64
C = 1024
SCALE = 0.125
NEG = -1e30
T = 128
KB = 256
NB = 16
NT = (((1,), (1,)), ((), ()))
TN = (((0,), (0,)), ((), ()))


def vm(n):
    return [pl.BlockSpec(memory_space=pltpu.VMEM)] * n


def loop(a, b, f):
    def step(d, _):
        f(d)
        return 0

    lax.fori_loop(a, b, step, 0)


def fold(x, op):
    return op(x.reshape(x.shape[0] // 8, 8, x.shape[1]), axis=0)


def remote(src, dst, snd, rcv, where):
    return pltpu.make_async_remote_copy(
        src_ref=src, dst_ref=dst, send_sem=snd, recv_sem=rcv, device_id=where, device_id_type=MESH
    )


def layer_kernel(
    len_ref, q_hbm, k_hbm, v_hbm, x_hbm, g_hbm, w_hbm, ck_ref,
    lo_hbm, ig_hbm, dq_ref, dk_ref, dv_ref, wo_ref, ko_ref,
    q_ref, k_ref, v_ref, x_ref, g_ref, w_ref, lo_ref, ig_ref, load, kvs, qs, kv_in, q_in, halo, kx, kt, both, back, m1, l8, acc, lse, rows, att, edge,
    at_in, eb, am, ap, igs, igp, dos, do_in, mx, ge, cs, mk, cf, wg, wg_in,
    kg, k1, k2, ksum, kall, st_a, st_b, sd_a, sd_b, pt_a, pt_b, ds_a, ds_b, top, dqa, dks, dkv_in, dqs, dq_in,
    kv_s, kv_r, q_s, q_r, h_s, h_r, a_s, a_r, e_s, e_r, d_s, d_r, p_s, p_r,
    f_s, f_r, r_s, r_r, w_s, w_r, k1_s, k1_r, k2_s, k2_r, k3_s, k3_r, g_s, g_r, y_s, y_r,
):
    dp, me = lax.axis_index("dp"), lax.axis_index("ctx")
    core, part, plane = dp % 2, me % 4, me // 4
    partner = {"dp": dp - core + (1 - core)}
    chip = (dp // 2) * 32 + me

    def plane_at(d):
        return {"ctx": (me + 4 * d) % 32}

    def chip_at(d):
        other = (chip + d) % 64
        return {"dp": (other // 32) * 2 + core, "ctx": other % 32}

    def column_at(d):
        other = (dp * 4 + part + d) % 16
        return {"dp": other // 4, "ctx": plane * 4 + other % 4}

    homes = ((q_hbm, q_ref), (k_hbm, k_ref), (v_hbm, v_ref), (g_hbm, g_ref), (x_hbm, x_ref), (w_hbm, w_ref))
    loads = [pltpu.make_async_copy(src, dst, load.at[n]) for n, (src, dst) in enumerate(homes)]
    for c in loads:
        c.start()

    barrier = pltpu.get_barrier_semaphore()

    def signal(where):
        pl.semaphore_signal(barrier, inc=1, device_id=where, device_id_type=MESH)

    loop(1, 64, lambda d: signal(chip_at(d)))
    loop(0, 8, lambda d: signal({"dp": (d // 4) * 2 + 1 - core, "ctx": plane * 4 + d % 4}))

    for c in loads[:3]:
        c.wait()
    for h in range(H):
        cols = slice(h * E, (h + 1) * E)
        kvs[h] = jnp.concatenate([k_ref[:, cols], v_ref[:, cols]], axis=1)
    qt = (q_ref[...].astype(F32) * SCALE).T.astype(BF)
    for h in range(H):
        qs[h] = qt[h * E : (h + 1) * E, :]
    kv_in[0] = kvs[plane]
    q_in[0] = qs[plane]

    s1 = len_ref[dp, 0]
    s2 = s1 + len_ref[dp, 1]
    s3 = s2 + len_ref[dp, 2]
    s4 = s3 + len_ref[dp, 3]

    def record_of(pos):
        one = lambda s: jnp.where(pos >= s, 1, 0)
        return one(s1) + one(s2) + one(s3)

    pl.semaphore_wait(barrier, 71)

    q_copy = lambda d: remote(qs.at[(plane + d) % 8], q_in.at[d], q_s.at[d], q_r.at[d], plane_at(d))
    slot = lambda e, f: f // 2 * 16 + 2 * e + f % 2
    owner = lambda n: (plane - n // 2 % 8 + 8) % 8 * 4 + (part - n // 16 * 2 - n % 2 + 4) % 4
    kv_copy = lambda e: remote(
        kvs.at[(plane + e) % 8], kv_in.at[slot(e, 0)], kv_s.at[e], kv_r.at[e], plane_at(e)
    )
    up, down = {"ctx": plane * 4 + (part + 1) % 4}, {"ctx": plane * 4 + (part + 3) % 4}

    def pass_on(e, n):
        return remote(
            kv_in.at[slot(e, 0)], kv_in.at[slot(e, (3, 1)[n])], f_s.at[n, e], f_r.at[n, e], (down, up)[n]
        )

    def relay(e, n):
        half = pl.ds((1 - n) * 64, 64)
        return remote(
            kv_in.at[slot(e, (3, 1)[n]), half],
            kv_in.at[slot(e, 2), half],
            r_s.at[n, e],
            r_r.at[n, e],
            (down, up)[n],
        )

    def stage_pass(e):
        pass_on(e, 0).start()
        pass_on(e, 1).start()

    def stage_relay(e):
        for n in range(2):
            pass_on(e, n).wait_recv()
            relay(e, n).start()

    def stage_last(e):
        relay(e, 0).wait_recv()
        relay(e, 1).wait_recv()

    def stage_first(e):
        kv_copy(e).wait_recv()
        stage_pass(e)

    def halo_copy(a, up):
        ref, s = (x_ref, g_ref)[a], 0 if up else 1
        return remote(
            ref.at[pl.ds(T - 8, 8)] if up else ref.at[pl.ds(0, 8)],
            halo.at[a, s],
            h_s.at[a, s],
            h_r.at[a, s],
            {"ctx": (me + (1 if up else 31)) % 32},
        )

    halos = [halo_copy(a, up) for a in range(2) for up in (True, False)]
    loop(1, 8, lambda d: q_copy(d).start())
    loop(1, 8, lambda e: kv_copy(e).start())
    stage_pass(0)
    for c in loads[3:]:
        c.wait()
    for c in halos:
        c.start()

    m1[...] = jnp.full((1, H * T), NEG, F32)
    l8[...] = jnp.zeros((8, H * T), F32)
    acc[...] = jnp.zeros((E, H * T), F32)
    lane = lax.broadcasted_iota(jnp.int32, (1, 2 * E), 1)
    pick = lambda a, b, c, d, e: jnp.where(
        lane == 0, a, jnp.where(lane == 1, b, jnp.where(lane == 2, c, jnp.where(lane == 3, d, e)))
    )
    begin, end = pick(0, s1, s2, s3, s4), pick(s1, s2, s3, s4, s4)

    for i in range(H):
        pos = (i * 4 + part) * T + lax.broadcasted_iota(jnp.int32, (2 * E, T), 1)
        row = lax.broadcasted_iota(jnp.int32, (2 * E, T), 0)
        both[i, : 2 * E] = jnp.zeros((2 * E, 2 * T), BF)
        both[i, 2 * E :, :T] = jnp.where((row < 4) & (record_of(pos) != row), NEG, 0.0).astype(BF)
        both[i, 2 * E :, T:] = jnp.zeros((2 * E, T), BF)

    pos = me * T - 4 + lax.broadcasted_iota(jnp.int32, (136, 128), 0)
    label = lambda p: jnp.where((p >= 0) & (p < s4), record_of(p), -1)
    mine = label(pos)
    for j in range(9):
        mk[j] = jnp.where(label(pos + (j - 4)) == mine, 1.0, 0.0)
    cf[0:9] = ck_ref[...].astype(F32)
    ge[8:136] = g_ref[...].astype(F32)

    def mark(t):
        for u in range(2):
            p = owner(2 * t + u) * T + lax.broadcasted_iota(jnp.int32, (T, 2 * E), 0)
            one = jnp.where((p >= begin) & (p < end), 1.0, 0.0).astype(BF)
            kx[t, u * T : (u + 1) * T, 2 * E :] = one

    loop(0, NB, mark)
    loop(1, 8, lambda d: q_copy(d).wait_recv())
    for i in range(H):
        both[i, :E, :T] = q_in[(plane - i + 8) % 8]

    def build(t):
        for u in range(2):
            kv = kv_in[2 * t + u]
            at = slice(u * T, (u + 1) * T)
            kt[t, :, at] = kv.astype(F32).T.astype(BF)
            kx[t, at, : 2 * E] = kv

    def score(t, st):
        for i in range(H):
            s = jnp.dot(kx[t], both[i, :, :T], preferred_element_type=F32)
            st[i] = s
            top[:, i * T : (i + 1) * T] = fold(s, jnp.max)

    def weigh(t, st, pt):
        old = m1[...]
        new = jnp.maximum(old, jnp.max(top[...], axis=0, keepdims=True))
        scale = jnp.exp(old - new)
        m1[...] = new
        return new, scale

    def spread(t, st, pt, new, scale):
        for i in range(H):
            cols = slice(i * T, (i + 1) * T)
            p = jnp.exp(st[i] - new[:, cols])
            l8[:, cols] = l8[:, cols] * scale[:, cols] + fold(p, jnp.sum)
            pt[:, cols] = p.astype(BF)
        for i in range(0, H, 2):
            cols = slice(i * T, (i + 2) * T)
            acc[:, cols] = acc[:, cols] * scale[:, cols] + jnp.dot(
                kt[t, E:], pt[:, cols], preferred_element_type=F32
            )

    loop(1, 8, stage_first)
    stage_relay(0)
    build(0)
    score(0, st_a)

    def forward_step(u):
        t = 2 * u

        @pl.when(u < 4)
        def _():
            stage_relay(2 * u + 1)

        @pl.when(u < 3)
        def _():
            stage_relay(2 * u + 2)

        @pl.when(u > 3)
        def _():
            stage_last(2 * u - 7)

        @pl.when((u > 2) & (u < 7))
        def _():
            stage_last(2 * u - 6)

        later = jnp.minimum(t + 2, NB - 1)
        build(t + 1)
        build(later)
        w = weigh(t, st_a, pt_a)
        score(t + 1, st_b)
        spread(t, st_a, pt_a, *w)
        w = weigh(t + 1, st_b, pt_b)
        score(later, st_a)
        spread(t + 1, st_b, pt_b, *w)

    loop(0, NB // 2, forward_step)
    for i in range(H):
        cols = slice(i * T, (i + 1) * T)
        total = jnp.sum(l8[:, cols], axis=0, keepdims=True)
        lse[:, cols] = m1[:, cols] + jnp.log(total)
        out = acc[:, cols] / total
        att[i] = out.astype(BF)
        wide = jnp.concatenate([out, jnp.zeros((E, T), F32)], axis=0).T
        edge[i, 0] = wide[:8].astype(BF)
        edge[i, 1] = wide[T - 8 :].astype(BF)

    a_copy = lambda d: remote(att.at[(plane + d) % 8], at_in.at[plane], a_s.at[d], a_r.at[d], plane_at(d))

    def e_copy(i, late):
        other = (4 * i + part + (1 if late else 31)) % 32
        u = 1 if late else 0
        return remote(
            edge.at[i, u], eb.at[1 - u, plane], e_s.at[u, i], e_r.at[1 - u, plane], {"ctx": other}
        )

    e_arrival = lambda h, s: remote(edge.at[0, 0], eb.at[s, h], e_s.at[0, 0], e_r.at[s, h], partner)
    loop(1, 8, lambda d: a_copy(d).start())

    def edge_start(i):
        e_copy(i, True).start()
        e_copy(i, False).start()

    loop(0, 8, edge_start)
    at_in[plane] = att[plane]
    for c in halos:
        c.wait()
    ge[0:8] = halo[1, 0].astype(F32)
    ge[136:144] = halo[1, 1].astype(F32)
    loop(1, 8, lambda d: q_copy(d).wait_send())
    loop(1, 8, lambda e: kv_copy(e).wait_send())

    def sent(e):
        for n in range(2):
            pass_on(e, n).wait_send()
            relay(e, n).wait_send()

    loop(0, 8, sent)
    loop(1, 8, lambda d: a_copy(d).wait())

    def edge_wait(i):
        e_copy(i, True).wait_send()
        e_copy(i, False).wait_send()
        e_arrival(i, 0).wait_recv()
        e_arrival(i, 1).wait_recv()

    loop(0, 8, edge_wait)

    am[...] = at_in[...].astype(F32).reshape(H * E, T).T.astype(BF)
    pair = lambda src, dst, n: remote(src, dst, p_s.at[n], p_r.at[n], partner)
    send_att = pair(am, ap, 0)
    send_att.start()
    sides = jnp.concatenate(
        [jnp.concatenate([eb[s, h][:, :E] for h in range(H)], axis=1) for s in range(2)], axis=0
    )

    def chunk(c):
        cols = pl.ds(pl.multiple_of(c * 128, 128), 128)
        wc = w_ref[cols, :]
        main = lax.dot_general(am[...], wc, NT, preferred_element_type=F32)
        rim = lax.dot_general(sides, wc, NT, preferred_element_type=F32)
        rnd = lambda y: y.astype(BF).astype(F32)
        mx[8:136] = rnd(x_ref[:, cols].astype(F32) + main)
        mx[0:8] = rnd(halo[0, 0, :, cols].astype(F32) + rim[0:8])
        mx[136:144] = rnd(halo[0, 1, :, cols].astype(F32) + rim[8:16])
        conv = jnp.zeros((136, 128), F32)
        for j in range(9):
            conv = conv + mx[pl.ds(j, 136)] * mk[j] * cf[j : j + 1, cols]
        gate = jax.nn.sigmoid(conv)
        cg = ge[pl.ds(4, 136), cols] * gate * (1.0 + conv * (1.0 - gate))
        cs[...] = rnd(cg)
        silu = conv * gate
        lo_ref[:, cols] = (mx[8:136] + silu[4:132]).astype(BF)
        deep = ge[8:136, cols]
        for j in range(9):
            deep = deep + cs[pl.ds(8 - j, 128)] * mk[8 - j, pl.ds(4, 128)] * cf[j : j + 1, cols]
        ig = deep.astype(BF)
        ig_ref[:, cols] = ig
        igs[c // 2, :, pl.ds(pl.multiple_of((c % 2) * 128, 128), 128)] = ig
        cg_own = cs[pl.ds(4, 128)]
        sums = []
        for j in range(9):
            sums.append(
                jnp.sum(cg_own * mx[pl.ds(4 + j, 128)] * mk[j, pl.ds(4, 128)], axis=0, keepdims=True)
            )
        sums.append(jnp.zeros((7, 128), F32))
        kg[c] = jnp.concatenate(sums, axis=0)

    loop(0, 8, chunk)
    stores = [
        pltpu.make_async_copy(src, dst, load.at[6 + n])
        for n, (src, dst) in enumerate(((lo_ref, lo_hbm), (ig_ref, ig_hbm)))
    ]
    send_ig = [pair(igs.at[2 * z + 1 - core], igp.at[z], 1 + z) for z in range(2)]
    for c in send_ig:
        c.start()
    ag = jnp.zeros((T, H * E), F32)
    for z in range(4):
        ag = ag + jnp.dot(igs[z], w_ref[z * 256 : (z + 1) * 256, :], preferred_element_type=F32)
    dos[...] = ag.astype(BF).astype(F32).T.astype(BF).reshape(H, E, T)
    d_copy = lambda d: remote(dos.at[(plane + d) % 8], do_in.at[plane], d_s.at[d], d_r.at[d], plane_at(d))
    loop(1, 8, lambda d: d_copy(d).start())
    do_in[plane] = dos[plane]

    k1_copy = lambda d: remote(kg.at[(plane + d) % 8], k1.at[plane], k1_s.at[d], k1_r.at[d], plane_at(d))
    k2_copy = lambda d: remote(ksum.at[0], k2.at[dp * 4 + part], k2_s.at[d], k2_r.at[d], column_at(d))
    k3_copy = lambda d: remote(ksum.at[1], kall.at[plane], k3_s.at[d], k3_r.at[d], plane_at(d))
    loop(1, 8, lambda d: k1_copy(d).start())
    k1[plane] = kg[plane]

    w_copy = lambda d: remote(wg.at[(chip + d) % 64], wg_in.at[d], w_s.at[d], w_r.at[d], chip_at(d))
    send_att.wait()
    for c in send_ig:
        c.wait()
    for z in range(2):
        part_sum = lax.dot_general(igs[2 * z + core], am[...], TN, preferred_element_type=F32)
        part_sum = part_sum + lax.dot_general(igp[z], ap[...], TN, preferred_element_type=F32)
        wg[z * 32 : (z + 1) * 32] = part_sum.reshape(32, 8, H * E).astype(BF)
    loop(1, 64, lambda d: w_copy(d).start())
    for c in stores:
        c.start()

    dqa[...] = jnp.zeros((E, H * T), F32)
    zero = jnp.zeros((E, T), BF)
    loop(1, 8, lambda d: d_copy(d).wait())
    for i in range(H):
        dot = do_in[i]
        rows[i] = jnp.sum(dot.astype(F32) * att[i].astype(F32), axis=0, keepdims=True)
        both[i, E : 2 * E, T:] = dot
        pair_t = jnp.concatenate(
            [
                jnp.concatenate([both[i, :E, :T], zero], axis=0),
                jnp.concatenate([zero, dot], axis=0),
            ],
            axis=1,
        )
        turned = pair_t.astype(F32).T.astype(BF)
        back[i * T : (i + 1) * T] = turned[:T]
        back[(H + i) * T : (H + i + 1) * T] = turned[T:]
    loop(1, 8, lambda d: k1_copy(d).wait())
    ksum[0] = jnp.sum(k1[...], axis=0)
    k2[dp * 4 + part] = ksum[0]
    loop(1, 16, lambda d: k2_copy(d).start())

    g_copy = lambda n: remote(
        dks.at[n],
        dkv_in.at[n],
        g_s.at[n],
        g_r.at[n],
        {"ctx": owner(n)},
    )

    def product(t, sd):
        for i in range(H):
            sd[i] = jnp.dot(kx[t], both[i], preferred_element_type=F32)

    def backward_part(t, sd, pt, dst):
        for i in range(H):
            cols = slice(i * T, (i + 1) * T)
            p = jnp.exp(sd[i, :, :T] - lse[:, cols])
            ds = (p * (sd[i, :, T:] - rows[i])).astype(BF)
            dst[:, cols] = ds
            pt[:, cols] = p.astype(BF)
        for i in range(0, H, 2):
            cols = slice(i * T, (i + 2) * T)
            dqa[:, cols] += jnp.dot(kt[t, :E], dst[:, cols], preferred_element_type=F32)
        dkv = jnp.dot(dst[...], back[: H * T], preferred_element_type=F32)
        dkv = dkv + jnp.dot(pt[...], back[H * T :], preferred_element_type=F32)
        dkv = dkv.astype(BF)
        dks[2 * t] = dkv[:T]
        dks[2 * t + 1] = dkv[T:]

    def backward_step(u):
        t = 2 * u
        product(t + 1, sd_b)
        backward_part(t, sd_a, pt_a, ds_a)
        product(jnp.minimum(t + 2, NB - 1), sd_a)
        backward_part(t + 1, sd_b, pt_b, ds_b)

        @pl.when(u > 0)
        def _():
            g_copy(2 * t).start()

        g_copy(2 * t + 1).start()
        g_copy(2 * t + 2).start()
        g_copy(2 * t + 3).start()

    product(0, sd_a)
    loop(0, NB // 4, backward_step)
    loop(1, 16, lambda d: k2_copy(d).wait())
    ksum[1] = jnp.sum(k2[...], axis=0)
    kall[plane] = ksum[1]
    loop(1, 8, lambda d: k3_copy(d).start())
    loop(NB // 4, NB // 2, backward_step)
    for i in range(H):
        dqs[i] = dqa[:, i * T : (i + 1) * T].astype(BF)
    y_copy = lambda d: remote(dqs.at[(plane + d) % 8], dq_in.at[plane], y_s.at[d], y_r.at[d], plane_at(d))
    loop(1, 8, lambda d: y_copy(d).start())
    dq_in[plane] = dqs[plane]
    dkv_in[0] = dks[0]

    for c in stores:
        c.wait()
    loop(1, 8, lambda d: k3_copy(d).wait())
    ko_ref[...] = kall[...]

    def add(d, total):
        w_copy(d).wait()
        return total + wg_in[d].astype(F32)

    wo_ref[...] = lax.fori_loop(1, 64, add, wg[chip].astype(F32))
    loop(1, 8, lambda d: y_copy(d).wait())
    dq_ref[...] = (dq_in[...].astype(F32).reshape(H * E, T) * SCALE).T.astype(BF)
    loop(1, 32, lambda d: g_copy(d).wait())
    for h in range(H):
        parts = [dkv_in[slot((h - plane + 8) % 8, f)].astype(F32) for f in range(4)]
        total = (parts[0] + parts[1]) + (parts[2] + parts[3])
        cols = slice(h * E, (h + 1) * E)
        dk_ref[:, cols] = total[:, :E].astype(BF)
        dv_ref[:, cols] = total[:, E:].astype(BF)


def layer(lens, q, k, v, x, g, w, ck):
    dma = pltpu.SemaphoreType.DMA
    V = pltpu.VMEM
    return pl.pallas_call(
        layer_kernel,
        name="layer",
        out_shape=(
            jax.ShapeDtypeStruct((T, C), BF),
            jax.ShapeDtypeStruct((T, C), BF),
            jax.ShapeDtypeStruct((T, H * E), BF),
            jax.ShapeDtypeStruct((T, H * E), BF),
            jax.ShapeDtypeStruct((T, H * E), BF),
            jax.ShapeDtypeStruct((8, H * E), F32),
            jax.ShapeDtypeStruct((8, 16, 128), F32),
        ),
        in_specs=[pl.BlockSpec(memory_space=pltpu.SMEM)] + [pl.BlockSpec(memory_space=pl.ANY)] * 6 + vm(1),
        out_specs=(pl.BlockSpec(memory_space=pl.ANY),) * 2 + tuple(vm(5)),
        scratch_shapes=[
            V((T, H * E), BF),
            V((T, H * E), BF),
            V((T, H * E), BF),
            V((T, C), BF),
            V((T, C), BF),
            V((C, H * E), BF),
            V((T, C), BF),
            V((T, C), BF),
            dma((8,)),
            V((H, T, 2 * E), BF),
            V((H, E, T), BF),
            V((32, T, 2 * E), BF),
            V((H, E, T), BF),
            V((2, 2, 8, C), BF),
            V((NB, KB, 4 * E), BF),
            V((NB, 2 * E, KB), BF),
            V((H, 4 * E, 2 * T), BF),
            V((H * 2 * T, 2 * E), BF),
            V((1, H * T), F32),
            V((8, H * T), F32),
            V((E, H * T), F32),
            V((1, H * T), F32),
            V((H, 1, T), F32),
            V((H, E, T), BF),
            V((H, 2, 8, 128), BF),
            V((H, E, T), BF),
            V((2, H, 8, 128), BF),
            V((T, H * E), BF),
            V((T, H * E), BF),
            V((4, T, 256), BF),
            V((2, T, 256), BF),
            V((H, E, T), BF),
            V((H, E, T), BF),
            V((144, 128), F32),
            V((144, C), F32),
            V((136, 128), F32),
            V((9, 136, 128), F32),
            V((16, C), F32),
            V((64, 8, H * E), BF),
            V((64, 8, H * E), BF),
            V((8, 16, 128), F32),
            V((8, 16, 128), F32),
            V((16, 16, 128), F32),
            V((2, 16, 128), F32),
            V((8, 16, 128), F32),
            V((H, KB, T), F32),
            V((H, KB, T), F32),
            V((H, KB, 2 * T), F32),
            V((H, KB, 2 * T), F32),
            V((KB, H * T), BF),
            V((KB, H * T), BF),
            V((KB, H * T), BF),
            V((KB, H * T), BF),
            V((8, H * T), F32),
            V((E, H * T), F32),
            V((32, T, 2 * E), BF),
            V((32, T, 2 * E), BF),
            V((H, E, T), BF),
            V((H, E, T), BF),
        ]
        + [dma((n,)) for n in (8, 8, 8, 8)]
        + [dma((2, 2))] * 2
        + [dma((8,))] * 2
        + [dma((2, 8))] * 2
        + [dma((n,)) for n in (8, 8, 3, 3)]
        + [dma((2, 8))] * 4
        + [dma((n,)) for n in (64, 64, 8, 8, 16, 16, 8, 8, 32, 32, 8, 8)],
        compiler_params=pltpu.CompilerParams(collective_id=0, has_side_effects=True),
    )(lens, q, k, v, x, g, w, ck)


def hand_on_kernel(a, b, c, d, e, f, k, ao, bo, co, do, eo, fo, ko):
    for src, dst in ((a, ao), (b, bo), (c, co), (d, do), (e, eo), (f, fo)):
        dst[...] = src[...]
    for h in range(8):
        ko[:, h * 128 : (h + 1) * 128] = k[h, :9]


def hand_on(*xs):
    shapes = [jax.ShapeDtypeStruct(x.shape, x.dtype) for x in xs[:6]]
    return pl.pallas_call(
        hand_on_kernel,
        name="hand_on",
        out_shape=tuple(shapes) + (jax.ShapeDtypeStruct((9, C), F32),),
        in_specs=vm(7),
        out_specs=tuple(vm(7)),
    )(*xs)


def body(x, q, k, v, w, ck, lens, g):
    outs = hand_on(*layer(lens, q, k, v, x, g, w, ck.T))
    return outs[:6] + (outs[6].T,)


def solution(mesh):
    row = P(("dp", "ctx"), None)
    return jax.shard_map(
        body,
        mesh=mesh,
        in_specs=(row, row, row, row, P(), P(), P(), row),
        out_specs=(row, row, row, row, row, row, P()),
        check_vma=False,
    )
```

```python
import jax
import jax.numpy as jnp
from jax import lax
from jax.experimental import pallas as pl
from jax.experimental.pallas import tpu as pltpu
from jax.sharding import PartitionSpec as P

MESH = pl.DeviceIdType.MESH
BF = jnp.bfloat16
F32 = jnp.float32
H = 8
E = 64
C = 1024
SCALE = 0.125
NEG = -1e30
T = 128
KB = 256
NB = 16
NT = (((1,), (1,)), ((), ()))
TN = (((0,), (0,)), ((), ()))


def vm(n):
    return [pl.BlockSpec(memory_space=pltpu.VMEM)] * n


def loop(a, b, f):
    def step(d, _):
        f(d)
        return 0

    lax.fori_loop(a, b, step, 0)


def fold(x, op):
    return op(x.reshape(x.shape[0] // 8, 8, x.shape[1]), axis=0)


def remote(src, dst, snd, rcv, where):
    return pltpu.make_async_remote_copy(
        src_ref=src, dst_ref=dst, send_sem=snd, recv_sem=rcv, device_id=where, device_id_type=MESH
    )


def layer_kernel(
    len_ref, q_hbm, k_hbm, v_hbm, x_hbm, g_hbm, w_hbm, ck_ref,
    lo_hbm, ig_hbm, dq_ref, dk_ref, dv_ref, wo_ref, ko_ref,
    q_ref, k_ref, v_ref, x_ref, g_ref, w_ref, lo_ref, ig_ref, load, kvs, qs, kv_in, q_in, halo, kx, kt, both, back, m1, l8, acc, lse, rows, att, edge,
    at_in, eb, am, ap, igs, igp, dos, do_in, mx, ge, cs, mk, cf, wg, wg_in,
    kg, k1, k2, ksum, kall, st_a, st_b, sd_a, sd_b, pt_a, pt_b, ds_a, ds_b, top, dqa, dks, dkv_in, dqs, dq_in,
    met, kv_s, kv_r, q_s, q_r, h_s, h_r, a_s, a_r, e_s, e_r, d_s, d_r, p_s, p_r,
    f_s, f_r, r_s, r_r, w_s, w_r, k1_s, k1_r, k2_s, k2_r, k3_s, k3_r, g_s, g_r, y_s, y_r,
):
    dp, me = lax.axis_index("dp"), lax.axis_index("ctx")
    core, part, plane = dp % 2, me % 4, me // 4
    partner = {"dp": dp - core + (1 - core)}
    chip = (dp // 2) * 32 + me

    def plane_at(d):
        return {"ctx": (me + 4 * d) % 32}

    def chip_at(d):
        other = (chip + d) % 64
        return {"dp": (other // 32) * 2 + core, "ctx": other % 32}

    def column_at(d):
        other = (dp * 4 + part + d) % 16
        return {"dp": other // 4, "ctx": plane * 4 + other % 4}

    homes = ((q_hbm, q_ref), (k_hbm, k_ref), (v_hbm, v_ref), (g_hbm, g_ref), (x_hbm, x_ref), (w_hbm, w_ref))
    loads = [pltpu.make_async_copy(src, dst, load.at[n]) for n, (src, dst) in enumerate(homes)]
    for c in loads:
        c.start()

    barrier = pltpu.get_barrier_semaphore()

    def signal(where):
        pl.semaphore_signal(barrier, inc=1, device_id=where, device_id_type=MESH)

    beyond = {"dp": (dp + 2) % 4}
    up, down = {"ctx": plane * 4 + (part + 1) % 4}, {"ctx": plane * 4 + (part + 3) % 4}
    loop(1, 8, lambda d: signal(plane_at(d)))
    for where in (up, down, {"ctx": (me + 1) % 32}, {"ctx": (me + 31) % 32}, partner, beyond):
        signal(where)

    for c in loads[:3]:
        c.wait()
    for h in range(H):
        cols = slice(h * E, (h + 1) * E)
        kvs[h] = jnp.concatenate([k_ref[:, cols], v_ref[:, cols]], axis=1)
    qt = (q_ref[...].astype(F32) * SCALE).T.astype(BF)
    for h in range(H):
        qs[h] = qt[h * E : (h + 1) * E, :]
    kv_in[0] = kvs[plane]
    q_in[0] = qs[plane]

    s1 = len_ref[dp, 0]
    s2 = s1 + len_ref[dp, 1]
    s3 = s2 + len_ref[dp, 2]
    s4 = s3 + len_ref[dp, 3]

    def record_of(pos):
        one = lambda s: jnp.where(pos >= s, 1, 0)
        return one(s1) + one(s2) + one(s3)

    pl.semaphore_wait(barrier, 13)

    q_copy = lambda d: remote(qs.at[(plane + d) % 8], q_in.at[d], q_s.at[d], q_r.at[d], plane_at(d))
    slot = lambda e, f: f // 2 * 16 + 2 * e + f % 2
    owner = lambda n: (plane - n // 2 % 8 + 8) % 8 * 4 + (part - n // 16 * 2 - n % 2 + 4) % 4
    kv_copy = lambda e: remote(
        kvs.at[(plane + e) % 8], kv_in.at[slot(e, 0)], kv_s.at[e], kv_r.at[e], plane_at(e)
    )

    def pass_on(e, n):
        return remote(
            kv_in.at[slot(e, 0)], kv_in.at[slot(e, (3, 1)[n])], f_s.at[n, e], f_r.at[n, e], (down, up)[n]
        )

    def relay(e, n):
        half = pl.ds((1 - n) * 64, 64)
        return remote(
            kv_in.at[slot(e, (3, 1)[n]), half],
            kv_in.at[slot(e, 2), half],
            r_s.at[n, e],
            r_r.at[n, e],
            (down, up)[n],
        )

    def stage_pass(e):
        pass_on(e, 0).start()
        pass_on(e, 1).start()

    def stage_relay(e):
        for n in range(2):
            pass_on(e, n).wait_recv()
            relay(e, n).start()

    def stage_last(e):
        relay(e, 0).wait_recv()
        relay(e, 1).wait_recv()

    def stage_first(e):
        kv_copy(e).wait_recv()
        stage_pass(e)

    def halo_copy(a, up):
        ref, s = (x_ref, g_ref)[a], 0 if up else 1
        return remote(
            ref.at[pl.ds(T - 8, 8)] if up else ref.at[pl.ds(0, 8)],
            halo.at[a, s],
            h_s.at[a, s],
            h_r.at[a, s],
            {"ctx": (me + (1 if up else 31)) % 32},
        )

    halos = [halo_copy(a, up) for a in range(2) for up in (True, False)]
    loop(1, 8, lambda d: q_copy(d).start())
    loop(1, 8, lambda e: kv_copy(e).start())
    stage_pass(0)
    for c in loads[3:]:
        c.wait()
    for c in halos:
        c.start()

    m1[...] = jnp.full((1, H * T), NEG, F32)
    l8[...] = jnp.zeros((8, H * T), F32)
    acc[...] = jnp.zeros((E, H * T), F32)
    lane = lax.broadcasted_iota(jnp.int32, (1, 2 * E), 1)
    pick = lambda a, b, c, d, e: jnp.where(
        lane == 0, a, jnp.where(lane == 1, b, jnp.where(lane == 2, c, jnp.where(lane == 3, d, e)))
    )
    begin, end = pick(0, s1, s2, s3, s4), pick(s1, s2, s3, s4, s4)

    for i in range(H):
        pos = (i * 4 + part) * T + lax.broadcasted_iota(jnp.int32, (2 * E, T), 1)
        row = lax.broadcasted_iota(jnp.int32, (2 * E, T), 0)
        both[i, : 2 * E] = jnp.zeros((2 * E, 2 * T), BF)
        both[i, 2 * E :, :T] = jnp.where((row < 4) & (record_of(pos) != row), NEG, 0.0).astype(BF)
        both[i, 2 * E :, T:] = jnp.zeros((2 * E, T), BF)

    pos = me * T - 4 + lax.broadcasted_iota(jnp.int32, (136, 128), 0)
    label = lambda p: jnp.where((p >= 0) & (p < s4), record_of(p), -1)
    mine = label(pos)
    for j in range(9):
        mk[j] = jnp.where(label(pos + (j - 4)) == mine, 1.0, 0.0)
    cf[0:9] = ck_ref[...].astype(F32)
    ge[8:136] = g_ref[...].astype(F32)

    def mark(t):
        for u in range(2):
            p = owner(2 * t + u) * T + lax.broadcasted_iota(jnp.int32, (T, 2 * E), 0)
            one = jnp.where((p >= begin) & (p < end), 1.0, 0.0).astype(BF)
            kx[t, u * T : (u + 1) * T, 2 * E :] = one

    loop(0, NB, mark)
    loop(1, 8, lambda d: q_copy(d).wait_recv())
    for i in range(H):
        both[i, :E, :T] = q_in[(plane - i + 8) % 8]

    def build(t):
        for u in range(2):
            kv = kv_in[2 * t + u]
            at = slice(u * T, (u + 1) * T)
            kt[t, :, at] = kv.astype(F32).T.astype(BF)
            kx[t, at, : 2 * E] = kv

    def score(t, st):
        for i in range(H):
            s = jnp.dot(kx[t], both[i, :, :T], preferred_element_type=F32)
            st[i] = s
            top[:, i * T : (i + 1) * T] = fold(s, jnp.max)

    def weigh(t, st, pt):
        old = m1[...]
        new = jnp.maximum(old, jnp.max(top[...], axis=0, keepdims=True))
        scale = jnp.exp(old - new)
        m1[...] = new
        return new, scale

    def spread(t, st, pt, new, scale):
        for i in range(H):
            cols = slice(i * T, (i + 1) * T)
            p = jnp.exp(st[i] - new[:, cols])
            l8[:, cols] = l8[:, cols] * scale[:, cols] + fold(p, jnp.sum)
            pt[:, cols] = p.astype(BF)
        for i in range(0, H, 2):
            cols = slice(i * T, (i + 2) * T)
            acc[:, cols] = acc[:, cols] * scale[:, cols] + jnp.dot(
                kt[t, E:], pt[:, cols], preferred_element_type=F32
            )

    loop(1, 8, stage_first)
    stage_relay(0)
    build(0)
    score(0, st_a)

    def forward_step(u):
        t = 2 * u

        @pl.when(u < 4)
        def _():
            stage_relay(2 * u + 1)

        @pl.when(u < 3)
        def _():
            stage_relay(2 * u + 2)

        @pl.when(u > 3)
        def _():
            stage_last(2 * u - 7)

        @pl.when((u > 2) & (u < 7))
        def _():
            stage_last(2 * u - 6)

        later = jnp.minimum(t + 2, NB - 1)
        build(t + 1)
        build(later)
        w = weigh(t, st_a, pt_a)
        score(t + 1, st_b)
        spread(t, st_a, pt_a, *w)
        w = weigh(t + 1, st_b, pt_b)
        score(later, st_a)
        spread(t + 1, st_b, pt_b, *w)

    loop(0, NB // 2, forward_step)
    pl.semaphore_signal(met, inc=1, device_id=beyond, device_id_type=MESH)
    for i in range(H):
        cols = slice(i * T, (i + 1) * T)
        total = jnp.sum(l8[:, cols], axis=0, keepdims=True)
        lse[:, cols] = m1[:, cols] + jnp.log(total)
        out = acc[:, cols] / total
        att[i] = out.astype(BF)
        wide = jnp.concatenate([out, jnp.zeros((E, T), F32)], axis=0).T
        edge[i, 0] = wide[:8].astype(BF)
        edge[i, 1] = wide[T - 8 :].astype(BF)

    a_copy = lambda d: remote(att.at[(plane + d) % 8], at_in.at[plane], a_s.at[d], a_r.at[d], plane_at(d))

    def e_copy(i, late):
        other = (4 * i + part + (1 if late else 31)) % 32
        u = 1 if late else 0
        return remote(
            edge.at[i, u], eb.at[1 - u, plane], e_s.at[u, i], e_r.at[1 - u, plane], {"ctx": other}
        )

    e_arrival = lambda h, s: remote(edge.at[0, 0], eb.at[s, h], e_s.at[0, 0], e_r.at[s, h], partner)
    loop(1, 8, lambda d: a_copy(d).start())

    def edge_start(i):
        e_copy(i, True).start()
        e_copy(i, False).start()

    loop(0, 8, edge_start)
    at_in[plane] = att[plane]
    for c in halos:
        c.wait()
    ge[0:8] = halo[1, 0].astype(F32)
    ge[136:144] = halo[1, 1].astype(F32)
    loop(1, 8, lambda d: q_copy(d).wait_send())
    loop(1, 8, lambda e: kv_copy(e).wait_send())

    def sent(e):
        for n in range(2):
            pass_on(e, n).wait_send()
            relay(e, n).wait_send()

    loop(0, 8, sent)
    loop(1, 8, lambda d: a_copy(d).wait())

    def edge_wait(i):
        e_copy(i, True).wait_send()
        e_copy(i, False).wait_send()
        e_arrival(i, 0).wait_recv()
        e_arrival(i, 1).wait_recv()

    loop(0, 8, edge_wait)

    am[...] = at_in[...].astype(F32).reshape(H * E, T).T.astype(BF)
    pair = lambda src, dst, n: remote(src, dst, p_s.at[n], p_r.at[n], partner)
    pl.semaphore_wait(met, 1)
    send_att = pair(am, ap, 0)
    send_att.start()
    sides = jnp.concatenate(
        [jnp.concatenate([eb[s, h][:, :E] for h in range(H)], axis=1) for s in range(2)], axis=0
    )

    def chunk(c):
        cols = pl.ds(pl.multiple_of(c * 128, 128), 128)
        wc = w_ref[cols, :]
        main = lax.dot_general(am[...], wc, NT, preferred_element_type=F32)
        rim = lax.dot_general(sides, wc, NT, preferred_element_type=F32)
        rnd = lambda y: y.astype(BF).astype(F32)
        mx[8:136] = rnd(x_ref[:, cols].astype(F32) + main)
        mx[0:8] = rnd(halo[0, 0, :, cols].astype(F32) + rim[0:8])
        mx[136:144] = rnd(halo[0, 1, :, cols].astype(F32) + rim[8:16])
        conv = jnp.zeros((136, 128), F32)
        for j in range(9):
            conv = conv + mx[pl.ds(j, 136)] * mk[j] * cf[j : j + 1, cols]
        gate = jax.nn.sigmoid(conv)
        cg = ge[pl.ds(4, 136), cols] * gate * (1.0 + conv * (1.0 - gate))
        cs[...] = rnd(cg)
        silu = conv * gate
        lo_ref[:, cols] = (mx[8:136] + silu[4:132]).astype(BF)
        deep = ge[8:136, cols]
        for j in range(9):
            deep = deep + cs[pl.ds(8 - j, 128)] * mk[8 - j, pl.ds(4, 128)] * cf[j : j + 1, cols]
        ig = deep.astype(BF)
        ig_ref[:, cols] = ig
        igs[c // 2, :, pl.ds(pl.multiple_of((c % 2) * 128, 128), 128)] = ig
        cg_own = cs[pl.ds(4, 128)]
        sums = []
        for j in range(9):
            sums.append(
                jnp.sum(cg_own * mx[pl.ds(4 + j, 128)] * mk[j, pl.ds(4, 128)], axis=0, keepdims=True)
            )
        sums.append(jnp.zeros((7, 128), F32))
        kg[c] = jnp.concatenate(sums, axis=0)

    loop(0, 8, chunk)
    stores = [
        pltpu.make_async_copy(src, dst, load.at[6 + n])
        for n, (src, dst) in enumerate(((lo_ref, lo_hbm), (ig_ref, ig_hbm)))
    ]
    send_ig = [pair(igs.at[2 * z + 1 - core], igp.at[z], 1 + z) for z in range(2)]
    for c in send_ig:
        c.start()
    ag = jnp.zeros((T, H * E), F32)
    for z in range(4):
        ag = ag + jnp.dot(igs[z], w_ref[z * 256 : (z + 1) * 256, :], preferred_element_type=F32)
    dos[...] = ag.astype(BF).astype(F32).T.astype(BF).reshape(H, E, T)
    d_copy = lambda d: remote(dos.at[(plane + d) % 8], do_in.at[plane], d_s.at[d], d_r.at[d], plane_at(d))
    loop(1, 8, lambda d: d_copy(d).start())
    do_in[plane] = dos[plane]

    k1_copy = lambda d: remote(kg.at[(plane + d) % 8], k1.at[plane], k1_s.at[d], k1_r.at[d], plane_at(d))
    k2_copy = lambda d: remote(ksum.at[0], k2.at[dp * 4 + part], k2_s.at[d], k2_r.at[d], column_at(d))
    k3_copy = lambda d: remote(ksum.at[1], kall.at[plane], k3_s.at[d], k3_r.at[d], plane_at(d))
    loop(1, 8, lambda d: k1_copy(d).start())
    k1[plane] = kg[plane]

    w_copy = lambda d: remote(wg.at[(chip + d) % 64], wg_in.at[d], w_s.at[d], w_r.at[d], chip_at(d))
    send_att.wait()
    for c in send_ig:
        c.wait()
    for z in range(2):
        part_sum = lax.dot_general(igs[2 * z + core], am[...], TN, preferred_element_type=F32)
        part_sum = part_sum + lax.dot_general(igp[z], ap[...], TN, preferred_element_type=F32)
        wg[z * 32 : (z + 1) * 32] = part_sum.reshape(32, 8, H * E).astype(BF)
    loop(1, 64, lambda d: w_copy(d).start())
    for c in stores:
        c.start()

    dqa[...] = jnp.zeros((E, H * T), F32)
    zero = jnp.zeros((E, T), BF)
    loop(1, 8, lambda d: d_copy(d).wait())
    for i in range(H):
        dot = do_in[i]
        rows[i] = jnp.sum(dot.astype(F32) * att[i].astype(F32), axis=0, keepdims=True)
        both[i, E : 2 * E, T:] = dot
        pair_t = jnp.concatenate(
            [
                jnp.concatenate([both[i, :E, :T], zero], axis=0),
                jnp.concatenate([zero, dot], axis=0),
            ],
            axis=1,
        )
        turned = pair_t.astype(F32).T.astype(BF)
        back[i * T : (i + 1) * T] = turned[:T]
        back[(H + i) * T : (H + i + 1) * T] = turned[T:]
    loop(1, 8, lambda d: k1_copy(d).wait())
    ksum[0] = jnp.sum(k1[...], axis=0)
    k2[dp * 4 + part] = ksum[0]
    loop(1, 16, lambda d: k2_copy(d).start())

    g_copy = lambda n: remote(
        dks.at[n],
        dkv_in.at[n],
        g_s.at[n],
        g_r.at[n],
        {"ctx": owner(n)},
    )

    def product(t, sd):
        for i in range(H):
            sd[i] = jnp.dot(kx[t], both[i], preferred_element_type=F32)

    def backward_part(t, sd, pt, dst):
        for i in range(H):
            cols = slice(i * T, (i + 1) * T)
            p = jnp.exp(sd[i, :, :T] - lse[:, cols])
            ds = (p * (sd[i, :, T:] - rows[i])).astype(BF)
            dst[:, cols] = ds
            pt[:, cols] = p.astype(BF)
        for i in range(0, H, 2):
            cols = slice(i * T, (i + 2) * T)
            dqa[:, cols] += jnp.dot(kt[t, :E], dst[:, cols], preferred_element_type=F32)
        dkv = jnp.dot(dst[...], back[: H * T], preferred_element_type=F32)
        dkv = dkv + jnp.dot(pt[...], back[H * T :], preferred_element_type=F32)
        dkv = dkv.astype(BF)
        dks[2 * t] = dkv[:T]
        dks[2 * t + 1] = dkv[T:]

    def backward_step(u):
        t = 2 * u
        product(t + 1, sd_b)
        backward_part(t, sd_a, pt_a, ds_a)
        product(jnp.minimum(t + 2, NB - 1), sd_a)
        backward_part(t + 1, sd_b, pt_b, ds_b)

        @pl.when(u > 0)
        def _():
            g_copy(2 * t).start()

        g_copy(2 * t + 1).start()
        g_copy(2 * t + 2).start()
        g_copy(2 * t + 3).start()

    product(0, sd_a)
    loop(0, NB // 4, backward_step)
    loop(1, 16, lambda d: k2_copy(d).wait())
    ksum[1] = jnp.sum(k2[...], axis=0)
    kall[plane] = ksum[1]
    loop(1, 8, lambda d: k3_copy(d).start())
    loop(NB // 4, NB // 2, backward_step)
    for i in range(H):
        dqs[i] = dqa[:, i * T : (i + 1) * T].astype(BF)
    y_copy = lambda d: remote(dqs.at[(plane + d) % 8], dq_in.at[plane], y_s.at[d], y_r.at[d], plane_at(d))
    loop(1, 8, lambda d: y_copy(d).start())
    dq_in[plane] = dqs[plane]
    dkv_in[0] = dks[0]

    for c in stores:
        c.wait()
    loop(1, 8, lambda d: k3_copy(d).wait())
    ko_ref[...] = kall[...]

    def add(d, total):
        w_copy(d).wait()
        return total + wg_in[d].astype(F32)

    wo_ref[...] = lax.fori_loop(1, 64, add, wg[chip].astype(F32))
    loop(1, 8, lambda d: y_copy(d).wait())
    dq_ref[...] = (dq_in[...].astype(F32).reshape(H * E, T) * SCALE).T.astype(BF)
    loop(1, 32, lambda d: g_copy(d).wait())
    for h in range(H):
        parts = [dkv_in[slot((h - plane + 8) % 8, f)].astype(F32) for f in range(4)]
        total = (parts[0] + parts[1]) + (parts[2] + parts[3])
        cols = slice(h * E, (h + 1) * E)
        dk_ref[:, cols] = total[:, :E].astype(BF)
        dv_ref[:, cols] = total[:, E:].astype(BF)


def layer(lens, q, k, v, x, g, w, ck):
    dma = pltpu.SemaphoreType.DMA
    V = pltpu.VMEM
    return pl.pallas_call(
        layer_kernel,
        name="layer",
        out_shape=(
            jax.ShapeDtypeStruct((T, C), BF),
            jax.ShapeDtypeStruct((T, C), BF),
            jax.ShapeDtypeStruct((T, H * E), BF),
            jax.ShapeDtypeStruct((T, H * E), BF),
            jax.ShapeDtypeStruct((T, H * E), BF),
            jax.ShapeDtypeStruct((8, H * E), F32),
            jax.ShapeDtypeStruct((8, 16, 128), F32),
        ),
        in_specs=[pl.BlockSpec(memory_space=pltpu.SMEM)] + [pl.BlockSpec(memory_space=pl.ANY)] * 6 + vm(1),
        out_specs=(pl.BlockSpec(memory_space=pl.ANY),) * 2 + tuple(vm(5)),
        scratch_shapes=[
            V((T, H * E), BF),
            V((T, H * E), BF),
            V((T, H * E), BF),
            V((T, C), BF),
            V((T, C), BF),
            V((C, H * E), BF),
            V((T, C), BF),
            V((T, C), BF),
            dma((8,)),
            V((H, T, 2 * E), BF),
            V((H, E, T), BF),
            V((32, T, 2 * E), BF),
            V((H, E, T), BF),
            V((2, 2, 8, C), BF),
            V((NB, KB, 4 * E), BF),
            V((NB, 2 * E, KB), BF),
            V((H, 4 * E, 2 * T), BF),
            V((H * 2 * T, 2 * E), BF),
            V((1, H * T), F32),
            V((8, H * T), F32),
            V((E, H * T), F32),
            V((1, H * T), F32),
            V((H, 1, T), F32),
            V((H, E, T), BF),
            V((H, 2, 8, 128), BF),
            V((H, E, T), BF),
            V((2, H, 8, 128), BF),
            V((T, H * E), BF),
            V((T, H * E), BF),
            V((4, T, 256), BF),
            V((2, T, 256), BF),
            V((H, E, T), BF),
            V((H, E, T), BF),
            V((144, 128), F32),
            V((144, C), F32),
            V((136, 128), F32),
            V((9, 136, 128), F32),
            V((16, C), F32),
            V((64, 8, H * E), BF),
            V((64, 8, H * E), BF),
            V((8, 16, 128), F32),
            V((8, 16, 128), F32),
            V((16, 16, 128), F32),
            V((2, 16, 128), F32),
            V((8, 16, 128), F32),
            V((H, KB, T), F32),
            V((H, KB, T), F32),
            V((H, KB, 2 * T), F32),
            V((H, KB, 2 * T), F32),
            V((KB, H * T), BF),
            V((KB, H * T), BF),
            V((KB, H * T), BF),
            V((KB, H * T), BF),
            V((8, H * T), F32),
            V((E, H * T), F32),
            V((32, T, 2 * E), BF),
            V((32, T, 2 * E), BF),
            V((H, E, T), BF),
            V((H, E, T), BF),
        ]
        + [pltpu.SemaphoreType.REGULAR]
        + [dma((n,)) for n in (8, 8, 8, 8)]
        + [dma((2, 2))] * 2
        + [dma((8,))] * 2
        + [dma((2, 8))] * 2
        + [dma((n,)) for n in (8, 8, 3, 3)]
        + [dma((2, 8))] * 4
        + [dma((n,)) for n in (64, 64, 8, 8, 16, 16, 8, 8, 32, 32, 8, 8)],
        compiler_params=pltpu.CompilerParams(collective_id=0, has_side_effects=True),
    )(lens, q, k, v, x, g, w, ck)


def hand_on_kernel(a, b, c, d, e, f, k, ao, bo, co, do, eo, fo, ko):
    for src, dst in ((a, ao), (b, bo), (c, co), (d, do), (e, eo), (f, fo)):
        dst[...] = src[...]
    for h in range(8):
        ko[:, h * 128 : (h + 1) * 128] = k[h, :9]


def hand_on(*xs):
    shapes = [jax.ShapeDtypeStruct(x.shape, x.dtype) for x in xs[:6]]
    return pl.pallas_call(
        hand_on_kernel,
        name="hand_on",
        out_shape=tuple(shapes) + (jax.ShapeDtypeStruct((9, C), F32),),
        in_specs=vm(7),
        out_specs=tuple(vm(7)),
    )(*xs)


def body(x, q, k, v, w, ck, lens, g):
    outs = hand_on(*layer(lens, q, k, v, x, g, w, ck.T))
    return outs[:6] + (outs[6].T,)


def solution(mesh):
    row = P(("dp", "ctx"), None)
    return jax.shard_map(
        body,
        mesh=mesh,
        in_specs=(row, row, row, row, P(), P(), P(), row),
        out_specs=(row, row, row, row, row, row, P()),
        check_vma=False,
    )
```

```python
import jax
import jax.numpy as jnp
from jax import lax
from jax.experimental import pallas as pl
from jax.experimental.pallas import tpu as pltpu
from jax.sharding import PartitionSpec as P

MESH = pl.DeviceIdType.MESH
BF = jnp.bfloat16
F32 = jnp.float32
H = 8
E = 64
C = 1024
SCALE = 0.125
NEG = -1e30
T = 128
KB = 256
NB = 16
NT = (((1,), (1,)), ((), ()))
TN = (((0,), (0,)), ((), ()))


def vm(n):
    return [pl.BlockSpec(memory_space=pltpu.VMEM)] * n


def loop(a, b, f):
    def step(d, _):
        f(d)
        return 0

    lax.fori_loop(a, b, step, 0)


def fold(x, op):
    return op(x.reshape(x.shape[0] // 8, 8, x.shape[1]), axis=0)


def remote(src, dst, snd, rcv, where):
    return pltpu.make_async_remote_copy(
        src_ref=src, dst_ref=dst, send_sem=snd, recv_sem=rcv, device_id=where, device_id_type=MESH
    )


def layer_kernel(
    len_ref, q_hbm, k_hbm, v_hbm, x_hbm, g_hbm, w_hbm, ck_ref,
    lo_hbm, ig_hbm, dq_ref, dk_ref, dv_ref, wo_ref, ko_ref,
    q_ref, k_ref, v_ref, x_ref, g_ref, w_ref, lo_ref, ig_ref, load, kvs, qs, kv_in, q_in, halo, kx, kt, both, back, m1, l8, acc, lse, rows, att, edge,
    at_in, eb, am, ap, igs, igp, dos, do_in, mx, ge, cs, mk, cf, wg, wg_in,
    kg, k1, k2, ksum, kall, st_a, st_b, sd_a, sd_b, pt_a, pt_b, ds_a, ds_b, top, dqa, dks, dkv_in, dqs, dq_in,
    met, kv_s, kv_r, q_s, q_r, h_s, h_r, a_s, a_r, e_s, e_r, d_s, d_r, p_s, p_r,
    f_s, f_r, r_s, r_r, w_s, w_r, k1_s, k1_r, k2_s, k2_r, k3_s, k3_r, g_s, g_r, y_s, y_r,
):
    dp, me = lax.axis_index("dp"), lax.axis_index("ctx")
    core, part, plane = dp % 2, me % 4, me // 4
    partner = {"dp": dp - core + (1 - core)}
    chip = (dp // 2) * 32 + me

    def plane_at(d):
        return {"ctx": (me + 4 * d) % 32}

    def chip_at(d):
        other = (chip + d) % 64
        return {"dp": (other // 32) * 2 + core, "ctx": other % 32}

    def column_at(d):
        other = (dp * 4 + part + d) % 16
        return {"dp": other // 4, "ctx": plane * 4 + other % 4}

    homes = ((q_hbm, q_ref), (k_hbm, k_ref), (v_hbm, v_ref), (g_hbm, g_ref), (x_hbm, x_ref), (w_hbm, w_ref))
    loads = [pltpu.make_async_copy(src, dst, load.at[n]) for n, (src, dst) in enumerate(homes)]
    for c in loads:
        c.start()

    barrier = pltpu.get_barrier_semaphore()

    def signal(where):
        pl.semaphore_signal(barrier, inc=1, device_id=where, device_id_type=MESH)

    beyond = {"dp": (dp + 2) % 4}
    up, down = {"ctx": plane * 4 + (part + 1) % 4}, {"ctx": plane * 4 + (part + 3) % 4}
    loop(1, 8, lambda d: signal(plane_at(d)))
    for where in (up, down, {"ctx": (me + 1) % 32}, {"ctx": (me + 31) % 32}, partner, beyond):
        signal(where)

    for c in loads[:3]:
        c.wait()
    for h in range(H):
        cols = slice(h * E, (h + 1) * E)
        kvs[h] = jnp.concatenate([k_ref[:, cols], v_ref[:, cols]], axis=1)
    qt = (q_ref[...].astype(F32) * SCALE).T.astype(BF)
    for h in range(H):
        qs[h] = qt[h * E : (h + 1) * E, :]
    kv_in[0] = kvs[plane]
    q_in[0] = qs[plane]

    s1 = len_ref[dp, 0]
    s2 = s1 + len_ref[dp, 1]
    s3 = s2 + len_ref[dp, 2]
    s4 = s3 + len_ref[dp, 3]

    def record_of(pos):
        one = lambda s: jnp.where(pos >= s, 1, 0)
        return one(s1) + one(s2) + one(s3)

    pl.semaphore_wait(barrier, 13)

    q_copy = lambda d: remote(qs.at[(plane + d) % 8], q_in.at[d], q_s.at[d], q_r.at[d], plane_at(d))
    slot = lambda e, f: f // 2 * 16 + 2 * e + f % 2
    owner = lambda n: (plane - n // 2 % 8 + 8) % 8 * 4 + (part - n // 16 * 2 - n % 2 + 4) % 4
    kv_copy = lambda e: remote(
        kvs.at[(plane + e) % 8], kv_in.at[slot(e, 0)], kv_s.at[e], kv_r.at[e], plane_at(e)
    )

    def pass_on(e, n):
        return remote(
            kv_in.at[slot(e, 0)], kv_in.at[slot(e, (3, 1)[n])], f_s.at[n, e], f_r.at[n, e], (down, up)[n]
        )

    def relay(e, n):
        half = pl.ds((1 - n) * 64, 64)
        return remote(
            kv_in.at[slot(e, (3, 1)[n]), half],
            kv_in.at[slot(e, 2), half],
            r_s.at[n, e],
            r_r.at[n, e],
            (down, up)[n],
        )

    def stage_pass(e):
        pass_on(e, 0).start()
        pass_on(e, 1).start()

    def stage_relay(e):
        for n in range(2):
            pass_on(e, n).wait_recv()
            relay(e, n).start()

    def stage_last(e):
        relay(e, 0).wait_recv()
        relay(e, 1).wait_recv()

    def stage_first(e):
        kv_copy(e).wait_recv()
        stage_pass(e)

    def halo_copy(a, up):
        ref, s = (x_ref, g_ref)[a], 0 if up else 1
        return remote(
            ref.at[pl.ds(T - 8, 8)] if up else ref.at[pl.ds(0, 8)],
            halo.at[a, s],
            h_s.at[a, s],
            h_r.at[a, s],
            {"ctx": (me + (1 if up else 31)) % 32},
        )

    halos = [halo_copy(a, up) for a in range(2) for up in (True, False)]
    loop(1, 8, lambda d: q_copy(d).start())
    loop(1, 8, lambda e: kv_copy(e).start())
    stage_pass(0)
    for c in loads[3:]:
        c.wait()
    for c in halos:
        c.start()

    m1[...] = jnp.full((1, H * T), NEG, F32)
    l8[...] = jnp.zeros((8, H * T), F32)
    acc[...] = jnp.zeros((E, H * T), F32)
    lane = lax.broadcasted_iota(jnp.int32, (1, 2 * E), 1)
    pick = lambda a, b, c, d, e: jnp.where(
        lane == 0, a, jnp.where(lane == 1, b, jnp.where(lane == 2, c, jnp.where(lane == 3, d, e)))
    )
    begin, end = pick(0, s1, s2, s3, s4), pick(s1, s2, s3, s4, s4)

    for i in range(H):
        pos = (i * 4 + part) * T + lax.broadcasted_iota(jnp.int32, (2 * E, T), 1)
        row = lax.broadcasted_iota(jnp.int32, (2 * E, T), 0)
        both[i, : 2 * E] = jnp.zeros((2 * E, 2 * T), BF)
        both[i, 2 * E :, :T] = jnp.where((row < 4) & (record_of(pos) != row), NEG, 0.0).astype(BF)
        both[i, 2 * E :, T:] = jnp.zeros((2 * E, T), BF)

    pos = me * T - 4 + lax.broadcasted_iota(jnp.int32, (136, 128), 0)
    label = lambda p: jnp.where((p >= 0) & (p < s4), record_of(p), -1)
    mine = label(pos)
    for j in range(9):
        mk[j] = jnp.where(label(pos + (j - 4)) == mine, 1.0, 0.0)
    cf[0:9] = ck_ref[...].astype(F32)
    ge[8:136] = g_ref[...].astype(F32)

    def mark(t):
        for u in range(2):
            p = owner(2 * t + u) * T + lax.broadcasted_iota(jnp.int32, (T, 2 * E), 0)
            one = jnp.where((p >= begin) & (p < end), 1.0, 0.0).astype(BF)
            kx[t, u * T : (u + 1) * T, 2 * E :] = one

    loop(0, NB, mark)
    loop(1, 8, lambda d: q_copy(d).wait_recv())
    for i in range(H):
        both[i, :E, :T] = q_in[(plane - i + 8) % 8]

    def build(t):
        for u in range(2):
            kv = kv_in[2 * t + u]
            at = slice(u * T, (u + 1) * T)
            kt[t, :, at] = kv.astype(F32).T.astype(BF)
            kx[t, at, : 2 * E] = kv

    def score(t, st):
        for i in range(H):
            s = jnp.dot(kx[t], both[i, :, :T], preferred_element_type=F32)
            st[i] = s
            top[:, i * T : (i + 1) * T] = fold(s, jnp.max)

    def weigh(t, st, pt):
        old = m1[...]
        new = jnp.maximum(old, jnp.max(top[...], axis=0, keepdims=True))
        scale = jnp.exp(old - new)
        m1[...] = new
        return new, scale

    def spread(t, st, pt, new, scale):
        for i in range(H):
            cols = slice(i * T, (i + 1) * T)
            p = jnp.exp(st[i] - new[:, cols])
            l8[:, cols] = l8[:, cols] * scale[:, cols] + fold(p, jnp.sum)
            pt[:, cols] = p.astype(BF)
        for i in range(0, H, 2):
            cols = slice(i * T, (i + 2) * T)
            acc[:, cols] = acc[:, cols] * scale[:, cols] + jnp.dot(
                kt[t, E:], pt[:, cols], preferred_element_type=F32
            )

    loop(1, 8, stage_first)
    stage_relay(0)
    build(0)
    score(0, st_a)

    def forward_step(u):
        t = 2 * u

        @pl.when(u < 4)
        def _():
            stage_relay(2 * u + 1)

        @pl.when(u < 3)
        def _():
            stage_relay(2 * u + 2)

        @pl.when(u > 3)
        def _():
            stage_last(2 * u - 7)

        @pl.when((u > 2) & (u < 7))
        def _():
            stage_last(2 * u - 6)

        later = jnp.minimum(t + 2, NB - 1)
        build(t + 1)
        build(later)
        w = weigh(t, st_a, pt_a)
        score(t + 1, st_b)
        spread(t, st_a, pt_a, *w)
        w = weigh(t + 1, st_b, pt_b)
        score(later, st_a)
        spread(t + 1, st_b, pt_b, *w)

    loop(0, NB // 2, forward_step)
    pl.semaphore_signal(met, inc=1, device_id=beyond, device_id_type=MESH)
    for i in range(H):
        cols = slice(i * T, (i + 1) * T)
        total = jnp.sum(l8[:, cols], axis=0, keepdims=True)
        lse[:, cols] = m1[:, cols] + jnp.log(total)
        out = acc[:, cols] / total
        att[i] = out.astype(BF)
        wide = jnp.concatenate([out, jnp.zeros((E, T), F32)], axis=0).T
        edge[i, 0] = wide[:8].astype(BF)
        edge[i, 1] = wide[T - 8 :].astype(BF)

    a_copy = lambda d: remote(att.at[(plane + d) % 8], at_in.at[plane], a_s.at[d], a_r.at[d], plane_at(d))

    def e_copy(i, late):
        other = (4 * i + part + (1 if late else 31)) % 32
        u = 1 if late else 0
        return remote(
            edge.at[i, u], eb.at[1 - u, plane], e_s.at[u, i], e_r.at[1 - u, plane], {"ctx": other}
        )

    e_arrival = lambda h, s: remote(edge.at[0, 0], eb.at[s, h], e_s.at[0, 0], e_r.at[s, h], partner)
    loop(1, 8, lambda d: a_copy(d).start())

    def edge_start(i):
        e_copy(i, True).start()
        e_copy(i, False).start()

    loop(0, 8, edge_start)
    at_in[plane] = att[plane]
    for c in halos:
        c.wait()
    ge[0:8] = halo[1, 0].astype(F32)
    ge[136:144] = halo[1, 1].astype(F32)
    loop(1, 8, lambda d: q_copy(d).wait_send())
    loop(1, 8, lambda e: kv_copy(e).wait_send())

    def sent(e):
        for n in range(2):
            pass_on(e, n).wait_send()
            relay(e, n).wait_send()

    loop(0, 8, sent)
    loop(1, 8, lambda d: a_copy(d).wait())

    def edge_wait(i):
        e_copy(i, True).wait_send()
        e_copy(i, False).wait_send()
        e_arrival(i, 0).wait_recv()
        e_arrival(i, 1).wait_recv()

    loop(0, 8, edge_wait)

    am[...] = at_in[...].astype(F32).reshape(H * E, T).T.astype(BF)
    pair = lambda src, dst, n: remote(src, dst, p_s.at[n], p_r.at[n], partner)
    pl.semaphore_wait(met, 1)
    send_att = pair(am, ap, 0)
    send_att.start()
    sides = jnp.concatenate(
        [jnp.concatenate([eb[s, h][:, :E] for h in range(H)], axis=1) for s in range(2)], axis=0
    )

    def chunk(c):
        cols = pl.ds(pl.multiple_of(c * 128, 128), 128)
        wc = w_ref[cols, :]
        main = lax.dot_general(am[...], wc, NT, preferred_element_type=F32)
        rim = lax.dot_general(sides, wc, NT, preferred_element_type=F32)
        rnd = lambda y: y.astype(BF).astype(F32)
        mx[8:136] = rnd(x_ref[:, cols].astype(F32) + main)
        mx[0:8] = rnd(halo[0, 0, :, cols].astype(F32) + rim[0:8])
        mx[136:144] = rnd(halo[0, 1, :, cols].astype(F32) + rim[8:16])
        conv = jnp.zeros((136, 128), F32)
        for j in range(9):
            conv = conv + mx[pl.ds(j, 136)] * mk[j] * cf[j : j + 1, cols]
        gate = jax.nn.sigmoid(conv)
        cg = ge[pl.ds(4, 136), cols] * gate * (1.0 + conv * (1.0 - gate))
        cs[...] = rnd(cg)
        silu = conv * gate
        lo_ref[:, cols] = (mx[8:136] + silu[4:132]).astype(BF)
        deep = ge[8:136, cols]
        for j in range(9):
            deep = deep + cs[pl.ds(8 - j, 128)] * mk[8 - j, pl.ds(4, 128)] * cf[j : j + 1, cols]
        ig = deep.astype(BF)
        ig_ref[:, cols] = ig
        igs[c // 2, :, pl.ds(pl.multiple_of((c % 2) * 128, 128), 128)] = ig
        cg_own = cs[pl.ds(4, 128)]
        sums = []
        for j in range(9):
            sums.append(
                jnp.sum(cg_own * mx[pl.ds(4 + j, 128)] * mk[j, pl.ds(4, 128)], axis=0, keepdims=True)
            )
        sums.append(jnp.zeros((7, 128), F32))
        kg[c] = jnp.concatenate(sums, axis=0)

    loop(0, 8, chunk)
    stores = [
        pltpu.make_async_copy(src, dst, load.at[6 + n])
        for n, (src, dst) in enumerate(((lo_ref, lo_hbm), (ig_ref, ig_hbm)))
    ]
    send_ig = [pair(igs.at[2 * z + 1 - core], igp.at[z], 1 + z) for z in range(2)]
    for c in send_ig:
        c.start()
    ag = jnp.zeros((T, H * E), F32)
    for z in range(4):
        ag = ag + jnp.dot(igs[z], w_ref[z * 256 : (z + 1) * 256, :], preferred_element_type=F32)
    dos[...] = ag.astype(BF).astype(F32).T.astype(BF).reshape(H, E, T)
    d_copy = lambda d: remote(dos.at[(plane + d) % 8], do_in.at[plane], d_s.at[d], d_r.at[d], plane_at(d))
    loop(1, 8, lambda d: d_copy(d).start())
    do_in[plane] = dos[plane]

    k1_copy = lambda d: remote(kg.at[(plane + d) % 8], k1.at[plane], k1_s.at[d], k1_r.at[d], plane_at(d))
    k2_copy = lambda d: remote(ksum.at[0], k2.at[dp * 4 + part], k2_s.at[d], k2_r.at[d], column_at(d))
    k3_copy = lambda d: remote(ksum.at[1], kall.at[plane], k3_s.at[d], k3_r.at[d], plane_at(d))
    loop(1, 8, lambda d: k1_copy(d).start())
    k1[plane] = kg[plane]

    w_copy = lambda d: remote(wg.at[(chip + d) % 64], wg_in.at[d], w_s.at[d], w_r.at[d], chip_at(d))
    send_att.wait()
    for c in send_ig:
        c.wait()
    for z in range(2):
        part_sum = lax.dot_general(igs[2 * z + core], am[...], TN, preferred_element_type=F32)
        part_sum = part_sum + lax.dot_general(igp[z], ap[...], TN, preferred_element_type=F32)
        wg[z * 32 : (z + 1) * 32] = part_sum.reshape(32, 8, H * E).astype(BF)
    loop(1, 64, lambda d: w_copy(d).start())
    for c in stores:
        c.start()

    dqa[...] = jnp.zeros((E, H * T), F32)
    zero = jnp.zeros((E, T), BF)
    loop(1, 8, lambda d: d_copy(d).wait())
    for i in range(H):
        dot = do_in[i]
        rows[i] = jnp.sum(dot.astype(F32) * att[i].astype(F32), axis=0, keepdims=True)
        both[i, E : 2 * E, T:] = dot
        pair_t = jnp.concatenate(
            [
                jnp.concatenate([both[i, :E, :T], zero], axis=0),
                jnp.concatenate([zero, dot], axis=0),
            ],
            axis=1,
        )
        turned = pair_t.astype(F32).T.astype(BF)
        back[i * T : (i + 1) * T] = turned[:T]
        back[(H + i) * T : (H + i + 1) * T] = turned[T:]
    loop(1, 8, lambda d: k1_copy(d).wait())
    ksum[0] = jnp.sum(k1[...], axis=0)
    k2[dp * 4 + part] = ksum[0]
    loop(1, 16, lambda d: k2_copy(d).start())

    g_copy = lambda n: remote(
        dks.at[n],
        dkv_in.at[n],
        g_s.at[n],
        g_r.at[n],
        {"ctx": owner(n)},
    )

    def product(t, sd):
        for i in range(H):
            sd[i] = jnp.dot(kx[t], both[i], preferred_element_type=F32)

    def backward_part(t, sd, pt, dst):
        for i in range(H):
            cols = slice(i * T, (i + 1) * T)
            p = jnp.exp(sd[i, :, :T] - lse[:, cols])
            ds = (p * (sd[i, :, T:] - rows[i])).astype(BF)
            dst[:, cols] = ds
            pt[:, cols] = p.astype(BF)
        for i in range(0, H, 2):
            cols = slice(i * T, (i + 2) * T)
            dqa[:, cols] += jnp.dot(kt[t, :E], dst[:, cols], preferred_element_type=F32)
        dkv = jnp.dot(dst[...], back[: H * T], preferred_element_type=F32)
        dkv = dkv + jnp.dot(pt[...], back[H * T :], preferred_element_type=F32)
        dkv = dkv.astype(BF)
        dks[2 * t] = dkv[:T]
        dks[2 * t + 1] = dkv[T:]

    def backward_step(u):
        t = 2 * u
        product(t + 1, sd_b)
        backward_part(t, sd_a, pt_a, ds_a)

        @pl.when(u > 0)
        def _():
            g_copy(2 * t).start()

        g_copy(2 * t + 1).start()
        product(jnp.minimum(t + 2, NB - 1), sd_a)
        backward_part(t + 1, sd_b, pt_b, ds_b)
        g_copy(2 * t + 2).start()
        g_copy(2 * t + 3).start()

    product(0, sd_a)
    loop(0, NB // 4, backward_step)
    loop(1, 16, lambda d: k2_copy(d).wait())
    ksum[1] = jnp.sum(k2[...], axis=0)
    kall[plane] = ksum[1]
    loop(1, 8, lambda d: k3_copy(d).start())
    loop(NB // 4, NB // 2, backward_step)
    for i in range(H):
        dqs[i] = dqa[:, i * T : (i + 1) * T].astype(BF)
    y_copy = lambda d: remote(dqs.at[(plane + d) % 8], dq_in.at[plane], y_s.at[d], y_r.at[d], plane_at(d))
    loop(1, 8, lambda d: y_copy(d).start())
    dq_in[plane] = dqs[plane]
    dkv_in[0] = dks[0]

    for c in stores:
        c.wait()
    loop(1, 8, lambda d: k3_copy(d).wait())
    ko_ref[...] = kall[...]

    def add(d, total):
        w_copy(d).wait()
        return total + wg_in[d].astype(F32)

    wo_ref[...] = lax.fori_loop(1, 64, add, wg[chip].astype(F32))
    loop(1, 8, lambda d: y_copy(d).wait())
    dq_ref[...] = (dq_in[...].astype(F32).reshape(H * E, T) * SCALE).T.astype(BF)
    loop(1, 32, lambda d: g_copy(d).wait())
    for h in range(H):
        parts = [dkv_in[slot((h - plane + 8) % 8, f)].astype(F32) for f in range(4)]
        total = (parts[0] + parts[1]) + (parts[2] + parts[3])
        cols = slice(h * E, (h + 1) * E)
        dk_ref[:, cols] = total[:, :E].astype(BF)
        dv_ref[:, cols] = total[:, E:].astype(BF)


def layer(lens, q, k, v, x, g, w, ck):
    dma = pltpu.SemaphoreType.DMA
    V = pltpu.VMEM
    return pl.pallas_call(
        layer_kernel,
        name="layer",
        out_shape=(
            jax.ShapeDtypeStruct((T, C), BF),
            jax.ShapeDtypeStruct((T, C), BF),
            jax.ShapeDtypeStruct((T, H * E), BF),
            jax.ShapeDtypeStruct((T, H * E), BF),
            jax.ShapeDtypeStruct((T, H * E), BF),
            jax.ShapeDtypeStruct((8, H * E), F32),
            jax.ShapeDtypeStruct((8, 16, 128), F32),
        ),
        in_specs=[pl.BlockSpec(memory_space=pltpu.SMEM)] + [pl.BlockSpec(memory_space=pl.ANY)] * 6 + vm(1),
        out_specs=(pl.BlockSpec(memory_space=pl.ANY),) * 2 + tuple(vm(5)),
        scratch_shapes=[
            V((T, H * E), BF),
            V((T, H * E), BF),
            V((T, H * E), BF),
            V((T, C), BF),
            V((T, C), BF),
            V((C, H * E), BF),
            V((T, C), BF),
            V((T, C), BF),
            dma((8,)),
            V((H, T, 2 * E), BF),
            V((H, E, T), BF),
            V((32, T, 2 * E), BF),
            V((H, E, T), BF),
            V((2, 2, 8, C), BF),
            V((NB, KB, 4 * E), BF),
            V((NB, 2 * E, KB), BF),
            V((H, 4 * E, 2 * T), BF),
            V((H * 2 * T, 2 * E), BF),
            V((1, H * T), F32),
            V((8, H * T), F32),
            V((E, H * T), F32),
            V((1, H * T), F32),
            V((H, 1, T), F32),
            V((H, E, T), BF),
            V((H, 2, 8, 128), BF),
            V((H, E, T), BF),
            V((2, H, 8, 128), BF),
            V((T, H * E), BF),
            V((T, H * E), BF),
            V((4, T, 256), BF),
            V((2, T, 256), BF),
            V((H, E, T), BF),
            V((H, E, T), BF),
            V((144, 128), F32),
            V((144, C), F32),
            V((136, 128), F32),
            V((9, 136, 128), F32),
            V((16, C), F32),
            V((64, 8, H * E), BF),
            V((64, 8, H * E), BF),
            V((8, 16, 128), F32),
            V((8, 16, 128), F32),
            V((16, 16, 128), F32),
            V((2, 16, 128), F32),
            V((8, 16, 128), F32),
            V((H, KB, T), F32),
            V((H, KB, T), F32),
            V((H, KB, 2 * T), F32),
            V((H, KB, 2 * T), F32),
            V((KB, H * T), BF),
            V((KB, H * T), BF),
            V((KB, H * T), BF),
            V((KB, H * T), BF),
            V((8, H * T), F32),
            V((E, H * T), F32),
            V((32, T, 2 * E), BF),
            V((32, T, 2 * E), BF),
            V((H, E, T), BF),
            V((H, E, T), BF),
        ]
        + [pltpu.SemaphoreType.REGULAR]
        + [dma((n,)) for n in (8, 8, 8, 8)]
        + [dma((2, 2))] * 2
        + [dma((8,))] * 2
        + [dma((2, 8))] * 2
        + [dma((n,)) for n in (8, 8, 3, 3)]
        + [dma((2, 8))] * 4
        + [dma((n,)) for n in (64, 64, 8, 8, 16, 16, 8, 8, 32, 32, 8, 8)],
        compiler_params=pltpu.CompilerParams(collective_id=0, has_side_effects=True),
    )(lens, q, k, v, x, g, w, ck)


def hand_on_kernel(a, b, c, d, e, f, k, ao, bo, co, do, eo, fo, ko):
    for src, dst in ((a, ao), (b, bo), (c, co), (d, do), (e, eo), (f, fo)):
        dst[...] = src[...]
    for h in range(8):
        ko[:, h * 128 : (h + 1) * 128] = k[h, :9]


def hand_on(*xs):
    shapes = [jax.ShapeDtypeStruct(x.shape, x.dtype) for x in xs[:6]]
    return pl.pallas_call(
        hand_on_kernel,
        name="hand_on",
        out_shape=tuple(shapes) + (jax.ShapeDtypeStruct((9, C), F32),),
        in_specs=vm(7),
        out_specs=tuple(vm(7)),
    )(*xs)


def body(x, q, k, v, w, ck, lens, g):
    outs = hand_on(*layer(lens, q, k, v, x, g, w, ck.T))
    return outs[:6] + (outs[6].T,)


def solution(mesh):
    row = P(("dp", "ctx"), None)
    return jax.shard_map(
        body,
        mesh=mesh,
        in_specs=(row, row, row, row, P(), P(), P(), row),
        out_specs=(row, row, row, row, row, row, P()),
        check_vma=False,
    )
```
